32 devices in a mesh: dp: 4 (over x, core), expert: 8 (over z, y).
Axes of the slice: x: 2, y: 2, z: 4, core: 2. Of those that a mesh axis runs over, the one named last changes fastest.
Arguments:
- block_entries: bfloat16 [32768, 768], P(('dp', 'expert')), may hold values from -6 to 6
- assignments: int32 [32768], P(('dp', 'expert')), may hold values from 0 to 7, as said below
- positions_within: int32 [32768], P(('dp', 'expert')), may hold values from 0 to 128, as said below
- specialist_quotas: int32 [8], replicated, may hold values from 64 to 128, as said below
- standardize_one_scale: bfloat16 [768], P('expert'), may hold values from 0.5 to 1.5
- standardize_one_shift: bfloat16 [768], P('expert'), may hold values from -0.625 to 0.625
- asking_weights: bfloat16 [768, 768], P('expert', 'dp'), may hold values from -0.21875 to 0.21875
- asking_shift: bfloat16 [768], P('expert'), may hold values from -0.625 to 0.625
- lookup_weights: bfloat16 [768, 768], P('expert', 'dp'), may hold values from -0.21875 to 0.21875
- content_weights: bfloat16 [768, 768], P('expert', 'dp'), may hold values from -0.21875 to 0.21875
- content_shift: bfloat16 [768], P('expert'), may hold values from -0.625 to 0.625
- context_mixing_weights: bfloat16 [768, 768], P('expert', 'dp'), may hold values from -1.75 to 1.75
- context_mixing_shift: bfloat16 [768], P('expert'), may hold values from -0.625 to 0.625
- standardize_two_scale: bfloat16 [768], P('expert'), may hold values from 0.5 to 1.5
- standardize_two_shift: bfloat16 [768], P('expert'), may hold values from -0.625 to 0.625
- gating_prototypes: bfloat16 [8, 768], P('expert'), may hold values from -0.15625 to 0.15625
- specialist_widen_weights: bfloat16 [8, 768, 3072], P('expert'), may hold values from -0.21875 to 0.21875
- specialist_widen_shift: bfloat16 [8, 3072], P('expert'), may hold values from -0.625 to 0.625
- specialist_contract_weights: bfloat16 [8, 3072, 768], P('expert'), may hold values from -0.21875 to 0.21875
- specialist_contract_shift: bfloat16 [8, 768], P('expert'), may hold values from -0.625 to 0.625
- upstream_adjoint: bfloat16 [32768, 768], P(('dp', 'expert')), may hold values from -6 to 6
Outputs:
- output: bfloat16 [32768, 768], P(('dp', 'expert'))
- input_grad: float32 [32768, 768], P(('dp', 'expert'))
- ln1_gain_grad: float32 [768], P('expert')
- ln1_shift_grad: float32 [768], P('expert')
- query_weight_grad: float32 [768, 768], P('expert', 'dp')
- query_bias_grad: float32 [768], P('expert')
- key_weight_grad: float32 [768, 768], P('expert', 'dp')
- value_weight_grad: float32 [768, 768], P('expert', 'dp')
- value_bias_grad: float32 [768], P('expert')
- out_weight_grad: float32 [768, 768], P('expert', 'dp')
- out_bias_grad: float32 [768], P('expert')
- ln2_gain_grad: float32 [768], P('expert')
- ln2_shift_grad: float32 [768], P('expert')
- centroid_grad: float32 [8, 768], P('expert')
- expert_in_grad: float32 [8, 768, 3072], P('expert', None, 'dp')
- expert_in_bias_grad: float32 [8, 3072], P('expert', 'dp')
- expert_out_grad: float32 [8, 3072, 768], P('expert', 'dp')
- expert_out_bias_grad: float32 [8, 768], P('expert', 'dp')
The draws below stay inside these ranges and needn't reach their ends.
Inputs may be any that keep to these rules, and one draw needn't show every extreme that they name: `assignments`: in the rows of each device (aligned blocks of 1024 rows), one expert, the same for all devices, is named by 128 + 1 or more rows. positions_within[t] is the number of earlier rows of the same device's block of 1024 rows whose route equals assignments[t], clamped at 128; every device has a row whose slot is 128. `specialist_quotas`: A row is kept when its slot is below its expert's capacity; the expert named by 128 + 1 or more rows of every device has capacity 128.
All inputs are finite; a program needn't handle non-finite values.
Results may differ from the reference program's by a relative error of at most 0.019.
Values may be sent and summed in bfloat16 or wider, within the bound.
No kernel may reach another device: no remote copies, remote signals or barrier semaphores. Data moves between devices by JAX's collectives and lax.ppermute only.
A program may use at most 320 MiB of HBM per device.

```python
from functools import partial
import jax
import jax.numpy as jnp
import numpy as np
from jax import lax

D = 768
HEADS = 12
HEAD_DIM = 64
FF = 3072
SEQ_LEN = 1024
EXPERTS = 8
TOK_DEV = 1024
TOKENS = 32768
CAP = 128
DEVICES = 32


def routing_tables(key):
    hot = jax.random.randint(jax.random.fold_in(key, 7), (), 0, EXPERTS)
    weights = np.array([1000000 // (rank + 3) for rank in range(EXPERTS)], dtype=np.int64)
    bounds = jnp.asarray(np.cumsum(weights)[:-1].astype(np.int32))
    total_weight = int(weights.sum())
    picks = jax.random.randint(jax.random.fold_in(key, 11), (TOKENS,), 0, total_weight)
    ranks = jnp.sum((picks[:, None] >= bounds[None, :]).astype(jnp.int32), axis=1)
    order = jax.random.permutation(jax.random.fold_in(key, 13), EXPERTS).astype(jnp.int32)
    assignments = order[ranks]
    blocks = TOKENS // TOK_DEV
    spread = max(1, (1 << 30) // TOK_DEV)
    scores = jax.random.randint(jax.random.fold_in(key, 17), (blocks, TOK_DEV), 0, spread) * TOK_DEV
    scores = scores + jnp.arange(TOK_DEV, dtype=jnp.int32)[None, :]
    places = jnp.argsort(jnp.argsort(scores, axis=1), axis=1)
    forced = (places < CAP + 1).reshape(TOKENS)
    assignments = jnp.where(forced, hot, assignments).astype(jnp.int32)
    onehot = (assignments.reshape(blocks, TOK_DEV)[:, :, None] == jnp.arange(EXPERTS, dtype=jnp.int32)[None, None, :]).astype(jnp.int32)
    earlier = jnp.cumsum(onehot, axis=1) - onehot
    positions_within = jnp.sum(earlier * onehot, axis=2).reshape(TOKENS)
    positions_within = jnp.minimum(positions_within, CAP).astype(jnp.int32)
    return (hot, assignments, positions_within)


def draw_assignments(key, part):
    return routing_tables(key)[1]


def draw_positions_within(key, part):
    return routing_tables(key)[2]


def draw_specialist_quotas(key, part):
    hot = routing_tables(key)[0]
    levels = jax.random.randint(jax.random.fold_in(key, 19), (EXPERTS,), CAP // 2, CAP + 1)
    return jnp.where(jnp.arange(EXPERTS, dtype=jnp.int32) == hot, CAP, levels).astype(jnp.int32)


def steps_of(key, extent, split, least, largest):
    def one(axis_at, parts):
        draws = jax.random.uniform(jax.random.fold_in(jax.random.fold_in(key, 6), axis_at), (parts,), jnp.float32, least / len(split), largest / len(split))
        return jnp.repeat(jnp.exp(draws), extent[axis_at] // parts).reshape((-1,) + (1,) * (len(extent) - axis_at - 1))

    factor_of = one(*split[0])
    for cut in split[1:]:
        factor_of = factor_of * one(*cut)
    return factor_of


def scatter_about(rng, shape, scale, reach, cuts=(), kind=jnp.bfloat16):
    values = scale * jax.random.normal(rng, shape, jnp.float32)
    if cuts:
        values = values * steps_of(rng, shape, cuts, -0.22, 0.18)
    return jnp.clip(values, -reach, reach).astype(kind)


def setup_inputs(seed: int = 0) -> dict:
    seeds = jax.random.split(jax.random.key(seed), 22)
    block_entries = scatter_about(seeds[0], (TOKENS, D), 1.0, 6.0, ((0, 32),))
    assignments = draw_assignments(jax.random.fold_in(seeds[21], 71), 0)
    positions_within = draw_positions_within(jax.random.fold_in(seeds[21], 71), 0)
    specialist_quotas = draw_specialist_quotas(jax.random.fold_in(seeds[21], 71), 0)
    standardize_one_scale = jnp.clip(1.0 + 0.1 * jax.random.normal(seeds[4], (D,), jnp.float32), 0.5, 1.5).astype(jnp.bfloat16)
    standardize_one_shift = scatter_about(seeds[5], (D,), 0.1, 0.625, ((0, 8),))
    asking_weights = scatter_about(seeds[6], (D, D), D ** -0.5, 0.21875, ((0, 8), (1, 4)))
    asking_shift = scatter_about(seeds[7], (D,), 0.1, 0.625, ((0, 8),))
    lookup_weights = scatter_about(seeds[8], (D, D), D ** -0.5, 0.21875, ((0, 8), (1, 4)))
    content_weights = scatter_about(seeds[9], (D, D), D ** -0.5, 0.21875, ((0, 8), (1, 4)))
    content_shift = scatter_about(seeds[10], (D,), 0.1, 0.625, ((0, 8),))
    context_mixing_weights = scatter_about(seeds[11], (D, D), (D // 64) ** -0.5, 1.75, ((0, 8), (1, 4)))
    context_mixing_shift = scatter_about(seeds[12], (D,), 0.1, 0.625, ((0, 8),))
    standardize_two_scale = jnp.clip(1.0 + 0.1 * jax.random.normal(seeds[13], (D,), jnp.float32), 0.5, 1.5).astype(jnp.bfloat16)
    standardize_two_shift = scatter_about(seeds[14], (D,), 0.1, 0.625, ((0, 8),))
    gating_prototypes = scatter_about(seeds[15], (EXPERTS, D), 0.025, 0.15625, ((0, 8),))
    specialist_widen_weights = scatter_about(seeds[16], (EXPERTS, D, FF), D ** -0.5, 0.21875, ((0, 8),))
    specialist_widen_shift = scatter_about(seeds[17], (EXPERTS, FF), 0.1, 0.625, ((0, 8),))
    specialist_contract_weights = scatter_about(seeds[18], (EXPERTS, FF, D), (FF // 4) ** -0.5, 0.21875, ((0, 8),))
    specialist_contract_shift = scatter_about(seeds[19], (EXPERTS, D), 0.1, 0.625, ((0, 8),))
    upstream_adjoint = scatter_about(seeds[20], (TOKENS, D), 1.0, 6.0, ((0, 32),))
    return {"block_entries": block_entries, "assignments": assignments, "positions_within": positions_within, "specialist_quotas": specialist_quotas, "standardize_one_scale": standardize_one_scale, "standardize_one_shift": standardize_one_shift, "asking_weights": asking_weights, "asking_shift": asking_shift, "lookup_weights": lookup_weights, "content_weights": content_weights, "content_shift": content_shift, "context_mixing_weights": context_mixing_weights, "context_mixing_shift": context_mixing_shift, "standardize_two_scale": standardize_two_scale, "standardize_two_shift": standardize_two_shift, "gating_prototypes": gating_prototypes, "specialist_widen_weights": specialist_widen_weights, "specialist_widen_shift": specialist_widen_shift, "specialist_contract_weights": specialist_contract_weights, "specialist_contract_shift": specialist_contract_shift, "upstream_adjoint": upstream_adjoint}


@jax.custom_vjp
def low(v):
    return lax.optimization_barrier(v.astype(jnp.bfloat16)).astype(jnp.float32)

@jax.custom_vjp
def low_back(v):
    return v

def low_keep(v):
    return (low(v), None)

def low_pass(kept, grad):
    return (grad,)

def back_keep(v):
    return (v, None)

def back_low(kept, grad):
    return (low(grad),)
low.defvjp(low_keep, low_pass)
low_back.defvjp(back_keep, back_low)
highest = lax.Precision.HIGHEST

def normalize(values, gain, shift):
    center = lax.optimization_barrier(jnp.mean(values, axis=-1, keepdims=True))
    centered = values - center
    spread = lax.optimization_barrier(jnp.mean(centered * centered, axis=-1, keepdims=True))
    return centered * lax.rsqrt(spread + 1e-05) * gain + shift

def group_count():
    total = TOKENS // SEQ_LEN
    chosen = 1
    for count in range(1, total + 1):
        if total % count == 0 and count * SEQ_LEN <= 4096:
            chosen = count
    return chosen

def block_evaluate(learned_state, incoming_entries, assignments, positions_within, specialist_quotas):
    gain_one, shift_one, weight_q, bias_q, weight_k, weight_v, bias_v, weight_o, bias_o, gain_two, shift_two, centers, weight_in, bias_in, weight_out, bias_out = learned_state
    group = group_count()
    head_shape = (group, SEQ_LEN, HEADS, HEAD_DIM)
    causal = jnp.arange(SEQ_LEN)[None, :] <= jnp.arange(SEQ_LEN)[:, None]

    def attend_group(block):
        normed = low(normalize(block, gain_one, shift_one))
        queries = low(low_back(jnp.dot(normed, weight_q, precision=highest) + bias_q)).reshape(head_shape)
        keys = low(low_back(jnp.dot(normed, weight_k, precision=highest))).reshape(head_shape)
        values = low(low_back(jnp.dot(normed, weight_v, precision=highest) + bias_v)).reshape(head_shape)
        scores = low_back(jnp.einsum('gqhd,gkhd->ghqk', queries, keys, precision=highest) * HEAD_DIM ** (-0.5))
        scores = jnp.where(causal[None, None], scores, -1e+30)
        probs = low(jax.nn.softmax(scores, axis=-1))
        context = jnp.einsum('ghqk,gkhd->gqhd', probs, values, precision=highest).reshape(block.shape)
        context = low(low_back(context))
        return block + low_back(jnp.dot(context, weight_o, precision=highest) + bias_o)
    checked = jax.checkpoint(attend_group)
    blocks = incoming_entries.reshape(TOKENS // (group * SEQ_LEN), group * SEQ_LEN, D)
    _, hidden_one = lax.scan(lambda carry, block: (carry, checked(block)), None, blocks)
    hidden_one = hidden_one.reshape(TOKENS, D)
    middle = low(normalize(hidden_one, gain_two, shift_two))
    logits = jnp.dot(middle, centers.T, precision=highest)
    choose_specialist = assignments[:, None] == jnp.arange(EXPERTS, dtype=jnp.int32)[None, :]
    gate = jax.nn.sigmoid(lax.optimization_barrier(jnp.sum(jnp.where(choose_specialist, logits, 0.0), axis=1)))
    device = jnp.arange(TOKENS, dtype=jnp.int32) // TOK_DEV
    surviving = positions_within < specialist_quotas[assignments]
    rows_all = DEVICES * CAP
    dump = EXPERTS * rows_all
    target = jnp.where(surviving, assignments * rows_all + device * CAP + positions_within, dump).astype(jnp.int32)
    buffer = jnp.zeros((dump + 1, D), jnp.float32).at[target].add(low_back(middle))
    buffer = buffer[:dump].reshape(EXPERTS, rows_all, D)

    def expert_apply(packed):
        first, first_bias, second, second_bias, rows = packed
        before = low_back(jnp.dot(rows, first, precision=highest) + first_bias)
        active = low(jax.nn.gelu(before, approximate=False))
        return low(low_back(jnp.dot(active, second, precision=highest) + second_bias))
    results = lax.map(jax.checkpoint(expert_apply), (weight_in, bias_in, weight_out, bias_out, buffer))
    flat = jnp.concatenate([results.reshape(dump, D), jnp.zeros((1, D), jnp.float32)], 0)
    picked = flat[target]
    return hidden_one + gate[:, None] * picked

def reference(block_entries, assignments, positions_within, specialist_quotas, standardize_one_scale, standardize_one_shift, asking_weights, asking_shift, lookup_weights, content_weights, content_shift, context_mixing_weights, context_mixing_shift, standardize_two_scale, standardize_two_shift, gating_prototypes, specialist_widen_weights, specialist_widen_shift, specialist_contract_weights, specialist_contract_shift, upstream_adjoint):
    learned_state = (standardize_one_scale.astype(jnp.float32), standardize_one_shift.astype(jnp.float32), asking_weights.astype(jnp.float32), asking_shift.astype(jnp.float32), lookup_weights.astype(jnp.float32), content_weights.astype(jnp.float32), content_shift.astype(jnp.float32), context_mixing_weights.astype(jnp.float32), context_mixing_shift.astype(jnp.float32), standardize_two_scale.astype(jnp.float32), standardize_two_shift.astype(jnp.float32), gating_prototypes.astype(jnp.float32), specialist_widen_weights.astype(jnp.float32), specialist_widen_shift.astype(jnp.float32), specialist_contract_weights.astype(jnp.float32), specialist_contract_shift.astype(jnp.float32))
    incoming_entries = block_entries.astype(jnp.float32)
    block_result, gather_entries = jax.vjp(partial(block_evaluate, assignments=assignments, positions_within=positions_within, specialist_quotas=specialist_quotas), learned_state, incoming_entries)
    grads, input_grad = gather_entries(upstream_adjoint.astype(jnp.float32))
    return (block_result.astype(jnp.bfloat16), input_grad, grads[0], grads[1], grads[2], grads[3], grads[4], grads[5], grads[6], grads[7], grads[8], grads[9], grads[10], grads[11], grads[12], grads[13], grads[14], grads[15])
```

```python
from functools import partial

import jax
import jax.numpy as jnp
from jax import lax
from jax.experimental import pallas as pl
from jax.experimental.pallas import tpu as pltpu
from jax.sharding import PartitionSpec as P

HEADS = 12
HEAD_DIM = 64
SEQ_LEN = 1024
GROUPS = 4
SLAB = 896

EPSILON = 1e-05
MASKED = -1e30
BOTH = ("dp", "expert")
BF = jnp.bfloat16
F32 = jnp.float32


def dot(left, right, left_dim, right_dim):
    return lax.dot_general(
        left, right, (((left_dim,), (right_dim,)), ((), ())), preferred_element_type=F32
    )


def normalize(values):
    center = jnp.mean(values, axis=-1, keepdims=True)
    centered = values - center
    inverse = lax.rsqrt(jnp.mean(centered * centered, axis=-1, keepdims=True) + EPSILON)
    return (centered * inverse, inverse)


def normalize_back(grad, normed, inverse, gain):
    scaled = grad * gain
    return inverse * (
        scaled
        - jnp.mean(scaled, axis=-1, keepdims=True)
        - normed * jnp.mean(scaled * normed, axis=-1, keepdims=True)
    )


def call(kernel, name, grid, in_specs, outs, scratch=(), vmem=60, cost=(0, 0, 0), **more):
    return pl.pallas_call(
        kernel,
        name=name,
        grid=grid,
        in_specs=in_specs,
        out_specs=[o[0] for o in outs],
        out_shape=[jax.ShapeDtypeStruct(o[1], o[2]) for o in outs],
        scratch_shapes=list(scratch),
        compiler_params=pltpu.CompilerParams(vmem_limit_bytes=vmem << 20),
        cost_estimate=pl.CostEstimate(
            flops=cost[0], bytes_accessed=cost[1], transcendentals=cost[2]
        ),
        **more,
    )


def full(shape):
    return pl.BlockSpec(
        shape, lambda *_: (0,) * len(shape), pipeline_mode=pl.Buffered(1)
    )


SCALARS = pl.BlockSpec(memory_space=pltpu.SMEM)
PLACED = pl.BlockSpec(memory_space=pl.ANY)


def project_kernel(first, table, order, *refs):
    if first:
        x_ref, slabs, wq_ref, wo_ref, qkv_ref, low_ref, vec_ref, cols_ref, sems = refs
    else:
        low_ref, vec_ref, slabs, wq_ref, wo_ref, qkv_ref, sems = refs
    rows = slabs.shape[1]
    half = 2 * 96
    copies = []
    if first:
        for e in range(8):
            copies.append((slabs.at[table[e], :, 128:256], cols_ref.at[pl.ds(rows * e, rows)]))
    for g in range(2):
        for e in range(8):
            copies.append(
                (slabs.at[table[8 * g + e], :, 256:], wq_ref.at[g, pl.ds(rows * e, rows)])
            )
    for g in range(2):
        for e in range(8):
            at = pl.multiple_of(half * order[4 + e // 2] + rows * (e % 2), 32)
            copies.append((slabs.at[table[8 * g + e], :, :256], wo_ref.at[g, pl.ds(at, rows)]))
    copies = [pltpu.make_async_copy(s, d, sems.at[i]) for i, (s, d) in enumerate(copies)]
    for c in copies:
        c.start()
    count, width = low_ref.shape
    if first:
        for c in copies[:8]:
            c.wait()
        copies = copies[8:]
        vec_ref[...] = cols_ref[...].astype(F32).T[64:72]
        for at in range(0, count, 256):
            unit, _ = normalize(x_ref[at : at + 256].astype(F32))
            low_ref[at : at + 256] = (unit * vec_ref[0:1] + vec_ref[1:2]).astype(BF)
    zero = jnp.zeros((1, half), F32)
    for g in range(2):
        for c in copies[8 * g : 8 * g + 8]:
            c.wait()
        bias_q = bias_v = zero
        for n in range(GROUPS):
            here = order[(0 if first else 2) + g] == n
            bias_q = jnp.where(here, vec_ref[2:3, half * n : half * n + half], bias_q)
            bias_v = jnp.where(here, vec_ref[3:4, half * n : half * n + half], bias_v)
        bias = jnp.concatenate([bias_q, zero, bias_v], axis=1)
        for at in range(0, count, 512):
            qkv_ref[g, at : at + 512] = (
                dot(low_ref[at : at + 512], wq_ref[g, :, : 3 * half], 1, 0) + bias
            ).astype(BF)
    for c in copies[16:]:
        c.wait()


def project(table, order, slabs, x=None, low=None, vec=None):
    first = x is not None
    count, width = (x if first else low).shape
    part = width // GROUPS
    outs = [
        (full((2, width, 640)), (2, width, 640), BF),
        (full((2, width, 256)), (2, width, 256), BF),
        (full((2, count, 3 * part)), (2, count, 3 * part), BF),
    ]
    scratch = [pltpu.SemaphoreType.DMA((40,))]
    if first:
        outs += [
            (full((count, width)), (count, width), BF),
            (full((8, width)), (8, width), F32),
        ]
        scratch = [pltpu.VMEM((width, 128), BF)] + scratch
        ins, args = [full((count, width)), PLACED], (x, slabs)
    else:
        ins, args = [full((count, width)), full((8, width)), PLACED], (low, vec, slabs)
    return call(
        partial(project_kernel, first), "project", (1,), [SCALARS, SCALARS] + ins, outs, scratch,
        cost=(2 * count * width * 6 * part, 12_000_000, 0),
    )(table, order, *args)


def attend_kernel(qkv_ref, ctx_ref, lse_ref):
    length = qkv_ref.shape[1]
    width = qkv_ref.shape[2] // 3
    block = min(256, length)
    lane = lax.broadcasted_iota(jnp.int32, (block, 128), 1)
    row = lax.broadcasted_iota(jnp.int32, (block, block), 0)
    col = lax.broadcasted_iota(jnp.int32, (block, block), 1)
    for i in range(length // block):
        start = i * block
        stats = jnp.zeros((block, 128), F32)
        for h in range(width // HEAD_DIM):
            at = h * HEAD_DIM
            q = qkv_ref[0, start : start + block, at : at + HEAD_DIM] * BF(HEAD_DIM**-0.5)
            k = qkv_ref[0, : start + block, width + at : width + at + HEAD_DIM]
            v = qkv_ref[0, : start + block, 2 * width + at : 2 * width + at + HEAD_DIM]
            diag = jnp.where(col <= row, dot(q, k[start:], 1, 1), MASKED)
            top = jnp.max(diag, axis=-1, keepdims=True)
            if start:
                past = dot(q, k[:start], 1, 1)
                top = jnp.maximum(top, jnp.max(past, axis=-1, keepdims=True))
            diag = jnp.exp(diag - top)
            total = jnp.sum(diag, axis=-1, keepdims=True)
            out = dot(diag.astype(BF), v[start:], 1, 0)
            if start:
                past = jnp.exp(past - top)
                total += jnp.sum(past, axis=-1, keepdims=True)
                out += dot(past.astype(BF), v[:start], 1, 0)
            ctx_ref[0, start : start + block, at : at + HEAD_DIM] = (out / total).astype(BF)
            stats = jnp.where(lane == h, top + jnp.log(total), stats)
        lse_ref[0, start : start + block, :] = stats


def attend(qkv):
    groups, length, width = qkv.shape
    width //= 3
    seqs = length // SEQ_LEN
    at = lambda g, s: (g, s, 0)
    return call(
        attend_kernel, "attend", (groups, seqs),
        [pl.BlockSpec((1, SEQ_LEN, 3 * width), at)],
        [
            (pl.BlockSpec((1, SEQ_LEN, width), at), (groups, length, width), BF),
            (pl.BlockSpec((1, SEQ_LEN, 128), at), (groups, length, 128), F32),
        ],
        cost=(8_000_000_000, 5_000_000, 4_000_000),
    )(qkv)


def attend_back_kernel(qkv_ref, ctx_ref, dctx_ref, lse_ref, out_ref, sum_ref, dq_ref):
    length = qkv_ref.shape[1]
    width = qkv_ref.shape[2] // 3
    heads = width // HEAD_DIM
    block = min(256, length)
    lane = lax.broadcasted_iota(jnp.int32, (length, 128), 1)
    stats = lse_ref[0]
    for h in range(heads):
        at = h * HEAD_DIM
        o = ctx_ref[0, :, at : at + HEAD_DIM].astype(F32)
        do = dctx_ref[0, :, at : at + HEAD_DIM].astype(F32)
        stats = jnp.where(lane == 8 + h, jnp.sum(o * do, axis=-1, keepdims=True), stats)
    stats = stats.T
    row = lax.broadcasted_iota(jnp.int32, (block, block), 0)
    col = lax.broadcasted_iota(jnp.int32, (block, block), 1)
    for h in range(heads):
        at = h * HEAD_DIM
        q = qkv_ref[0, :, at : at + HEAD_DIM] * BF(HEAD_DIM**-0.5)
        do = dctx_ref[0, :, at : at + HEAD_DIM]
        for j in range(length // block):
            start = j * block
            k = qkv_ref[0, start : start + block, width + at : width + at + HEAD_DIM]
            v = qkv_ref[0, start : start + block, 2 * width + at : 2 * width + at + HEAD_DIM]
            dk = None
            for s, e, on_diag in ((start, start + block, True), (start + block, length, False)):
                if s == e:
                    continue
                lse = stats[h : h + 1, s:e]
                inner = stats[8 + h : 9 + h, s:e]
                probs = jnp.exp(dot(k, q[s:e], 1, 1) - lse)
                if on_diag:
                    probs = jnp.where(row <= col, probs, 0.0)
                dscores = (probs * (dot(v, do[s:e], 1, 1) - inner)).astype(BF)
                dk_part = dot(dscores, q[s:e], 1, 0)
                dv_part = dot(probs.astype(BF), do[s:e], 1, 0)
                dq_part = dot(dscores, k, 0, 0)
                dk = dk_part if dk is None else dk + dk_part
                dv = dv_part if on_diag else dv + dv_part
                if j == 0:
                    dq_ref[s:e, :] = dq_part
                else:
                    dq_ref[s:e, :] += dq_part
            out_ref[0, start : start + block, width + at : width + at + HEAD_DIM] = dk.astype(BF)
            out_ref[0, start : start + block, 2 * width + at : 2 * width + at + HEAD_DIM] = (
                dv.astype(BF)
            )
        out_ref[0, :, at : at + HEAD_DIM] = (dq_ref[...] * HEAD_DIM**-0.5).astype(BF)
    sums = jnp.sum(out_ref[0].astype(F32), axis=0, keepdims=True)
    first = pl.program_id(1) == 0

    @pl.when(first)
    def _():
        sum_ref[0] = jnp.broadcast_to(sums, sum_ref.shape[1:])

    @pl.when(jnp.logical_not(first))
    def _():
        sum_ref[0] += jnp.broadcast_to(sums, sum_ref.shape[1:])


def attend_back(qkv, ctx, dctx, lse):
    groups, length, width = qkv.shape
    width //= 3
    seqs = length // SEQ_LEN
    at = lambda g, s: (g, s, 0)
    return call(
        attend_back_kernel, "attend_back", (groups, seqs),
        [
            pl.BlockSpec((1, SEQ_LEN, 3 * width), at),
            pl.BlockSpec((1, SEQ_LEN, width), at),
            pl.BlockSpec((1, SEQ_LEN, width), at),
            pl.BlockSpec((1, SEQ_LEN, 128), at),
        ],
        [
            (pl.BlockSpec((1, SEQ_LEN, 3 * width), at), (groups, length, 3 * width), BF),
            (pl.BlockSpec((1, 8, 3 * width), lambda g, s: (g, 0, 0)), (groups, 8, 3 * width), F32),
        ],
        [pltpu.VMEM((SEQ_LEN, HEAD_DIM), F32)],
        cost=(20_000_000_000, 7_000_000, 4_000_000),
    )(qkv, ctx, dctx, lse)


def slot_of(index, half, cap):
    return index // (cap // 2) * cap + index % (cap // 2) + half * (cap // 2)


def dispatch_kernel(target_ref, rows_ref, out_ref):
    count = rows_ref.shape[0]
    for at in range(0, count, 256):
        slot = lax.broadcasted_iota(jnp.int32, (256, count), 0) + at
        picks = (target_ref[...] == slot).astype(F32).astype(BF)
        out_ref[at : at + 256] = dot(picks, rows_ref[...], 1, 0).astype(BF)


def dispatch(target, rows):
    count, width = rows.shape
    return call(
        dispatch_kernel, "dispatch", (1,),
        [full((1, count)), full((count, width))],
        [(full((count, width)), (count, width), BF)],
        cost=(2 * count * count * width, 3_000_000, 0),
    )(target.reshape(1, count), rows)[0]


def mix_kernel(
    cap, order, x_ref, near_ref, far_ref, wo_near, wo_far, vec_ref, target_ref,
    h_ref, whole_ref, *refs,
):
    *sent, low_ref = refs
    count, width = x_ref.shape
    part = width // GROUPS
    pieces = [wo_near[0], wo_near[1], wo_far[0], wo_far[1]]
    for n in range(GROUPS):
        piece = pieces[0][:, :part]
        for r in range(1, GROUPS):
            piece = jnp.where(order[r] == n, pieces[r][:, :part], piece)
        whole_ref[:, n * part : n * part + part] = piece
    for at in range(0, count, 256):
        h = x_ref[at : at + 256].astype(F32) + vec_ref[4:5]
        for r in range(GROUPS):
            ctx = (near_ref, far_ref)[r // 2][r % 2, at : at + 256]
            h += dot(ctx, whole_ref[r * part : r * part + part], 1, 0)
        h_ref[at : at + 256] = h
        unit, _ = normalize(h)
        low_ref[at : at + 256] = (unit * vec_ref[5:6] + vec_ref[6:7]).astype(BF)
    for half in range(2):
        for at in range(0, count // 2, 256):
            index = lax.broadcasted_iota(jnp.int32, (256, count), 0) + at
            picks = (target_ref[...] == slot_of(index, half, cap)).astype(F32).astype(BF)
            sent[half][at : at + 256] = dot(picks, low_ref[...], 1, 0).astype(BF)


def mix(order, x, near, far, wo_near, wo_far, vec, target, cap):
    count, width = x.shape
    part = width // GROUPS
    ctx = full((2, count, part))
    return call(
        partial(mix_kernel, cap), "mix", (1,),
        [SCALARS, full((count, width)), ctx, ctx, full((2, width, 256)), full((2, width, 256)),
         full((8, width)), full((1, count))],
        [
            (full((count, width)), (count, width), F32),
            (full((width, width)), (width, width), BF),
            (full((count // 2, width)), (count // 2, width), BF),
            (full((count // 2, width)), (count // 2, width), BF),
        ],
        [pltpu.VMEM((count, width), BF)],
        cost=(2 * count * width * (width + count), 12_000_000, 0),
    )(order, x, near, far, wo_near, wo_far, vec, target.reshape(1, count))


def unmix_kernel(
    cap, order, h_ref, g_ref, dm_one, dm_two, target_ref, near_ref, far_ref, whole_ref, vec_ref,
    dh_ref, dnear_ref, dfar_ref, gnear_ref, gfar_ref, sum_ref, do_ref,
):
    count, width = h_ref.shape
    part = width // GROUPS
    sums = [jnp.zeros((1, width), F32)] * 3
    for at in range(0, count, 256):
        dm = None
        for half, rows in enumerate((dm_one, dm_two)):
            index = lax.broadcasted_iota(jnp.int32, (256, count // 2), 1)
            picks = target_ref[at : at + 256] == slot_of(index, half, cap)
            got = dot(picks.astype(F32).astype(BF), rows[...], 1, 0)
            dm = got if dm is None else dm + got
        unit, inverse = normalize(h_ref[at : at + 256])
        dh = g_ref[at : at + 256].astype(F32) + normalize_back(dm, unit, inverse, vec_ref[5:6])
        dh_ref[at : at + 256] = dh
        low = dh.astype(BF)
        do_ref[at : at + 256] = low
        for i, term in enumerate((low.astype(F32), dm * unit, dm)):
            sums[i] = sums[i] + jnp.sum(term, axis=0, keepdims=True)
        for r in range(GROUPS):
            (dnear_ref, dfar_ref)[r // 2][r % 2, at : at + 256] = dot(
                low, whole_ref[r * part : r * part + part], 1, 1
            ).astype(BF)
    sum_ref[...] = jnp.concatenate([jnp.zeros((4, width), F32)] + sums + [jnp.zeros((1, width), F32)])
    for out in (gnear_ref, gfar_ref):
        out[:, :, part:] = jnp.zeros((2, width, 256 - part), BF)
    for q in range(GROUPS):
        ctx = (near_ref, far_ref)[q // 2][q % 2]
        grad = dot(ctx, do_ref[...], 0, 0).astype(BF)
        rows = pl.ds(pl.multiple_of(order[q] * part, 64), part)
        for r in range(GROUPS):
            piece = grad[:, :part]
            for n in range(1, GROUPS):
                piece = jnp.where(order[r] == n, grad[:, n * part : n * part + part], piece)
            (gnear_ref, gfar_ref)[r // 2][r % 2, rows, :part] = piece


def unmix(order, h, g, dm_one, dm_two, target, near, far, whole, vec, cap):
    count, width = h.shape
    part = width // GROUPS
    ctx = full((2, count, part))
    out_ctx = (ctx, (2, count, part), BF)
    out_grad = (full((2, width, 256)), (2, width, 256), BF)
    half = full((count // 2, width))
    return call(
        partial(unmix_kernel, cap), "unmix", (1,),
        [SCALARS, full((count, width)), full((count, width)), half, half, full((count, 1)),
         ctx, ctx, full((width, width)), full((8, width))],
        [
            (full((count, width)), (count, width), F32),
            out_ctx, out_ctx, out_grad, out_grad,
            (full((8, width)), (8, width), F32),
        ],
        [pltpu.VMEM((count, width), BF)],
        vmem=60,
        cost=(2 * count * width * (2 * width + count), 20_000_000, 0),
    )(order, h, g, dm_one, dm_two, target.reshape(count, 1), near, far, whole, vec)


def finish_kernel(h_ref, target_ref, gy_ref, out_ref):
    count = h_ref.shape[0]
    for at in range(0, count, 256):
        slot = lax.broadcasted_iota(jnp.int32, (256, count), 1)
        picks = (target_ref[at : at + 256] == slot).astype(F32).astype(BF)
        out_ref[at : at + 256] = (h_ref[at : at + 256] + dot(picks, gy_ref[...], 1, 0)).astype(BF)


def finish(h, target, gy):
    count, width = h.shape
    return call(
        finish_kernel, "finish", (1,),
        [full((count, width)), full((count, 1)), full((count, width))],
        [(full((count, width)), (count, width), BF)],
        cost=(2 * count * count * width, 6_000_000, 0),
    )(h, target.reshape(count, 1), gy)[0]


ERFC = (
    0.169189354,
    0.1706909295,
    0.1485212475,
    0.2141814502,
    -0.09282610738,
    0.5449670381,
    -0.5097724612,
    0.4843017683,
    -0.1292532277,
)


def gelu_pair(v):
    a = jnp.abs(v) * (0.5**0.5)
    bell = jnp.exp(-0.5 * v * v)
    t = 1.0 / (1.0 + 0.3 * a)
    poly = jnp.full_like(v, ERFC[-1])
    for c in ERFC[-2::-1]:
        poly = poly * t + c
    tail = 0.5 * bell * t * poly
    cdf = jnp.where(v < 0, tail, 1.0 - tail)
    return v * cdf, cdf + v * bell * (0.5 / jnp.pi) ** 0.5


def expert_kernel(
    x_ref, g_ref, win_ref, bin_ref, wout_ref, bout_ref, center_ref, _,
    gy_ref, dm_ref, dy_ref, hid_ref, du_ref, dbin_ref, small_ref,
    y_acc, dm_acc, gate_ref, gates,
):
    step = pl.program_id(0)
    rows, width = x_ref.shape

    @pl.when(step == 0)
    def _():
        z = jnp.sum(x_ref[...].astype(F32) * center_ref[...].astype(F32), axis=-1, keepdims=True)
        gate = 1.0 / (1.0 + jnp.exp(-z))
        gate_ref[...] = jnp.broadcast_to(gate, gate_ref.shape)
        dy_ref[...] = (gate * g_ref[...].reshape(rows, width).astype(F32)).astype(BF)

    act, slope = gelu_pair(dot(x_ref[...], win_ref[...], 1, 0) + bin_ref[...].astype(F32))
    hid = act.astype(BF)
    hid_ref[...] = hid
    y = dot(hid, wout_ref[...], 1, 0)
    du = (dot(dy_ref[...], wout_ref[...], 1, 1) * slope).astype(BF)
    du_ref[...] = du
    dbin_ref[...] = jnp.broadcast_to(
        jnp.sum(du.astype(F32), axis=0, keepdims=True), dbin_ref.shape
    )
    dm = dot(du, win_ref[...], 1, 1)

    @pl.when(step == 0)
    def _():
        y_acc[...] = y
        dm_acc[...] = dm

    @pl.when(step > 0)
    def _():
        y_acc[...] += y
        dm_acc[...] += dm

    @pl.when(step == pl.num_programs(0) - 1)
    def _():
        gate = gate_ref[:, :1]
        g = g_ref[...].reshape(rows, width).astype(F32)
        y = (y_acc[...] + bout_ref[...].astype(F32)).astype(BF).astype(F32)
        gy_ref[...] = (gate * y).astype(BF).reshape(gy_ref.shape)
        dz = gate * (1.0 - gate) * jnp.sum(g * y, axis=-1, keepdims=True)
        dm_ref[...] = (dm_acc[...] + dz * center_ref[...].astype(F32)).astype(BF)
        small_ref[0:1, :] = jnp.sum(dy_ref[...].astype(F32), axis=0, keepdims=True)
        small_ref[1:2, :] = jnp.sum(dz * x_ref[...].astype(F32), axis=0, keepdims=True)


def expert(half, x, g, win, bias_in, wout, bias_out, center, gy):
    rows, width = x.shape
    ff = win.shape[1]
    chunk = min(512, ff)
    along = lambda i: (0, i)
    side = pl.BlockSpec(
        (g.shape[0], 1) + g.shape[2:], lambda i: (0, half, 0, 0), pipeline_mode=pl.Buffered(1)
    )
    return call(
        expert_kernel, "expert", (ff // chunk,),
        [
            full((rows, width)),
            side,
            pl.BlockSpec((width, chunk), along),
            pl.BlockSpec((1, chunk), along),
            pl.BlockSpec((chunk, width), lambda i: (i, 0)),
            full((1, width)),
            full((1, width)),
            PLACED,
        ],
        [
            (side, g.shape, BF),
            (full((rows, width)), (rows, width), BF),
            (full((rows, width)), (rows, width), BF),
            (pl.BlockSpec((rows, chunk), along), (rows, ff), BF),
            (pl.BlockSpec((rows, chunk), along), (rows, ff), BF),
            (pl.BlockSpec((8, chunk), along), (8, ff), F32),
            (full((8, width)), (8, width), F32),
        ],
        [
            pltpu.VMEM((rows, width), F32),
            pltpu.VMEM((rows, width), F32),
            pltpu.VMEM((rows, 128), F32),
            pltpu.SMEM((1,), jnp.int32),
        ],
        cost=(8 * rows * width * ff, 22_000_000, 2 * rows * ff),
        input_output_aliases={} if gy is None else {7: 0},
    )(x, g, win, bias_in, wout, bias_out, center, x if gy is None else gy)


def weigh_kernel(
    hid_one, hid_two, du_one, du_two, dy_one, dy_two, x_one, x_two, bin_one, bin_two,
    small_one, small_two, out_ref,
):
    ff = hid_one.shape[1]
    width = dy_one.shape[1]
    n = pl.num_programs(0)
    out_ref[0, :ff] = (
        dot(hid_one[...], dy_one[...], 0, 0) + dot(hid_two[...], dy_two[...], 0, 0)
    ).astype(BF)
    out_ref[0, ff : 2 * ff] = (
        dot(du_one[...], x_one[...], 0, 0) + dot(du_two[...], x_two[...], 0, 0)
    ).astype(BF)
    small = small_one[...] + small_two[...]
    rest = jnp.zeros((16, width), F32)
    row = lax.broadcasted_iota(jnp.int32, (16, width), 0)
    bias = (bin_one[...] + bin_two[...])[0:1]
    if ff < width:
        bias = jnp.concatenate([bias, jnp.zeros((1, width - ff), F32)], axis=1)
    rest = jnp.where(row == 0, bias, rest)
    rest = jnp.where(row == 1, small[0:1], rest)
    rest = jnp.where(row == 2, small[1:2], rest)
    out_ref[0, 2 * ff :] = rest.astype(BF)


def weigh(n, hid, du, dy, x, bias, small):
    rows, ff = hid[0].shape
    width = dy[0].shape[1]
    part = ff // n
    along = lambda i: (0, i)
    wide = pl.BlockSpec((rows, part), along)
    return call(
        weigh_kernel, "weigh", (n,),
        [wide] * 4 + [full((rows, width))] * 4 + [pl.BlockSpec((8, part), along)] * 2
        + [full((8, width))] * 2,
        [(pl.BlockSpec((1, 2 * part + 16, width), lambda i: (i, 0, 0)),
          (n, 2 * part + 16, width), BF)],
        cost=(8 * rows * width * ff, 26_000_000, 0),
    )(*hid, *du, *dy, *x, *bias, *small)[0]


def unproject_kernel(
    order, near_ref, far_ref, wq_near, wq_far, x_ref, dh_ref, vec_ref, two_ref, bias_near, bias_far,
    out_ref, sum_ref,
):
    count, width = x_ref.shape
    part = width // GROUPS
    sums = [jnp.zeros((1, width), F32)] * 2
    for at in range(0, count, 256):
        da = None
        for r in range(GROUPS):
            grad = (near_ref, far_ref)[r // 2][r % 2, at : at + 256]
            got = dot(grad, (wq_near, wq_far)[r // 2][r % 2, :, : 3 * part], 1, 1)
            da = got if da is None else da + got
        unit, inverse = normalize(x_ref[at : at + 256].astype(F32))
        out_ref[at : at + 256] = dh_ref[at : at + 256] + normalize_back(
            da, unit, inverse, vec_ref[0:1]
        )
        for i, term in enumerate((da * unit, da)):
            sums[i] = sums[i] + jnp.sum(term, axis=0, keepdims=True)
    biases = []
    for first in (0, 2 * part):
        cols = []
        for n in range(GROUPS):
            piece = jnp.zeros((1, part), F32)
            for r in range(GROUPS):
                bias = (bias_near, bias_far)[r // 2][r % 2, 0:1, first : first + part]
                piece = jnp.where(order[r] == n, bias, piece)
            cols.append(piece)
        biases.append(jnp.concatenate(cols, axis=1))
    sum_ref[...] = jnp.concatenate(sums + biases + [two_ref[4:8]])


def unproject(order, near, far, wq_near, wq_far, x, dh, vec, two, bias_near, bias_far):
    count, width = x.shape
    part = width // GROUPS
    grads, weights, bias = full((2, count, 3 * part)), full((2, width, 640)), full((2, 8, 3 * part))
    return call(
        unproject_kernel, "unproject", (1,),
        [SCALARS, grads, grads, weights, weights, full((count, width)), full((count, width)),
         full((8, width)), full((8, width)), bias, bias],
        [(full((count, width)), (count, width), F32), (full((8, width)), (8, width), F32)],
        vmem=60,
        cost=(6 * count * width * width, 20_000_000, 0),
    )(order, near, far, wq_near, wq_far, x, dh, vec, two, bias_near, bias_far)


def slope_kernel(low_ref, grad_ref, o_ref, out_ref):
    cols = grad_ref.shape[2]
    out_ref[0, :, :256] = o_ref[0]
    out_ref[0, :, 256 : 256 + cols] = dot(low_ref[...], grad_ref[0], 0, 0).astype(BF)
    out_ref[0, :, 256 + cols :] = jnp.zeros((out_ref.shape[1], SLAB - 256 - cols), BF)


def slope(low, grads, o_part):
    count, width = low.shape
    cols = grads.shape[2]
    return call(
        slope_kernel, "slope", (2,),
        [
            full((count, width)),
            pl.BlockSpec((1, count, cols), lambda g: (g, 0, 0)),
            pl.BlockSpec((1, width, 256), lambda g: (g, 0, 0)),
        ],
        [(pl.BlockSpec((1, width, SLAB), lambda g: (g, 0, 0)), (2, width, SLAB), BF)],
        cost=(4 * count * width * cols, 8_000_000, 0),
    )(low, grads, o_part)[0]


def slope_add_kernel(table, low_ref, grad_ref, o_ref, vec_ref, more_ref, out_ref, stage, sems):
    g = pl.program_id(0)
    cols = grad_ref.shape[2]
    width = low_ref.shape[1]
    rows = width // 8
    more = more_ref[...].reshape(width, SLAB).astype(F32)
    vecs = jnp.concatenate(
        [jnp.zeros((64, width), F32), vec_ref[...], jnp.zeros((56, width), F32)]
    ).T
    stage[:, :128] = (o_ref[0, :, :128].astype(F32) + more[:, :128]).astype(BF)
    stage[:, 128:256] = (o_ref[0, :, 128:].astype(F32) + vecs + more[:, 128:256]).astype(BF)
    stage[:, 256 : 256 + cols] = (
        dot(low_ref[...], grad_ref[0], 0, 0) + more[:, 256 : 256 + cols]
    ).astype(BF)
    stage[:, 256 + cols :] = jnp.zeros((width, SLAB - 256 - cols), BF)
    copies = [
        pltpu.make_async_copy(
            stage.at[pl.ds(rows * e, rows)], out_ref.at[table[8 * g + e]], sems.at[e]
        )
        for e in range(8)
    ]
    for c in copies:
        c.start()
    for c in copies:
        c.wait()


def slope_add(table, low, grads, o_part, vecs, more):
    count, width = low.shape
    cols = grads.shape[2]
    rows = width // 8
    return call(
        slope_add_kernel, "slope_add", (2,),
        [
            SCALARS,
            full((count, width)),
            pl.BlockSpec((1, count, cols), lambda g: (g, 0, 0)),
            pl.BlockSpec((1, width, 256), lambda g: (g, 0, 0)),
            full((8, width)),
            pl.BlockSpec((1, width, SLAB), lambda g: (g, 0, 0)),
        ],
        [(PLACED, (16, rows, SLAB), BF)],
        [pltpu.VMEM((width, SLAB), BF), pltpu.SemaphoreType.DMA((8,))],
        cost=(4 * count * width * cols, 14_000_000, 0),
    )(table, low, grads, o_part, vecs, more)[0]


class Place:
    def __init__(self, mesh):
        self.n_dp = mesh.shape["dp"]
        self.n_e = mesh.shape["expert"]
        self.staged = self.n_dp == 4 and self.n_e == 8
        if not self.staged:
            return
        dev = lambda x, c, z, y: (x * 2 + c) * 8 + z * 2 + y
        every = [
            (x, c, z, y) for x in range(2) for c in range(2) for z in range(4) for y in range(2)
        ]
        to = lambda move: [(dev(*p), dev(*move(*p))) for p in every]
        self.core = to(lambda x, c, z, y: (x, 1 - c, z, y))
        self.second = to(lambda x, c, z, y: (x, c, z, 1 - y) if c == 0 else (1 - x, c, z, y))
        self.third = to(lambda x, c, z, y: (1 - x, c, z, y) if c == 0 else (x, c, z, 1 - y))
        self.along = [to(lambda x, c, z, y, k=k: (x, c, z ^ k, y)) for k in range(1, 4)]

    def tables(self):
        at = jnp.arange(16, dtype=jnp.int32)
        r = jnp.arange(4, dtype=jnp.int32)
        if not self.staged:
            return jnp.concatenate([r, r]), at, at, at
        d = lax.axis_index("dp")
        e = lax.axis_index("expert")
        x, c, z, y = d // 2, d % 2, e // 2, e % 2
        order = (x ^ (r % 2)) * 2 + (c ^ (r // 2))
        back = ((r % 2) ^ c) * 2 + ((r // 2) ^ x)
        across, zr, yr = at // 8, (at % 8 // 2) ^ z, (at % 2) ^ y
        zero = jnp.where(c == 0, across * 8 + yr * 4, yr * 8 + across * 4) + zr
        one = jnp.where(c == 1, across * 8 + yr * 4, yr * 8 + across * 4) + zr
        return jnp.concatenate([order, back]), zero, one, zero


def whole_of(have):
    n_dp, n_e = lax.axis_size("dp"), lax.axis_size("expert")
    rows, cols = have.shape[1:]
    have = have.reshape(n_dp, n_e, rows, cols).transpose(1, 2, 0, 3)
    return have.reshape(n_e * rows, n_dp * cols)


def gather_all(array):
    return whole_of(lax.all_gather(array, BOTH, axis=0, tiled=False))


def scatter_all(array):
    n_dp, n_e = lax.axis_size("dp"), lax.axis_size("expert")
    rows, cols = array.shape[0] // n_e, array.shape[1] // n_dp
    parts = array.reshape(n_e, rows, n_dp, cols).transpose(2, 0, 1, 3)
    parts = parts.reshape(n_dp * n_e, rows, cols)
    return lax.psum_scatter(parts, BOTH, scatter_dimension=0, tiled=False)


def fetch(place, weights, vectors, filler):
    count = len(vectors)
    stacked = jnp.stack(vectors)
    if place.staged:
        rows, cols = weights[0].shape
        extra = jnp.concatenate([stacked.T, jnp.zeros((rows, 64 - count), BF)], axis=1)
        rest = jnp.zeros((rows, SLAB - 4 * cols - 64), BF)
        shard = jnp.concatenate([weights[0], extra, *weights[1:], rest], axis=1)
        parts = [shard] + [lax.ppermute(shard, BOTH, p) for p in place.along]
        near = jnp.stack(parts)
        near = jnp.concatenate([near, lax.ppermute(near, BOTH, place.second)])
        near, filler = lax.optimization_barrier((near, filler))
        near = jnp.concatenate([near, lax.ppermute(near, BOTH, place.third)])
        far = lax.ppermute(near, BOTH, place.core)
        return near, far, filler
    vecs = lax.all_gather(stacked, "expert", axis=1, tiled=True)
    width = vecs.shape[1]
    part = width // GROUPS
    extra = jnp.concatenate([vecs.T, jnp.zeros((width, 64 - count), BF)], axis=1)
    extra = jnp.broadcast_to(extra[None], (GROUPS, width, 64))
    by_group = lambda w: gather_all(w).reshape(width, GROUPS, part).transpose(1, 0, 2)
    grouped = [by_group(w) for w in weights]
    rest = jnp.zeros((GROUPS, width, SLAB - 4 * part - 64), BF)
    slabs = jnp.concatenate([grouped[0], extra, *grouped[1:], rest], axis=2)
    slabs = slabs.reshape(2, 16, width // 8, SLAB)
    return slabs[0], slabs[1], filler


def split(total, cols, count):
    parts = [total[:, :cols]]
    parts += [total[:, 64 + i * cols : 64 + (i + 1) * cols] for i in (1, 2, 3)]
    return parts, total[:, cols : cols + count].T


def reduce_far(place, blocks):
    return lax.ppermute(blocks, BOTH, place.core) if place.staged else jnp.zeros_like(blocks)


def reduce_near(place, have, far, vecs, count):
    add = lambda a, b: (a.astype(F32) + b.astype(F32)).astype(BF)
    if place.staged:
        got = lax.ppermute(have[8:], BOTH, place.third)
        keep, send = add(have[:4], got[:4]), add(have[4:8], got[4:])
        got = lax.ppermute(send, BOTH, place.second)
        sends = [add(keep[k], got[k]) for k in range(1, 4)]
        got = [lax.ppermute(s, BOTH, p) for s, p in zip(sends, place.along)] + [
            keep[0].astype(F32) + got[0].astype(F32)
        ]
        total = sum(g.astype(F32) for g in got)
        parts, vecs = split(total, (SLAB - 128) // 4, count)
        vecs = vecs + lax.ppermute(vecs, BOTH, place.core)
        return parts, [vecs[i] for i in range(count)]
    slabs = jnp.concatenate([have.reshape(far.shape), far])
    width = slabs.shape[1]
    part = width // GROUPS
    parts = []
    for i in range(4):
        at = i * part + (64 if i else 0)
        grad = slabs[:, :, at : at + part].transpose(1, 0, 2).reshape(width, width)
        parts.append(scatter_all(grad).astype(F32))
    vecs = lax.psum_scatter(vecs[:count], "expert", scatter_dimension=1, tiled=True)
    vecs = lax.psum(vecs, "dp")
    return parts, [vecs[i] for i in range(count)]


def shards(
    place,
    block_entries,
    assignments,
    positions_within,
    specialist_quotas,
    standardize_one_scale,
    standardize_one_shift,
    asking_weights,
    asking_shift,
    lookup_weights,
    content_weights,
    content_shift,
    context_mixing_weights,
    context_mixing_shift,
    standardize_two_scale,
    standardize_two_shift,
    gating_prototypes,
    specialist_widen_weights,
    specialist_widen_shift,
    specialist_contract_weights,
    specialist_contract_shift,
    upstream_adjoint,
):
    count, width = block_entries.shape
    experts = specialist_quotas.shape[0]
    cap = count // experts
    n_dp = place.n_dp
    order, at_near, at_far, onward = place.tables()
    barrier = lax.optimization_barrier

    chosen = assignments[:, None] == lax.broadcasted_iota(jnp.int32, (count, experts), 1)
    limit = jnp.sum(jnp.where(chosen, specialist_quotas[None, :], 0), axis=1)
    target = jnp.where(positions_within < limit, assignments * cap + positions_within, count)

    def exchange(rows):
        sent = rows.reshape(experts, -1, width)
        got = lax.all_to_all(sent, "expert", split_axis=0, concat_axis=0, tiled=True)
        return got.reshape(rows.shape)

    near, far, sent_g = fetch(
        place,
        (context_mixing_weights, asking_weights, lookup_weights, content_weights),
        (
            standardize_one_scale,
            standardize_one_shift,
            asking_shift,
            content_shift,
            context_mixing_shift,
            standardize_two_scale,
            standardize_two_shift,
        ),
        dispatch(target, upstream_adjoint),
    )
    sent_g, far = barrier((sent_g, far))
    rows_g = exchange(sent_g).reshape(experts, 2, cap // 2, width)

    wq_near, wo_near, qkv_near, low_in, vec = project(at_near, order, near, x=block_entries)
    ctx_near, lse_near = attend(qkv_near)
    wq_far, wo_far, qkv_far = project(at_far, order, far, low=low_in, vec=vec)
    ctx_far, lse_far = attend(qkv_far)
    ctx_far, rows_g = barrier((ctx_far, rows_g))
    h1, whole_o, sent_one, sent_two = mix(
        order, block_entries, ctx_near, ctx_far, wo_near, wo_far, vec, target, cap
    )

    x_one = exchange(sent_one)
    x_one, sent_two = barrier((x_one, sent_two))
    x_two = exchange(sent_two)
    matrices = (
        specialist_widen_weights[0], specialist_widen_shift, specialist_contract_weights[0],
        specialist_contract_shift, gating_prototypes,
    )
    gy, dm_one, dy_one, hid_one, du_one, dbin_one, small_one = expert(
        0, x_one, rows_g, *matrices, None
    )
    x_two, dm_one = barrier((x_two, dm_one))
    dm_one = exchange(dm_one)
    gy, dm_two, dy_two, hid_two, du_two, dbin_two, small_two = expert(
        1, x_two, rows_g, *matrices, gy
    )
    dm_one, dm_two = barrier((dm_one, dm_two))
    dm_two = exchange(dm_two)
    grads = weigh(
        n_dp, (hid_one, hid_two), (du_one, du_two), (dy_one, dy_two), (x_one, x_two),
        (dbin_one, dbin_two), (small_one, small_two),
    )
    grads, dm_two, gy = barrier((grads, dm_two, gy))
    gy = exchange(gy.reshape(count, width))
    grads = lax.psum_scatter(grads, "dp", scatter_dimension=0, tiled=False)

    dh1, dctx_near, dctx_far, wog_near, wog_far, two = unmix(
        order, h1, upstream_adjoint, dm_one, dm_two, target, ctx_near, ctx_far, whole_o, vec, cap
    )
    dqkv_far, bias_far = attend_back(qkv_far, ctx_far, dctx_far, lse_far)
    slabs_far = slope(low_in, dqkv_far, wog_far)
    more = reduce_far(place, slabs_far)
    dqkv_near, bias_near = attend_back(qkv_near, ctx_near, dctx_near, lse_near)
    input_grad, vecs = unproject(
        order, dqkv_near, dqkv_far, wq_near, wq_far, block_entries, dh1, vec, two, bias_near,
        bias_far,
    )
    dqkv_near, gy = barrier((dqkv_near, gy))
    slabs = slope_add(onward, low_in, dqkv_near, wog_near, vecs, more)
    (sum_o, sum_q, sum_k, sum_v), small = reduce_near(place, slabs, slabs_far, vecs, 7)
    output = finish(h1, target, gy)

    part = (grads.shape[0] - 16) // 2
    own = lax.axis_index("dp") * (width // n_dp)
    grad_out = grads[:part].astype(F32)[None]
    grad_in = grads[part : 2 * part].astype(F32).T[None]
    grad_bin = grads[2 * part : 2 * part + 1, :part].astype(F32)
    grad_bout = lax.dynamic_slice(
        grads[2 * part + 1 : 2 * part + 2], (0, own), (1, width // n_dp)
    ).astype(F32)
    grad_centers = grads[2 * part + 2 : 2 * part + 3].astype(F32)
    return (
        output,
        input_grad,
        small[0],
        small[1],
        sum_q,
        small[2],
        sum_k,
        sum_v,
        small[3],
        sum_o,
        small[4],
        small[5],
        small[6],
        grad_centers,
        grad_in,
        grad_bin,
        grad_out,
        grad_bout,
    )


def solution(mesh):
    placed = (
        P(("dp", "expert"), None),
        P(("dp", "expert")),
        P(("dp", "expert")),
        P(),
        P("expert"),
        P("expert"),
        P("expert", "dp"),
        P("expert"),
        P("expert", "dp"),
        P("expert", "dp"),
        P("expert"),
        P("expert", "dp"),
        P("expert"),
        P("expert"),
        P("expert"),
        P("expert", None),
        P("expert", None, None),
        P("expert", None),
        P("expert", None, None),
        P("expert", None),
        P(("dp", "expert"), None),
    )
    return jax.shard_map(
        partial(shards, Place(mesh)),
        mesh=mesh,
        in_specs=placed,
        out_specs=(
            P(("dp", "expert"), None),
            P(("dp", "expert"), None),
            P("expert"),
            P("expert"),
            P("expert", "dp"),
            P("expert"),
            P("expert", "dp"),
            P("expert", "dp"),
            P("expert"),
            P("expert", "dp"),
            P("expert"),
            P("expert"),
            P("expert"),
            P("expert", None),
            P("expert", None, "dp"),
            P("expert", "dp"),
            P("expert", "dp", None),
            P("expert", "dp"),
        ),
        check_vma=False,
    )
```

```python
from functools import partial

import jax
import jax.numpy as jnp
from jax import lax
from jax.experimental import pallas as pl
from jax.experimental.pallas import tpu as pltpu
from jax.sharding import PartitionSpec as P

HEADS = 12
HEAD_DIM = 64
SEQ_LEN = 1024
GROUPS = 4

EPSILON = 1e-05
MASKED = -1e30
SLAB = 896
BOTH = ("dp", "expert")
BF = jnp.bfloat16
F32 = jnp.float32


def dot(left, right, left_dim, right_dim):
    return lax.dot_general(
        left, right, (((left_dim,), (right_dim,)), ((), ())), preferred_element_type=F32
    )


def normalize(values):
    center = jnp.mean(values, axis=-1, keepdims=True)
    centered = values - center
    inverse = lax.rsqrt(jnp.mean(centered * centered, axis=-1, keepdims=True) + EPSILON)
    return (centered * inverse, inverse)


def normalize_back(grad, normed, inverse, gain):
    scaled = grad * gain
    return inverse * (
        scaled
        - jnp.mean(scaled, axis=-1, keepdims=True)
        - normed * jnp.mean(scaled * normed, axis=-1, keepdims=True)
    )


def call(
    kernel, name, grid, in_specs, outs, scratch=(), vmem=60, cost=(0, 0, 0), ahead=0, **more
):
    return pl.pallas_call(
        kernel,
        name=name,
        grid_spec=pltpu.PrefetchScalarGridSpec(
            num_scalar_prefetch=ahead,
            grid=grid,
            in_specs=in_specs,
            out_specs=[o[0] for o in outs],
            scratch_shapes=list(scratch),
        ),
        out_shape=[jax.ShapeDtypeStruct(o[1], o[2]) for o in outs],
        compiler_params=pltpu.CompilerParams(vmem_limit_bytes=vmem << 20),
        cost_estimate=pl.CostEstimate(
            flops=cost[0], bytes_accessed=cost[1], transcendentals=cost[2]
        ),
        **more,
    )


def full(shape):
    return pl.BlockSpec(
        shape, lambda *_: (0,) * len(shape), pipeline_mode=pl.Buffered(1)
    )


SCALARS = pl.BlockSpec(memory_space=pltpu.SMEM)
PLACED = pl.BlockSpec(memory_space=pl.ANY)


def assemble_kernel(table, own_ref, got_ref, out_ref, sems):
    rows = own_ref.shape[1]
    copies = []
    for i in range(8):
        src = (own_ref, got_ref)[i // 4].at[i % 4]
        at = pl.multiple_of(rows * table[i], 32)
        copies.append(pltpu.make_async_copy(src, out_ref.at[pl.ds(at, rows)], sems.at[i]))
    for c in copies:
        c.start()
    for c in copies:
        c.wait()


def assemble(table, own, got):
    rows, cols = own.shape[1:]
    return call(
        assemble_kernel, "assemble", (1,), [SCALARS, PLACED, PLACED],
        [(full((8 * rows, cols)), (8 * rows, cols), BF)],
        [pltpu.SemaphoreType.DMA((8,))],
        cost=(0, 4 * rows * cols * 8, 0),
    )(table, own, got)[0]


def chunk(shape, axis=0):
    return pl.BlockSpec(shape, lambda i: tuple(i if a == axis else 0 for a in range(len(shape))))


def project_kernel(half, order, *refs):
    if half:
        low_ref, vec_ref, w_one, w_two, _, qkv_ref = refs
    else:
        x_ref, w_one, w_two, qkv_ref, low_ref, vec_ref = refs
    width = low_ref.shape[1]
    part = width // GROUPS
    if not half:

        @pl.when(pl.program_id(0) == 0)
        def _():
            vec_ref[...] = w_one[:, 512:640].astype(F32).T[64:72]

        unit, _ = normalize(x_ref[...].astype(F32))
        low_ref[...] = (unit * vec_ref[0:1] + vec_ref[1:2]).astype(BF)
    zero = jnp.zeros((1, part), F32)
    for g, w_ref in enumerate((w_one, w_two)):
        bias_q = bias_v = zero
        for n in range(GROUPS):
            here = order[2 * half + g] == n
            bias_q = jnp.where(here, vec_ref[2:3, part * n : part * n + part], bias_q)
            bias_v = jnp.where(here, vec_ref[3:4, part * n : part * n + part], bias_v)
        bias = jnp.concatenate([bias_q, zero, bias_v], axis=1)
        qkv_ref[g] = (dot(low_ref[...], w_ref[:, : 3 * part], 1, 0) + bias).astype(BF)


def project(half, order, weights, x=None, low=None, vec=None, qkv=None):
    count, width = (low if half else x).shape
    part = width // GROUPS
    rows = min(256, count)
    whole = (GROUPS, count, 3 * part)
    outs = [(pl.BlockSpec((2, rows, 3 * part), lambda i: (half, i, 0)), whole, BF)]
    w = [pl.BlockSpec((width, 640), lambda i: (0, 0), pipeline_mode=pl.Buffered(1))] * 2
    if half:
        ins, args = [chunk((rows, width)), full((8, width))] + w + [PLACED], (low, vec, *weights, qkv)
    else:
        outs += [
            (chunk((rows, width)), (count, width), BF),
            (full((8, width)), (8, width), F32),
        ]
        ins, args = [chunk((rows, width))] + w, (x, *weights)
    return call(
        partial(project_kernel, half), "project", (count // rows,), [SCALARS] + ins, outs,
        cost=(2 * count * width * 6 * part, 8_000_000, 0),
        input_output_aliases={5: 0} if half else {},
    )(order, *args)


def attend_kernel(qkv_ref, *refs):
    ctx_ref, lse_ref = refs[-2:]
    length = qkv_ref.shape[1]
    width = qkv_ref.shape[2] // 3
    block = min(256, length)
    lane = lax.broadcasted_iota(jnp.int32, (block, 128), 1)
    row = lax.broadcasted_iota(jnp.int32, (block, block), 0)
    col = lax.broadcasted_iota(jnp.int32, (block, block), 1)
    for i in range(length // block):
        start = i * block
        stats = jnp.zeros((block, 128), F32)
        for h in range(width // HEAD_DIM):
            at = h * HEAD_DIM
            q = qkv_ref[0, start : start + block, at : at + HEAD_DIM] * BF(HEAD_DIM**-0.5)
            k = qkv_ref[0, : start + block, width + at : width + at + HEAD_DIM]
            v = qkv_ref[0, : start + block, 2 * width + at : 2 * width + at + HEAD_DIM]
            diag = jnp.where(col <= row, dot(q, k[start:], 1, 1), MASKED)
            top = jnp.max(diag, axis=-1, keepdims=True)
            if start:
                past = dot(q, k[:start], 1, 1)
                top = jnp.maximum(top, jnp.max(past, axis=-1, keepdims=True))
            diag = jnp.exp(diag - top)
            total = jnp.sum(diag, axis=-1, keepdims=True)
            out = dot(diag.astype(BF), v[start:], 1, 0)
            if start:
                past = jnp.exp(past - top)
                total += jnp.sum(past, axis=-1, keepdims=True)
                out += dot(past.astype(BF), v[:start], 1, 0)
            ctx_ref[0, start : start + block, at : at + HEAD_DIM] = (out / total).astype(BF)
            stats = jnp.where(lane == h, top + jnp.log(total), stats)
        lse_ref[0, start : start + block, :] = stats


def attend(half, qkv, before=()):
    groups, length, width = qkv.shape
    width //= 3
    at = lambda g, s: (2 * half + g, s, 0)
    return call(
        attend_kernel, "attend", (2, length // SEQ_LEN),
        [pl.BlockSpec((1, SEQ_LEN, 3 * width), at)] + [PLACED] * len(before),
        [
            (pl.BlockSpec((1, SEQ_LEN, width), at), (groups, length, width), BF),
            (pl.BlockSpec((1, SEQ_LEN, 128), at), (groups, length, 128), F32),
        ],
        cost=(8_000_000_000, 5_000_000, 4_000_000),
        input_output_aliases={1 + i: i for i in range(len(before))},
    )(qkv, *before)


def attend_back_kernel(qkv_ref, ctx_ref, dctx_ref, lse_ref, *refs):
    out_ref, sum_ref, dq_ref = refs[-3:]
    length = qkv_ref.shape[1]
    width = qkv_ref.shape[2] // 3
    heads = width // HEAD_DIM
    block = min(256, length)
    lane = lax.broadcasted_iota(jnp.int32, (length, 128), 1)
    stats = lse_ref[0]
    for h in range(heads):
        at = h * HEAD_DIM
        o = ctx_ref[0, :, at : at + HEAD_DIM].astype(F32)
        do = dctx_ref[0, :, at : at + HEAD_DIM].astype(F32)
        stats = jnp.where(lane == 8 + h, jnp.sum(o * do, axis=-1, keepdims=True), stats)
    stats = stats.T
    row = lax.broadcasted_iota(jnp.int32, (block, block), 0)
    col = lax.broadcasted_iota(jnp.int32, (block, block), 1)
    for h in range(heads):
        at = h * HEAD_DIM
        q = qkv_ref[0, :, at : at + HEAD_DIM] * BF(HEAD_DIM**-0.5)
        do = dctx_ref[0, :, at : at + HEAD_DIM]
        for j in range(length // block):
            start = j * block
            k = qkv_ref[0, start : start + block, width + at : width + at + HEAD_DIM]
            v = qkv_ref[0, start : start + block, 2 * width + at : 2 * width + at + HEAD_DIM]
            dk = None
            for s, e, on_diag in ((start, start + block, True), (start + block, length, False)):
                if s == e:
                    continue
                lse = stats[h : h + 1, s:e]
                inner = stats[8 + h : 9 + h, s:e]
                probs = jnp.exp(dot(k, q[s:e], 1, 1) - lse)
                if on_diag:
                    probs = jnp.where(row <= col, probs, 0.0)
                dscores = (probs * (dot(v, do[s:e], 1, 1) - inner)).astype(BF)
                dk_part = dot(dscores, q[s:e], 1, 0)
                dv_part = dot(probs.astype(BF), do[s:e], 1, 0)
                dq_part = dot(dscores, k, 0, 0)
                dk = dk_part if dk is None else dk + dk_part
                dv = dv_part if on_diag else dv + dv_part
                if j == 0:
                    dq_ref[s:e, :] = dq_part
                else:
                    dq_ref[s:e, :] += dq_part
            out_ref[0, start : start + block, width + at : width + at + HEAD_DIM] = dk.astype(BF)
            out_ref[0, start : start + block, 2 * width + at : 2 * width + at + HEAD_DIM] = (
                dv.astype(BF)
            )
        out_ref[0, :, at : at + HEAD_DIM] = (dq_ref[...] * HEAD_DIM**-0.5).astype(BF)
    sums = jnp.sum(out_ref[0].astype(F32), axis=0, keepdims=True)
    first = pl.program_id(0) == 0

    @pl.when(first)
    def _():
        sum_ref[0] = jnp.broadcast_to(sums, sum_ref.shape[1:])

    @pl.when(jnp.logical_not(first))
    def _():
        sum_ref[0] += jnp.broadcast_to(sums, sum_ref.shape[1:])


def attend_back(group, qkv, ctx, dctx, lse):
    groups, length, width = qkv.shape
    width //= 3
    at = lambda s: (group, s, 0)
    return call(
        attend_back_kernel, "attend_back", (length // SEQ_LEN,),
        [
            pl.BlockSpec((1, SEQ_LEN, 3 * width), at),
            pl.BlockSpec((1, SEQ_LEN, width), at),
            pl.BlockSpec((1, SEQ_LEN, width), at),
            pl.BlockSpec((1, SEQ_LEN, 128), at),
        ],
        [
            (pl.BlockSpec((1, SEQ_LEN, 3 * width), lambda s: (0, s, 0)), (1, length, 3 * width), BF),
            (full((1, 8, 3 * width)), (1, 8, 3 * width), F32),
        ],
        [pltpu.VMEM((SEQ_LEN, HEAD_DIM), F32)],
        cost=(10_000_000_000, 4_000_000, 2_000_000),
    )(qkv, ctx, dctx, lse)


def slot_of(index, half, cap):
    return index // (cap // 2) * cap + index % (cap // 2) + half * (cap // 2)


def dispatch_kernel(target_ref, rows_ref, out_ref):
    count = rows_ref.shape[0]
    for at in range(0, count, 256):
        slot = lax.broadcasted_iota(jnp.int32, (256, count), 0) + at
        picks = (target_ref[...] == slot).astype(F32).astype(BF)
        out_ref[at : at + 256] = dot(picks, rows_ref[...], 1, 0).astype(BF)


def dispatch(target, rows):
    count, width = rows.shape
    return call(
        dispatch_kernel, "dispatch", (1,),
        [full((1, count)), full((count, width))],
        [(full((count, width)), (count, width), BF)],
        cost=(2 * count * count * width, 3_000_000, 0),
    )(target.reshape(1, count), rows)[0]


def mix_kernel(cap, order, x_ref, ctx_ref, vec_ref, target_ref, *refs):
    wo_refs, (h_ref, whole_ref, *sent, low_ref) = refs[:GROUPS], refs[GROUPS:]
    rows, width = x_ref.shape
    count = low_ref.shape[0]
    part = width // GROUPS
    step = pl.program_id(0)

    @pl.when(step == 0)
    def _():
        for q in range(GROUPS):
            at = pl.ds(pl.multiple_of(order[q] * part, 64), part)
            pieces = [wo[at, :part] for wo in wo_refs]
            for n in range(GROUPS):
                piece = pieces[0]
                for r in range(1, GROUPS):
                    piece = jnp.where(order[r] == n, pieces[r], piece)
                whole_ref[q * part : q * part + part, n * part : n * part + part] = piece

    h = x_ref[...].astype(F32) + vec_ref[4:5]
    for r in range(GROUPS):
        h += dot(ctx_ref[r], whole_ref[r * part : r * part + part], 1, 0)
    h_ref[...] = h
    unit, _ = normalize(h)
    low_ref[pl.ds(pl.multiple_of(step * rows, 256), rows)] = (
        unit * vec_ref[5:6] + vec_ref[6:7]
    ).astype(BF)

    @pl.when(step == pl.num_programs(0) - 1)
    def _():
        for half in range(2):
            for at in range(0, count // 2, 256):
                index = lax.broadcasted_iota(jnp.int32, (256, count), 0) + at
                picks = (target_ref[...] == slot_of(index, half, cap)).astype(F32).astype(BF)
                sent[half][at : at + 256] = dot(picks, low_ref[...], 1, 0).astype(BF)


def mix(order, x, ctx, weights, vec, target, cap):
    count, width = x.shape
    part = width // GROUPS
    rows = min(256, count)
    columns = pl.BlockSpec(
        (pl.Element(width), pl.Element(256)), lambda *_: (0, 640), pipeline_mode=pl.Buffered(1)
    )
    return call(
        partial(mix_kernel, cap), "mix", (count // rows,),
        [SCALARS, chunk((rows, width)), chunk((GROUPS, rows, part), 1), full((8, width)),
         full((1, count))] + [columns] * GROUPS,
        [
            (chunk((rows, width)), (count, width), F32),
            (full((width, width)), (width, width), BF),
            (full((count // 2, width)), (count // 2, width), BF),
            (full((count // 2, width)), (count // 2, width), BF),
        ],
        [pltpu.VMEM((count, width), BF)],
        cost=(2 * count * width * (width + count), 12_000_000, 0),
    )(order, x, ctx, vec, target.reshape(1, count), *weights)


def unmix_kernel(
    cap, order, h_ref, g_ref, dm_one, dm_two, target_ref, ctx_ref, whole_ref, vec_ref,
    dh_ref, dctx_ref, grad_ref, sum_ref, total_ref,
):
    rows, width = h_ref.shape
    part = width // GROUPS
    step = pl.program_id(0)
    dm = None
    for half, sent in enumerate((dm_one, dm_two)):
        index = lax.broadcasted_iota(jnp.int32, (rows, sent.shape[0]), 1)
        picks = (target_ref[...] == slot_of(index, half, cap)).astype(F32).astype(BF)
        got = dot(picks, sent[...], 1, 0)
        dm = got if dm is None else dm + got
    unit, inverse = normalize(h_ref[...])
    dh = g_ref[...].astype(F32) + normalize_back(dm, unit, inverse, vec_ref[5:6])
    dh_ref[...] = dh
    low = dh.astype(BF)
    sums = [
        jnp.sum(term, axis=0, keepdims=True) for term in (low.astype(F32), dm * unit, dm)
    ]
    zeros = jnp.zeros((1, width), F32)
    sums = jnp.concatenate([zeros] * 4 + sums + [zeros])
    for r in range(GROUPS):
        dctx_ref[r] = dot(low, whole_ref[r * part : r * part + part], 1, 1).astype(BF)
    grads = [dot(ctx_ref[q], low, 0, 0) for q in range(GROUPS)]

    @pl.when(step == 0)
    def _():
        sum_ref[...] = sums
        for q in range(GROUPS):
            total_ref[q] = grads[q]

    @pl.when(step > 0)
    def _():
        sum_ref[...] += sums
        for q in range(GROUPS):
            total_ref[q] += grads[q]

    @pl.when(step == pl.num_programs(0) - 1)
    def _():
        for q in range(GROUPS):
            grad = total_ref[q].astype(BF)
            at = pl.ds(pl.multiple_of(order[q] * part, 64), part)
            for r in range(GROUPS):
                piece = grad[:, :part]
                for n in range(1, GROUPS):
                    piece = jnp.where(order[r] == n, grad[:, n * part : n * part + part], piece)
                grad_ref[r, at, :] = piece


def unmix(order, h, g, dm_one, dm_two, target, ctx, whole, vec, cap):
    count, width = h.shape
    part = width // GROUPS
    rows = min(256, count)
    half = full((count // 2, width))
    by_rows, by_ctx = chunk((rows, width)), chunk((GROUPS, rows, part), 1)
    return call(
        partial(unmix_kernel, cap), "unmix", (count // rows,),
        [SCALARS, by_rows, by_rows, half, half, chunk((rows, 1)), by_ctx, full((width, width)),
         full((8, width))],
        [
            (by_rows, (count, width), F32),
            (by_ctx, (GROUPS, count, part), BF),
            (full((GROUPS, width, part)), (GROUPS, width, part), BF),
            (full((8, width)), (8, width), F32),
        ],
        [pltpu.VMEM((GROUPS, part, width), F32)],
        cost=(2 * count * width * (2 * width + count), 20_000_000, 0),
    )(order, h, g, dm_one, dm_two, target.reshape(count, 1), ctx, whole, vec)


def finish_kernel(h_ref, target_ref, gy_ref, out_ref):
    slot = lax.broadcasted_iota(jnp.int32, (h_ref.shape[0], gy_ref.shape[0]), 1)
    picks = (target_ref[...] == slot).astype(F32).astype(BF)
    out_ref[...] = (h_ref[...] + dot(picks, gy_ref[...], 1, 0)).astype(BF)


def finish(h, target, gy):
    count, width = h.shape
    rows = min(256, count)
    return call(
        finish_kernel, "finish", (count // rows,),
        [chunk((rows, width)), chunk((rows, 1)), full((count, width))],
        [(chunk((rows, width)), (count, width), BF)],
        cost=(2 * count * count * width, 6_000_000, 0),
    )(h, target.reshape(count, 1), gy)[0]


ERFC = (
    0.169189354,
    0.1706909295,
    0.1485212475,
    0.2141814502,
    -0.09282610738,
    0.5449670381,
    -0.5097724612,
    0.4843017683,
    -0.1292532277,
)


def gelu_pair(v):
    a = jnp.abs(v) * (0.5**0.5)
    bell = jnp.exp(-0.5 * v * v)
    t = 1.0 / (1.0 + 0.3 * a)
    poly = jnp.full_like(v, ERFC[-1])
    for c in ERFC[-2::-1]:
        poly = poly * t + c
    tail = 0.5 * bell * t * poly
    cdf = jnp.where(v < 0, tail, 1.0 - tail)
    return v * cdf, cdf + v * bell * (0.5 / jnp.pi) ** 0.5


def expert_kernel(
    x_ref, g_ref, win_ref, bin_ref, wout_ref, bout_ref, center_ref, _,
    gy_ref, dm_ref, dy_ref, hid_ref, du_ref, dbin_ref, small_ref,
    y_acc, dm_acc, gate_ref, gates,
):
    step = pl.program_id(0)
    rows, width = x_ref.shape

    @pl.when(step == 0)
    def _():
        z = jnp.sum(x_ref[...].astype(F32) * center_ref[...].astype(F32), axis=-1, keepdims=True)
        gate = 1.0 / (1.0 + jnp.exp(-z))
        gate_ref[...] = jnp.broadcast_to(gate, gate_ref.shape)
        dy_ref[...] = (gate * g_ref[...].reshape(rows, width).astype(F32)).astype(BF)

    act, slope = gelu_pair(dot(x_ref[...], win_ref[...], 1, 0) + bin_ref[...].astype(F32))
    hid = act.astype(BF)
    hid_ref[...] = hid
    y = dot(hid, wout_ref[...], 1, 0)
    du = (dot(dy_ref[...], wout_ref[...], 1, 1) * slope).astype(BF)
    du_ref[...] = du
    dbin_ref[...] = jnp.broadcast_to(
        jnp.sum(du.astype(F32), axis=0, keepdims=True), dbin_ref.shape
    )
    dm = dot(du, win_ref[...], 1, 1)

    @pl.when(step == 0)
    def _():
        y_acc[...] = y
        dm_acc[...] = dm

    @pl.when(step > 0)
    def _():
        y_acc[...] += y
        dm_acc[...] += dm

    @pl.when(step == pl.num_programs(0) - 1)
    def _():
        gate = gate_ref[:, :1]
        g = g_ref[...].reshape(rows, width).astype(F32)
        y = (y_acc[...] + bout_ref[...].astype(F32)).astype(BF).astype(F32)
        gy_ref[...] = (gate * y).astype(BF).reshape(gy_ref.shape)
        dz = gate * (1.0 - gate) * jnp.sum(g * y, axis=-1, keepdims=True)
        dm_ref[...] = (dm_acc[...] + dz * center_ref[...].astype(F32)).astype(BF)
        small_ref[0:1, :] = jnp.sum(dy_ref[...].astype(F32), axis=0, keepdims=True)
        small_ref[1:2, :] = jnp.sum(dz * x_ref[...].astype(F32), axis=0, keepdims=True)


def expert(half, x, g, win, bias_in, wout, bias_out, center, gy):
    rows, width = x.shape
    ff = win.shape[1]
    step = min(512, ff)
    along = lambda i: (0, i)
    side = pl.BlockSpec(
        (g.shape[0], 1) + g.shape[2:], lambda i: (0, half, 0, 0), pipeline_mode=pl.Buffered(1)
    )
    return call(
        expert_kernel, "expert", (ff // step,),
        [
            full((rows, width)),
            side,
            pl.BlockSpec((width, step), along),
            pl.BlockSpec((1, step), along),
            pl.BlockSpec((step, width), lambda i: (i, 0)),
            full((1, width)),
            full((1, width)),
            PLACED,
        ],
        [
            (side, g.shape, BF),
            (full((rows, width)), (rows, width), BF),
            (full((rows, width)), (rows, width), BF),
            (pl.BlockSpec((rows, step), along), (rows, ff), BF),
            (pl.BlockSpec((rows, step), along), (rows, ff), BF),
            (pl.BlockSpec((8, step), along), (8, ff), F32),
            (full((8, width)), (8, width), F32),
        ],
        [
            pltpu.VMEM((rows, width), F32),
            pltpu.VMEM((rows, width), F32),
            pltpu.VMEM((rows, 128), F32),
            pltpu.SMEM((1,), jnp.int32),
        ],
        cost=(8 * rows * width * ff, 22_000_000, 2 * rows * ff),
        input_output_aliases={} if gy is None else {7: 0},
    )(x, g, win, bias_in, wout, bias_out, center, x if gy is None else gy)


def weigh_kernel(split, which, *refs):
    hid, du, dy, x, bias, small = (refs[i : i + 2] for i in range(0, 12, 2))
    ff = hid[0].shape[1]
    width = dy[0].shape[1]
    step = pl.program_id(0)
    small = small[0][...] + small[1][...]
    row = lax.broadcasted_iota(jnp.int32, (16, width), 0)
    bias = (bias[0][...] + bias[1][...])[0:1]
    if ff < width:
        bias = jnp.concatenate([bias, jnp.zeros((1, width - ff), F32)], axis=1)
    rest = jnp.where(row == 0, bias, 0.0)
    rest = jnp.where(row == 1, small[0:1], rest)
    rest = jnp.where(row == 2, small[1:2], rest)

    def pair(i):
        rows, cols = (x, du) if split else (du, x)
        return rows[i][...], cols[i][...]

    def put(out):
        out[:ff] = (dot(hid[0][...], dy[0][...], 0, 0) + dot(hid[1][...], dy[1][...], 0, 0)).astype(BF)
        out[ff : 2 * ff] = (
            dot(*pair(0), 0, 0) + dot(*pair(1), 0, 0)
        ).astype(BF)
        out[2 * ff :] = rest.astype(BF)

    if not split:
        put(refs[12].at[0])
        return
    far_ref, across_ref, own_ref, total = refs[12:]
    put(total)
    for at, out in ((0, far_ref.at[0]), (1, far_ref.at[0]), (2, across_ref), (3, own_ref)):

        @pl.when(step == at)
        def _(out=out):
            out[...] = total[...]


def weigh(which, n, split, hid, du, dy, x, bias, small):
    rows, ff = hid[0].shape
    width = dy[0].shape[1]
    part = ff // n
    size = 2 * part + 16
    along = lambda i, which: (0, which[i])
    wide = pl.BlockSpec((rows, part), along)
    if split:
        first = pl.BlockSpec((1, size, width), lambda i, which: (jnp.minimum(i, 1), 0, 0))
        outs = [(first, (2, size, width), BF)] + [(full((size, width)), (size, width), BF)] * 2
        scratch = [pltpu.VMEM((size, width), BF)]
    else:
        outs = [(pl.BlockSpec((1, size, width), lambda i, which: (i, 0, 0)), (n, size, width), BF)]
        scratch = []
    got = call(
        partial(weigh_kernel, split), "weigh", (n,),
        [wide] * 4 + [full((rows, width))] * 4 + [pl.BlockSpec((8, part), along)] * 2
        + [full((8, width))] * 2,
        outs, scratch,
        cost=(8 * rows * width * ff, 26_000_000, 0), ahead=1,
    )(which, *hid, *du, *dy, *x, *bias, *small)
    return got if split else got[0]


def unproject_kernel(*refs):
    grad_refs, w_refs = refs[:GROUPS], refs[GROUPS : 2 * GROUPS]
    x_ref, dh_ref, vec_ref, out_ref = refs[2 * GROUPS :]
    part = x_ref.shape[1] // GROUPS
    da = None
    for grad, w in zip(grad_refs, w_refs):
        got = dot(grad[0], w[:, : 3 * part], 1, 1)
        da = got if da is None else da + got
    unit, inverse = normalize(x_ref[...].astype(F32))
    out_ref[...] = dh_ref[...] + normalize_back(da, unit, inverse, vec_ref[0:1])


def unproject(grads, weights, x, dh, vec):
    count, width = x.shape
    part = width // GROUPS
    rows = min(256, count)
    w = pl.BlockSpec((width, 640), lambda i: (0, 0), pipeline_mode=pl.Buffered(1))
    return call(
        unproject_kernel, "unproject", (count // rows,),
        [chunk((1, rows, 3 * part), 1)] * GROUPS + [w] * GROUPS
        + [chunk((rows, width)), chunk((rows, width)), full((8, width))],
        [(chunk((rows, width)), (count, width), F32)],
        cost=(6 * count * width * width, 20_000_000, 0),
    )(*grads, *weights, x, dh, vec)[0]


def slope_kernel(group, extra, staged, halves, order, *refs):
    if staged:
        table, *refs = refs
    low_ref, grad_ref, sum_ref, o_ref, w_ref, two_ref = refs[:6]
    more, refs = refs[6 : 6 + extra], refs[6 + extra :]
    if staged:
        keep_ref, send_ref, stage, sems = refs
    elif halves:
        outs = refs
    else:
        outs = refs[:1]
    width = low_ref.shape[1]
    part = width // GROUPS
    grad = dot(low_ref[...], grad_ref[0], 0, 0)
    w = w_ref[...].astype(F32)
    sums = sum_ref[0, 0:1]
    shift = jnp.sum(w[:, : 3 * part] * sums, axis=-1, keepdims=True)
    gain = jnp.sum(w[:, : 3 * part] * grad, axis=-1, keepdims=True)
    gain = (gain - w[:, 577:578] * shift) / w[:, 576:577]
    row = lax.broadcasted_iota(jnp.int32, (width, part), 0) - order[group] * part
    here = row == lax.broadcasted_iota(jnp.int32, (width, part), 1)
    columns = [gain, shift] + [
        jnp.sum(jnp.where(here, sums[:, at : at + part], 0.0), axis=-1, keepdims=True)
        for at in (0, 2 * part)
    ]
    lane = lax.broadcasted_iota(jnp.int32, (width, 64), 1)
    if group:
        vecs = jnp.zeros((width, 64), F32)
    else:
        vecs = jnp.concatenate([two_ref[...], jnp.zeros((120, width), F32)]).T[:, :64]
    for i, column in enumerate(columns):
        vecs = jnp.where(lane == i, column, vecs)
    o = o_ref[0].astype(F32)
    if extra:
        more = [more[:1]] + [more[1:]] * (extra > 1)
    for refs in more:
        got = jnp.concatenate([ref[...] for ref in refs]) if len(refs) > 1 else refs[0][...]
        grad += got[:, : 3 * part].astype(F32)
        vecs += got[:, 3 * part : 640].astype(F32)
        o += got[:, 640 : 640 + part].astype(F32)
    if staged:
        outs = (stage,)
    rows = width // len(outs)
    for i, out in enumerate(outs):
        at = slice(i * rows, i * rows + rows)
        out[:, : 3 * part] = grad[at].astype(BF)
        out[:, 3 * part : 640] = vecs[at].astype(BF)
        out[:, 640 : 640 + part] = o[at].astype(BF)
        out[:, 640 + part :] = jnp.zeros((rows, SLAB - 640 - part), BF)
    if staged:
        rows = width // 8
        copies = []
        for i in range(8):
            src = stage.at[pl.ds(pl.multiple_of(rows * table[i], 32), rows)]
            copies.append(
                pltpu.make_async_copy(src, (keep_ref, send_ref)[i // 4].at[i % 4], sems.at[i])
            )
        for c in copies:
            c.start()
        for c in copies:
            c.wait()


def slope(group, order, low, grads, o_part, w, two, more=(), table=None, halves=False):
    count, width = low.shape
    part = width // GROUPS
    cols = 3 * part
    ins = [
        full((count, width)),
        full((1, count, cols)),
        full((1, 8, cols)),
        pl.BlockSpec((1, width, part), lambda i: (group, 0, 0)),
        pl.BlockSpec((width, 640), lambda i: (0, 0), pipeline_mode=pl.Buffered(1)),
        full((8, width)),
    ] + [full(m.shape) for m in more]
    args = (low, *grads, o_part, w, two, *more)
    if table is None:
        rows = width // (1 + halves)
        outs, scratch = [(full((rows, SLAB)), (rows, SLAB), BF)] * (1 + halves), []
    else:
        ins, args = [SCALARS] + ins, (table, *args)
        outs = [(PLACED, (4, width // 8, SLAB), BF)] * 2
        scratch = [pltpu.VMEM((width, SLAB), BF), pltpu.SemaphoreType.DMA((8,))]
    got = call(
        partial(slope_kernel, group, len(more), table is not None, halves), "slope", (1,),
        [SCALARS] + ins, outs, scratch,
        cost=(2 * count * width * cols, 6_000_000, 0),
    )(order, *args)
    return got if table is not None or halves else got[0]


def add(a, b):
    return (a.astype(F32) + b.astype(F32)).astype(BF)


class Place:
    def __init__(self, mesh):
        self.n_dp = mesh.shape["dp"]
        self.n_e = mesh.shape["expert"]
        self.staged = self.n_dp == 4 and self.n_e == 8
        if not self.staged:
            return
        dev = lambda x, c, z, y: (x * 2 + c) * 8 + z * 2 + y
        every = [
            (x, c, z, y) for x in range(2) for c in range(2) for z in range(4) for y in range(2)
        ]
        to = lambda move: [(dev(*p), dev(*move(*p))) for p in every]
        self.core = to(lambda x, c, z, y: (x, 1 - c, z, y))
        self.x = to(lambda x, c, z, y: (1 - x, c, z, y))
        self.y = to(lambda x, c, z, y: (x, c, z, 1 - y))
        self.z = [to(lambda x, c, z, y, k=k: (x, c, z ^ k, y)) for k in range(1, 4)]

    def tables(self):
        r = jnp.arange(4, dtype=jnp.int32)
        i = jnp.arange(8, dtype=jnp.int32)
        if not self.staged:
            return r, i, r
        d, e = lax.axis_index("dp"), lax.axis_index("expert")
        z, y = e // 2, e % 2
        weighed = d ^ jnp.where(r < 2, 3 - 2 * r, 6 - 2 * r)
        return d ^ r, (z ^ i % 4) * 2 + (y ^ i // 4), weighed

    def move(self, array, way):
        return lax.ppermute(array, BOTH, way)


def whole_of(have):
    n_dp, n_e = lax.axis_size("dp"), lax.axis_size("expert")
    rows, cols = have.shape[1:]
    have = have.reshape(n_dp, n_e, rows, cols).transpose(1, 2, 0, 3)
    return have.reshape(n_e * rows, n_dp * cols)


def gather_all(array):
    return whole_of(lax.all_gather(array, BOTH, axis=0, tiled=False))


def scatter_all(array):
    n_dp, n_e = lax.axis_size("dp"), lax.axis_size("expert")
    rows, cols = array.shape[0] // n_e, array.shape[1] // n_dp
    parts = array.reshape(n_e, rows, n_dp, cols).transpose(2, 0, 1, 3)
    parts = parts.reshape(n_dp * n_e, rows, cols)
    return lax.psum_scatter(parts, BOTH, scatter_dimension=0, tiled=False)


def fetch(place, table, weights, vectors, filler):
    stacked = jnp.stack(vectors)
    pad = 64 - len(vectors)
    if place.staged:
        rows, cols = weights[0].shape
        extra = jnp.concatenate([stacked.T, jnp.zeros((rows, pad), BF)], axis=1)
        rest = jnp.zeros((rows, SLAB - 64 - 4 * cols), BF)
        shard = jnp.concatenate([*weights[:3], extra, weights[3], rest], axis=1)
        own = jnp.stack([shard] + [place.move(shard, way) for way in place.z])
        got = place.move(own, place.y)
        got, filler = lax.optimization_barrier((got, filler))
        near = assemble(table, own, got)
        across = place.move(near, place.x)
        far = place.move(near, place.core)
        return near, far, across, filler
    vecs = lax.all_gather(stacked, "expert", axis=1, tiled=True)
    width = vecs.shape[1]
    extra = jnp.concatenate([vecs, jnp.zeros((pad, width), BF)]).T
    extra = jnp.broadcast_to(extra[None], (GROUPS, width, 64))
    by_group = lambda w: gather_all(w).reshape(width, GROUPS, -1).transpose(1, 0, 2)
    weights = [by_group(w) for w in weights]
    rest = jnp.zeros((GROUPS, width, SLAB - 64 - 4 * (width // GROUPS)), BF)
    grouped = jnp.concatenate([*weights[:3], extra, weights[3], rest], axis=2)
    return grouped[0], grouped[1], grouped[2:], filler


def reduce_last(place, keep, send, count, first, second, later):
    barrier = lax.optimization_barrier
    cols = (SLAB - 128) // 4
    got, first, later = barrier((place.move(send, place.y), first(), later))
    sends = [add(keep[k], got[k]) for k in range(1, 4)]
    total = keep[0].astype(F32) + got[0].astype(F32)
    got = [place.move(part, way) for part, way in zip(sends, place.z)]
    got, second = barrier((got, second(*later)))
    for part in got:
        total += part.astype(F32)
    parts = [total[:, i : i + cols] for i in (0, cols, 2 * cols, 640)]
    vecs = total[:, 576 : 576 + 8].T
    vecs = vecs + place.move(vecs, place.core)
    vecs = vecs + place.move(vecs, place.x)
    return parts, [vecs[i] for i in range(count)], first, second


def reduce_plain(slabs, count):
    slabs = jnp.stack(slabs)
    width = slabs.shape[1]
    part = width // GROUPS
    parts = []
    for at in (0, part, 2 * part, 640):
        grad = slabs[:, :, at : at + part].transpose(1, 0, 2).reshape(width, width)
        parts.append(scatter_all(grad).astype(F32))
    vecs = jnp.sum(slabs[:, :, 576 : 576 + count].astype(F32), axis=0).T
    vecs = lax.psum_scatter(vecs, "expert", scatter_dimension=1, tiled=True)
    vecs = lax.psum(vecs, "dp")
    return parts, [vecs[i] for i in range(count)]


def shards(
    place,
    block_entries,
    assignments,
    positions_within,
    specialist_quotas,
    standardize_one_scale,
    standardize_one_shift,
    asking_weights,
    asking_shift,
    lookup_weights,
    content_weights,
    content_shift,
    context_mixing_weights,
    context_mixing_shift,
    standardize_two_scale,
    standardize_two_shift,
    gating_prototypes,
    specialist_widen_weights,
    specialist_widen_shift,
    specialist_contract_weights,
    specialist_contract_shift,
    upstream_adjoint,
):
    count, width = block_entries.shape
    experts = specialist_quotas.shape[0]
    cap = count // experts
    n_dp = place.n_dp
    order, table, weighed = place.tables()
    barrier = lax.optimization_barrier

    chosen = assignments[:, None] == lax.broadcasted_iota(jnp.int32, (count, experts), 1)
    limit = jnp.sum(jnp.where(chosen, specialist_quotas[None, :], 0), axis=1)
    target = jnp.where(positions_within < limit, assignments * cap + positions_within, count)

    def exchange(rows):
        sent = rows.reshape(experts, -1, width)
        got = lax.all_to_all(sent, "expert", split_axis=0, concat_axis=0, tiled=True)
        return got.reshape(rows.shape)

    near, far, across, sent_g = fetch(
        place,
        table,
        (asking_weights, lookup_weights, content_weights, context_mixing_weights),
        (
            standardize_one_scale,
            standardize_one_shift,
            asking_shift,
            content_shift,
            context_mixing_shift,
            standardize_two_scale,
            standardize_two_shift,
        ),
        dispatch(target, upstream_adjoint),
    )
    sent_g, far = barrier((sent_g, far))
    rows_g = exchange(sent_g).reshape(experts, 2, cap // 2, width)

    qkv, low_in, vec = project(0, order, (near, far), x=block_entries)
    ctx = attend(0, qkv)
    if place.staged:
        ctx, across = barrier((ctx, across))
        weights = (near, far, across, place.move(across, place.core))
    else:
        weights = (near, far, across[0], across[1])
    (qkv,) = project(1, order, weights[2:], low=low_in, vec=vec, qkv=qkv)
    ctx, lse = attend(1, qkv, ctx)
    ctx, rows_g = barrier((ctx, rows_g))
    h1, whole_o, sent_one, sent_two = mix(order, block_entries, ctx, weights, vec, target, cap)

    x_one = exchange(sent_one)
    x_one, sent_two = barrier((x_one, sent_two))
    x_two = exchange(sent_two)
    matrices = (
        specialist_widen_weights[0], specialist_widen_shift, specialist_contract_weights[0],
        specialist_contract_shift, gating_prototypes,
    )
    gy, dm_one, dy_one, hid_one, du_one, dbin_one, small_one = expert(
        0, x_one, rows_g, *matrices, None
    )
    x_two, dm_one = barrier((x_two, dm_one))
    dm_one = exchange(dm_one)
    gy, dm_two, dy_two, hid_two, du_two, dbin_two, small_two = expert(
        1, x_two, rows_g, *matrices, gy
    )
    dm_one, dm_two, hid_two = barrier((dm_one, dm_two, hid_two))
    dm_two = exchange(dm_two)
    sides = (
        (hid_one, hid_two), (du_one, du_two), (dy_one, dy_two), (x_one, x_two),
        (dbin_one, dbin_two), (small_one, small_two),
    )
    if place.staged:
        grads_far, grads_across, grads = weigh(
            weighed, n_dp, True, *sides
        )
        grads_far, gy, dm_two = barrier((grads_far, gy, dm_two))
        came_far = place.move(grads_far, place.core)
        crossing = add(grads_across, came_far[0])
        crossing, h1 = barrier((crossing, h1))
        came = place.move(crossing, place.x)
    else:
        grads = weigh(jnp.arange(n_dp, dtype=jnp.int32), n_dp, False, *sides)
        grads = lax.psum_scatter(grads, "dp", scatter_dimension=0, tiled=False)
    gy = exchange(gy.reshape(count, width))

    dh1, dctx, grad_o, two = unmix(
        order, h1, upstream_adjoint, dm_one, dm_two, target, ctx, whole_o, vec, cap
    )
    back = lambda r, dctx: attend_back(r, qkv, ctx, dctx, lse)
    tilt = lambda r, grads, *rest: slope(r, order, low_in, grads, grad_o, weights[r], two, *rest)
    if place.staged:
        three = back(3, dctx)
        slab = tilt(3, three)
        dctx, slab = barrier((dctx, slab))
        more = place.move(slab, place.core)
        duo = back(2, dctx)
        slab, rest = tilt(2, duo, (more,), None, True)
        dctx, slab, rest, gy, came = barrier((dctx, slab, rest, gy, came))
        across = place.move(slab, place.x)
        one = back(1, dctx)
        slab = tilt(1, one)
        dctx, slab, across = barrier((dctx, slab, across))
        more = place.move(slab, place.core)
        across = (across, place.move(rest, place.x))
        zero = back(0, dctx)
        keep, send = tilt(0, zero, (more, *across), table)
        last, send, came, gy = barrier((zero[0], send, came, gy))
        dqkv = (last, one[0], duo[0], three[0])

        def finishing(gy, came):
            pick = lambda at: sum(
                a[at : at + width].astype(F32) for a in (grads, came_far[1], came)
            )
            return finish(h1, target, gy), pick(0), pick(width), pick(2 * width)

        (sum_q, sum_k, sum_v, sum_o), small, input_grad, (output, *grads) = reduce_last(
            place, keep, send, 7, lambda: unproject(dqkv, weights, block_entries, dh1, vec),
            finishing, (gy, came),
        )
    else:
        parts = [back(r, dctx) for r in range(GROUPS)]
        (sum_q, sum_k, sum_v, sum_o), small = reduce_plain(
            [tilt(r, parts[r]) for r in range(GROUPS)], 7
        )
        input_grad = unproject([p[0] for p in parts], weights, block_entries, dh1, vec)
        output = finish(h1, target, gy)

        part = (grads.shape[0] - 16) // 2
        grads = [grads[:part], grads[part : 2 * part].T, grads[2 * part :]]
        grads = [g.astype(F32) for g in grads]

    grad_out, grad_in, rest = grads
    part = grad_out.shape[0]
    own = lax.axis_index("dp") * (width // n_dp)
    grad_bin = rest[0:1, :part]
    grad_bout = lax.dynamic_slice(rest[1:2], (0, own), (1, width // n_dp))
    grad_centers = rest[2:3]
    return (
        output,
        input_grad,
        small[0],
        small[1],
        sum_q,
        small[2],
        sum_k,
        sum_v,
        small[3],
        sum_o,
        small[4],
        small[5],
        small[6],
        grad_centers,
        grad_in[None],
        grad_bin,
        grad_out[None],
        grad_bout,
    )


def solution(mesh):
    placed = (
        P(("dp", "expert"), None),
        P(("dp", "expert")),
        P(("dp", "expert")),
        P(),
        P("expert"),
        P("expert"),
        P("expert", "dp"),
        P("expert"),
        P("expert", "dp"),
        P("expert", "dp"),
        P("expert"),
        P("expert", "dp"),
        P("expert"),
        P("expert"),
        P("expert"),
        P("expert", None),
        P("expert", None, None),
        P("expert", None),
        P("expert", None, None),
        P("expert", None),
        P(("dp", "expert"), None),
    )
    return jax.shard_map(
        partial(shards, Place(mesh)),
        mesh=mesh,
        in_specs=placed,
        out_specs=(
            P(("dp", "expert"), None),
            P(("dp", "expert"), None),
            P("expert"),
            P("expert"),
            P("expert", "dp"),
            P("expert"),
            P("expert", "dp"),
            P("expert", "dp"),
            P("expert"),
            P("expert", "dp"),
            P("expert"),
            P("expert"),
            P("expert"),
            P("expert", None),
            P("expert", None, "dp"),
            P("expert", "dp"),
            P("expert", "dp", None),
            P("expert", "dp"),
        ),
        check_vma=False,
    )
```

```python
from functools import partial

import jax
import jax.numpy as jnp
from jax import lax
from jax.experimental import pallas as pl
from jax.experimental.pallas import tpu as pltpu
from jax.sharding import PartitionSpec as P

HEADS = 12
HEAD_DIM = 64
SEQ_LEN = 1024
GROUPS = 4

EPSILON = 1e-05
MASKED = -1e30
SLAB = 896
BOTH = ("dp", "expert")
BF = jnp.bfloat16
F32 = jnp.float32


def dot(left, right, left_dim, right_dim):
    return lax.dot_general(
        left, right, (((left_dim,), (right_dim,)), ((), ())), preferred_element_type=F32
    )


def normalize(values):
    center = jnp.mean(values, axis=-1, keepdims=True)
    centered = values - center
    inverse = lax.rsqrt(jnp.mean(centered * centered, axis=-1, keepdims=True) + EPSILON)
    return (centered * inverse, inverse)


def normalize_back(grad, normed, inverse, gain):
    scaled = grad * gain
    return inverse * (
        scaled
        - jnp.mean(scaled, axis=-1, keepdims=True)
        - normed * jnp.mean(scaled * normed, axis=-1, keepdims=True)
    )


def call(
    kernel, name, grid, in_specs, outs, scratch=(), vmem=60, cost=(0, 0, 0), ahead=0, **more
):
    return pl.pallas_call(
        kernel,
        name=name,
        grid_spec=pltpu.PrefetchScalarGridSpec(
            num_scalar_prefetch=ahead,
            grid=grid,
            in_specs=in_specs,
            out_specs=[o[0] for o in outs],
            scratch_shapes=list(scratch),
        ),
        out_shape=[jax.ShapeDtypeStruct(o[1], o[2]) for o in outs],
        compiler_params=pltpu.CompilerParams(vmem_limit_bytes=vmem << 20),
        cost_estimate=pl.CostEstimate(
            flops=cost[0], bytes_accessed=cost[1], transcendentals=cost[2]
        ),
        **more,
    )


def full(shape):
    return pl.BlockSpec(
        shape, lambda *_: (0,) * len(shape), pipeline_mode=pl.Buffered(1)
    )


SCALARS = pl.BlockSpec(memory_space=pltpu.SMEM)
PLACED = pl.BlockSpec(memory_space=pl.ANY)


def assemble_kernel(table, own_ref, got_ref, out_ref, sems):
    rows = own_ref.shape[1]
    copies = []
    for i in range(8):
        src = (own_ref, got_ref)[i // 4].at[i % 4]
        at = pl.multiple_of(rows * table[i], 32)
        copies.append(pltpu.make_async_copy(src, out_ref.at[pl.ds(at, rows)], sems.at[i]))
    for c in copies:
        c.start()
    for c in copies:
        c.wait()


def assemble(table, own, got):
    rows, cols = own.shape[1:]
    return call(
        assemble_kernel, "assemble", (1,), [SCALARS, PLACED, PLACED],
        [(full((8 * rows, cols)), (8 * rows, cols), BF)],
        [pltpu.SemaphoreType.DMA((8,))],
        cost=(0, 4 * rows * cols * 8, 0),
    )(table, own, got)[0]


def chunk(shape, axis=0):
    return pl.BlockSpec(shape, lambda i: tuple(i if a == axis else 0 for a in range(len(shape))))


def attend_kernel(half, order, *refs):
    if half:
        low_ref, vec_ref, w_one, w_two = refs[:4]
        qkv_ref, ctx_ref, lse_ref = refs[7:]
    else:
        x_ref, w_one, w_two, qkv_ref, ctx_ref, lse_ref, low_ref, vec_ref = refs
    step = pl.program_id(0)
    count, width = low_ref.shape
    part = width // GROUPS
    if not half:

        @pl.when(step == 0)
        def _():
            vec_ref[...] = w_one[:, 512:640].astype(F32).T[64:72]
            for at in range(0, count, 256):
                unit, _ = normalize(x_ref[at : at + 256].astype(F32))
                low_ref[at : at + 256] = (unit * vec_ref[0:1] + vec_ref[1:2]).astype(BF)

    zero = jnp.zeros((1, part), F32)
    bias_q = bias_v = zero
    for n in range(GROUPS):
        here = order[2 * half + step] == n
        bias_q = jnp.where(here, vec_ref[2:3, part * n : part * n + part], bias_q)
        bias_v = jnp.where(here, vec_ref[3:4, part * n : part * n + part], bias_v)
    bias = jnp.concatenate([bias_q, zero, bias_v], axis=1)
    w = jnp.where(step == 0, w_one[...], w_two[...])[:, : 3 * part]
    for at in range(0, count, 512):
        qkv_ref[0, at : at + 512] = (dot(low_ref[at : at + 512], w, 1, 0) + bias).astype(BF)
    for base in range(0, count, SEQ_LEN):
        block = min(512, SEQ_LEN)
        for h in range(part // HEAD_DIM):
            at = h * HEAD_DIM
            v = qkv_ref[0, base : base + SEQ_LEN, 2 * part + at : 2 * part + at + HEAD_DIM].T
            for start in range(0, SEQ_LEN, block):
                stop = start + block
                q = qkv_ref[0, base + start : base + stop, at : at + HEAD_DIM] * BF(HEAD_DIM**-0.5)
                k = qkv_ref[0, base : base + stop, part + at : part + at + HEAD_DIM]
                row = lax.broadcasted_iota(jnp.int32, (stop, block), 0)
                col = lax.broadcasted_iota(jnp.int32, (stop, block), 1) + start
                scores = jnp.where(row <= col, dot(k, q, 1, 1), MASKED)
                top = jnp.max(scores, axis=0, keepdims=True)
                probs = jnp.exp(scores - top)
                total = jnp.sum(probs, axis=0, keepdims=True)
                out = dot(v[:, :stop], probs.astype(BF), 1, 0) / total
                ctx_ref[0, base + start : base + stop, at : at + HEAD_DIM] = out.T.astype(BF)
                lse_ref[0, h : h + 1, base + start : base + stop] = top + jnp.log(total)


def attend(half, order, weights, x=None, low=None, vec=None, before=()):
    count, width = (low if half else x).shape
    part = width // GROUPS
    at = lambda g: (2 * half + g, 0, 0)
    outs = [
        (pl.BlockSpec((1, count, 3 * part), at), (GROUPS, count, 3 * part), BF),
        (pl.BlockSpec((1, count, part), at), (GROUPS, count, part), BF),
        (pl.BlockSpec((1, 8, count), at), (GROUPS, 8, count), F32),
    ]
    w = [pl.BlockSpec((width, 640), lambda g: (0, 0), pipeline_mode=pl.Buffered(1))] * 2
    if half:
        ins, args = [full((count, width)), full((8, width))] + w + [PLACED] * 3, (low, vec)
    else:
        outs += [(full((count, width)), (count, width), BF), (full((8, width)), (8, width), F32)]
        ins, args = [full((count, width))] + w, (x,)
    return call(
        partial(attend_kernel, half), "attend", (2,), [SCALARS] + ins, outs,
        cost=(12_000_000_000, 8_000_000, 4_000_000),
        input_output_aliases={5 + i: i for i in range(len(before))},
    )(order, *args, *weights, *before)


def attend_back_kernel(half, order, table, *refs):
    qkv_ref, ctx_ref, dctx_ref, lse_ref, low_ref, o_ref, w_one, w_two, two_ref = refs[:9]
    out_ref, *slabs, dq_ref, stage, sems = refs[9:]
    step = pl.program_id(0)
    count, width = low_ref.shape
    part = width // GROUPS
    inner = (ctx_ref[0].astype(F32) * dctx_ref[0].astype(F32)).T
    block = min(256, SEQ_LEN)
    for base in range(0, count, SEQ_LEN):
        last = base + SEQ_LEN
        for h in range(part // HEAD_DIM):
            at = h * HEAD_DIM
            q = qkv_ref[0, base:last, at : at + HEAD_DIM] * BF(HEAD_DIM**-0.5)
            do = dctx_ref[0, base:last, at : at + HEAD_DIM]
            turned = qkv_ref[0, base:last, part + at : part + at + HEAD_DIM].T
            row_dot = jnp.sum(inner[at : at + HEAD_DIM, base:last], axis=0, keepdims=True)
            for start in range(0, SEQ_LEN, block):
                stop = start + block
                rows = slice(base + start, base + stop)
                k = qkv_ref[0, rows, part + at : part + at + HEAD_DIM]
                v = qkv_ref[0, rows, 2 * part + at : 2 * part + at + HEAD_DIM]
                row = lax.broadcasted_iota(jnp.int32, (block, SEQ_LEN - start), 0)
                col = lax.broadcasted_iota(jnp.int32, (block, SEQ_LEN - start), 1)
                lse = lse_ref[0, h : h + 1, base + start : last]
                probs = jnp.where(row <= col, jnp.exp(dot(k, q[start:], 1, 1) - lse), 0.0)
                dscores = (probs * (dot(v, do[start:], 1, 1) - row_dot[:, start:])).astype(BF)
                dk = dot(dscores, q[start:], 1, 0)
                dv = dot(probs.astype(BF), do[start:], 1, 0)
                dq = dot(turned[:, start:stop], dscores, 1, 0)
                if start:
                    dq_ref[:, start:] += dq
                else:
                    dq_ref[...] = dq
                out_ref[0, rows, part + at : part + at + HEAD_DIM] = dk.astype(BF)
                out_ref[0, rows, 2 * part + at : 2 * part + at + HEAD_DIM] = dv.astype(BF)
            out_ref[0, base:last, at : at + HEAD_DIM] = (dq_ref[...].T * HEAD_DIM**-0.5).astype(BF)
    sums = jnp.sum(out_ref[0].astype(F32), axis=0, keepdims=True)
    grad = dot(low_ref[...], out_ref[0], 0, 0)
    w = jnp.where(step == 0, w_one[...], w_two[...]).astype(F32)
    shift = jnp.sum(w[:, : 3 * part] * sums, axis=-1, keepdims=True)
    gain = jnp.sum(w[:, : 3 * part] * grad, axis=-1, keepdims=True)
    gain = (gain - w[:, 577:578] * shift) / w[:, 576:577]
    row = lax.broadcasted_iota(jnp.int32, (width, part), 0) - order[2 * half + step] * part
    here = row == lax.broadcasted_iota(jnp.int32, (width, part), 1)
    columns = [gain, shift] + [
        jnp.sum(jnp.where(here, sums[:, at : at + part], 0.0), axis=-1, keepdims=True)
        for at in (0, 2 * part)
    ]
    lane = lax.broadcasted_iota(jnp.int32, (width, 64), 1)
    vecs = jnp.zeros((width, 64), F32)
    if not half:
        more = jnp.concatenate([two_ref[...], jnp.zeros((120, width), F32)]).T[:, :64]
        vecs = jnp.where(step == 0, more, vecs)
    for i, column in enumerate(columns):
        vecs = jnp.where(lane == i, column, vecs)
    stage[:, : 3 * part] = grad.astype(BF)
    stage[:, 3 * part : 640] = vecs.astype(BF)
    stage[:, 640 : 640 + part] = o_ref[0]
    stage[:, 640 + part :] = jnp.zeros((width, SLAB - 640 - part), BF)
    rows = width // 8
    for g in range(2):

        @pl.when(step == g)
        def _(g=g):
            copies = []
            for i in range(8):
                src = stage.at[pl.ds(pl.multiple_of(rows * table[i], 32), rows)]
                copies.append(
                    pltpu.make_async_copy(src, slabs[2 * g + i // 4].at[i % 4], sems.at[i])
                )
            for c in copies:
                c.start()
            for c in copies:
                c.wait()


def attend_back(half, order, table, qkv, ctx, dctx, lse, low, o_part, weights, two):
    groups, count, part = qkv.shape
    part //= 3
    width = low.shape[1]
    at = lambda g: (2 * half + g, 0, 0)
    slab = (PLACED, (4, width // 8, SLAB), BF)
    return call(
        partial(attend_back_kernel, half), "attend_back", (2,),
        [
            SCALARS,
            SCALARS,
            pl.BlockSpec((1, count, 3 * part), at),
            pl.BlockSpec((1, count, part), at),
            pl.BlockSpec((1, count, part), at),
            pl.BlockSpec((1, 8, count), at),
            full((count, width)),
            pl.BlockSpec((1, width, part), at),
        ]
        + [pl.BlockSpec((width, 640), lambda g: (0, 0), pipeline_mode=pl.Buffered(1))] * 2
        + [full((8, width))],
        [(pl.BlockSpec((1, count, 3 * part), lambda g: (g, 0, 0)), (2, count, 3 * part), BF)]
        + [slab] * 4,
        [
            pltpu.VMEM((HEAD_DIM, SEQ_LEN), F32),
            pltpu.VMEM((width, SLAB), BF),
            pltpu.SemaphoreType.DMA((8,)),
        ],
        cost=(24_000_000_000, 14_000_000, 4_000_000),
    )(order, table, qkv, ctx, dctx, lse, low, o_part, *weights, two)


def dispatch_kernel(target_ref, rows_ref, out_ref):
    count = rows_ref.shape[0]
    for at in range(0, count, 256):
        slot = lax.broadcasted_iota(jnp.int32, (256, count), 0) + at
        picks = (target_ref[...] == slot).astype(F32).astype(BF)
        out_ref[at : at + 256] = dot(picks, rows_ref[...], 1, 0).astype(BF)


def dispatch(target, rows):
    count, width = rows.shape
    return call(
        dispatch_kernel, "dispatch", (1,),
        [full((1, count)), full((count, width))],
        [(full((count, width)), (count, width), BF)],
        cost=(2 * count * count * width, 3_000_000, 0),
    )(target.reshape(1, count), rows)[0]


def mix_kernel(order, x_ref, ctx_ref, vec_ref, target_ref, *refs):
    wo_refs, (h_ref, whole_ref, *sent, low_ref) = refs[:GROUPS], refs[GROUPS:]
    rows, width = x_ref.shape
    count = low_ref.shape[0]
    part = width // GROUPS
    step = pl.program_id(0)

    @pl.when(step == 0)
    def _():
        for q in range(GROUPS):
            at = pl.ds(pl.multiple_of(order[q] * part, 64), part)
            pieces = [wo[at, :] for wo in wo_refs]
            for n in range(GROUPS):
                piece = pieces[0]
                for r in range(1, GROUPS):
                    piece = jnp.where(order[r] == n, pieces[r], piece)
                whole_ref[q * part : q * part + part, n * part : n * part + part] = piece

    h = x_ref[...].astype(F32) + vec_ref[4:5]
    for r in range(GROUPS):
        h += dot(ctx_ref[r], whole_ref[r * part : r * part + part], 1, 0)
    h_ref[...] = h
    unit, _ = normalize(h)
    low_ref[pl.ds(pl.multiple_of(step * rows, 256), rows)] = (
        unit * vec_ref[5:6] + vec_ref[6:7]
    ).astype(BF)

    @pl.when(step == pl.num_programs(0) - 1)
    def _():
        for half in range(2):
            for at in range(0, count // 2, 256):
                index = lax.broadcasted_iota(jnp.int32, (256, count), 0) + (half * count // 2 + at)
                picks = (target_ref[...] == index).astype(F32).astype(BF)
                sent[half][at : at + 256] = dot(picks, low_ref[...], 1, 0).astype(BF)


def mix(order, x, ctx, weights, vec, target):
    count, width = x.shape
    part = width // GROUPS
    rows = min(256, count)
    return call(
        mix_kernel, "mix", (count // rows,),
        [SCALARS, chunk((rows, width)), chunk((GROUPS, rows, part), 1), full((8, width)),
         full((1, count))] + [full((width, part))] * GROUPS,
        [
            (chunk((rows, width)), (count, width), F32),
            (full((width, width)), (width, width), BF),
            (full((count // 2, width)), (count // 2, width), BF),
            (full((count // 2, width)), (count // 2, width), BF),
        ],
        [pltpu.VMEM((count, width), BF)],
        cost=(2 * count * width * (width + count), 12_000_000, 0),
    )(order, x, ctx, vec, target.reshape(1, count), *weights)


def unmix_kernel(
    order, h_ref, g_ref, dm_one, dm_two, target_ref, ctx_ref, whole_ref, vec_ref,
    dh_ref, dctx_ref, grad_ref, sum_ref, total_ref,
):
    rows, width = h_ref.shape
    part = width // GROUPS
    step = pl.program_id(0)
    dm = None
    for half, sent in enumerate((dm_one, dm_two)):
        index = lax.broadcasted_iota(jnp.int32, (rows, sent.shape[0]), 1) + half * sent.shape[0]
        picks = (target_ref[...] == index).astype(F32).astype(BF)
        got = dot(picks, sent[...], 1, 0)
        dm = got if dm is None else dm + got
    unit, inverse = normalize(h_ref[...])
    dh = g_ref[...].astype(F32) + normalize_back(dm, unit, inverse, vec_ref[5:6])
    dh_ref[...] = dh
    low = dh.astype(BF)
    sums = [
        jnp.sum(term, axis=0, keepdims=True) for term in (low.astype(F32), dm * unit, dm)
    ]
    zeros = jnp.zeros((1, width), F32)
    sums = jnp.concatenate([zeros] * 4 + sums + [zeros])
    for r in range(GROUPS):
        dctx_ref[r] = dot(low, whole_ref[r * part : r * part + part], 1, 1).astype(BF)
    grads = [dot(ctx_ref[q], low, 0, 0) for q in range(GROUPS)]

    @pl.when(step == 0)
    def _():
        sum_ref[...] = sums
        for q in range(GROUPS):
            total_ref[q] = grads[q]

    @pl.when(step > 0)
    def _():
        sum_ref[...] += sums
        for q in range(GROUPS):
            total_ref[q] += grads[q]

    @pl.when(step == pl.num_programs(0) - 1)
    def _():
        for q in range(GROUPS):
            grad = total_ref[q].astype(BF)
            at = pl.ds(pl.multiple_of(order[q] * part, 64), part)
            for r in range(GROUPS):
                piece = grad[:, :part]
                for n in range(1, GROUPS):
                    piece = jnp.where(order[r] == n, grad[:, n * part : n * part + part], piece)
                grad_ref[r, at, :] = piece


def unmix(order, h, g, dm_one, dm_two, target, ctx, whole, vec):
    count, width = h.shape
    part = width // GROUPS
    rows = min(256, count)
    half = full((count // 2, width))
    by_rows, by_ctx = chunk((rows, width)), chunk((GROUPS, rows, part), 1)
    return call(
        unmix_kernel, "unmix", (count // rows,),
        [SCALARS, by_rows, by_rows, half, half, chunk((rows, 1)), by_ctx, full((width, width)),
         full((8, width))],
        [
            (by_rows, (count, width), F32),
            (by_ctx, (GROUPS, count, part), BF),
            (full((GROUPS, width, part)), (GROUPS, width, part), BF),
            (full((8, width)), (8, width), F32),
        ],
        [pltpu.VMEM((GROUPS, part, width), F32)],
        cost=(2 * count * width * (2 * width + count), 20_000_000, 0),
    )(order, h, g, dm_one, dm_two, target.reshape(count, 1), ctx, whole, vec)


def finish_kernel(h_ref, target_ref, gy_ref, out_ref):
    slot = lax.broadcasted_iota(jnp.int32, (h_ref.shape[0], gy_ref.shape[0]), 1)
    picks = (target_ref[...] == slot).astype(F32).astype(BF)
    out_ref[...] = (h_ref[...] + dot(picks, gy_ref[...], 1, 0)).astype(BF)


def finish(h, target, gy):
    count, width = h.shape
    rows = min(256, count)
    return call(
        finish_kernel, "finish", (count // rows,),
        [chunk((rows, width)), chunk((rows, 1)), full((count, width))],
        [(chunk((rows, width)), (count, width), BF)],
        cost=(2 * count * count * width, 6_000_000, 0),
    )(h, target.reshape(count, 1), gy)[0]


ERFC = (
    0.169189354,
    0.1706909295,
    0.1485212475,
    0.2141814502,
    -0.09282610738,
    0.5449670381,
    -0.5097724612,
    0.4843017683,
    -0.1292532277,
)


def gelu_pair(v):
    a = jnp.abs(v) * (0.5**0.5)
    bell = jnp.exp(-0.5 * v * v)
    t = 1.0 / (1.0 + 0.3 * a)
    poly = jnp.full_like(v, ERFC[-1])
    for c in ERFC[-2::-1]:
        poly = poly * t + c
    tail = 0.5 * bell * t * poly
    cdf = jnp.where(v < 0, tail, 1.0 - tail)
    return v * cdf, cdf + v * bell * (0.5 / jnp.pi) ** 0.5


def expert_kernel(
    x_ref, g_ref, win_ref, bin_ref, wout_ref, bout_ref, center_ref, _,
    gy_ref, dm_ref, dy_ref, hid_ref, du_ref, dbin_ref, small_ref,
    y_acc, dm_acc, gate_ref, gates,
):
    step = pl.program_id(0)
    rows, width = x_ref.shape

    @pl.when(step == 0)
    def _():
        z = jnp.sum(x_ref[...].astype(F32) * center_ref[...].astype(F32), axis=-1, keepdims=True)
        gate = 1.0 / (1.0 + jnp.exp(-z))
        gate_ref[...] = jnp.broadcast_to(gate, gate_ref.shape)
        dy_ref[...] = (gate * g_ref[...].reshape(rows, width).astype(F32)).astype(BF)

    act, slope = gelu_pair(dot(x_ref[...], win_ref[...], 1, 0) + bin_ref[...].astype(F32))
    hid = act.astype(BF)
    hid_ref[...] = hid
    y = dot(hid, wout_ref[...], 1, 0)
    du = (dot(dy_ref[...], wout_ref[...], 1, 1) * slope).astype(BF)
    du_ref[...] = du
    dbin_ref[...] = jnp.broadcast_to(
        jnp.sum(du.astype(F32), axis=0, keepdims=True), dbin_ref.shape
    )
    dm = dot(du, win_ref[...], 1, 1)

    @pl.when(step == 0)
    def _():
        y_acc[...] = y
        dm_acc[...] = dm

    @pl.when(step > 0)
    def _():
        y_acc[...] += y
        dm_acc[...] += dm

    @pl.when(step == pl.num_programs(0) - 1)
    def _():
        gate = gate_ref[:, :1]
        g = g_ref[...].reshape(rows, width).astype(F32)
        y = (y_acc[...] + bout_ref[...].astype(F32)).astype(BF).astype(F32)
        gy_ref[...] = (gate * y).astype(BF).reshape(gy_ref.shape)
        dz = gate * (1.0 - gate) * jnp.sum(g * y, axis=-1, keepdims=True)
        dm_ref[...] = (dm_acc[...] + dz * center_ref[...].astype(F32)).astype(BF)
        small_ref[0:1, :] = jnp.sum(dy_ref[...].astype(F32), axis=0, keepdims=True)
        small_ref[1:2, :] = jnp.sum(dz * x_ref[...].astype(F32), axis=0, keepdims=True)


def expert(half, x, g, win, bias_in, wout, bias_out, center, gy):
    rows, width = x.shape
    ff = win.shape[1]
    step = min(512, ff)
    along = lambda i: (0, i)
    side = pl.BlockSpec(
        (g.shape[0], 1) + g.shape[2:], lambda i: (0, half, 0, 0), pipeline_mode=pl.Buffered(1)
    )
    return call(
        expert_kernel, "expert", (ff // step,),
        [
            full((rows, width)),
            side,
            pl.BlockSpec((width, step), along),
            pl.BlockSpec((1, step), along),
            pl.BlockSpec((step, width), lambda i: (i, 0)),
            full((1, width)),
            full((1, width)),
            PLACED,
        ],
        [
            (side, g.shape, BF),
            (full((rows, width)), (rows, width), BF),
            (full((rows, width)), (rows, width), BF),
            (pl.BlockSpec((rows, step), along), (rows, ff), BF),
            (pl.BlockSpec((rows, step), along), (rows, ff), BF),
            (pl.BlockSpec((8, step), along), (8, ff), F32),
            (full((8, width)), (8, width), F32),
        ],
        [
            pltpu.VMEM((rows, width), F32),
            pltpu.VMEM((rows, width), F32),
            pltpu.VMEM((rows, 128), F32),
            pltpu.SMEM((1,), jnp.int32),
        ],
        cost=(8 * rows * width * ff, 22_000_000, 2 * rows * ff),
        input_output_aliases={} if gy is None else {7: 0},
    )(x, g, win, bias_in, wout, bias_out, center, x if gy is None else gy)


def weigh_kernel(split, which, *refs):
    hid, du, dy, x, bias, small = (refs[i : i + 2] for i in range(0, 12, 2))
    ff = hid[0].shape[1]
    width = dy[0].shape[1]
    step = pl.program_id(0)
    small = small[0][...] + small[1][...]
    row = lax.broadcasted_iota(jnp.int32, (16, width), 0)
    bias = (bias[0][...] + bias[1][...])[0:1]
    if ff < width:
        bias = jnp.concatenate([bias, jnp.zeros((1, width - ff), F32)], axis=1)
    rest = jnp.where(row == 0, bias, 0.0)
    rest = jnp.where(row == 1, small[0:1], rest)
    rest = jnp.where(row == 2, small[1:2], rest)

    def pair(i):
        rows, cols = (x, du) if split else (du, x)
        return rows[i][...], cols[i][...]

    def put(out):
        out[:ff] = (dot(hid[0][...], dy[0][...], 0, 0) + dot(hid[1][...], dy[1][...], 0, 0)).astype(BF)
        out[ff : 2 * ff] = (
            dot(*pair(0), 0, 0) + dot(*pair(1), 0, 0)
        ).astype(BF)
        out[2 * ff :] = rest.astype(BF)

    if not split:
        put(refs[12].at[0])
        return
    far_ref, across_ref, own_ref, total = refs[12:]
    put(total)
    for at, out in ((0, far_ref.at[0]), (1, far_ref.at[0]), (2, across_ref), (3, own_ref)):

        @pl.when(step == at)
        def _(out=out):
            out[...] = total[...]


def weigh(which, n, split, hid, du, dy, x, bias, small):
    rows, ff = hid[0].shape
    width = dy[0].shape[1]
    part = ff // n
    size = 2 * part + 16
    along = lambda i, which: (0, which[i])
    wide = pl.BlockSpec((rows, part), along)
    if split:
        first = pl.BlockSpec((1, size, width), lambda i, which: (jnp.minimum(i, 1), 0, 0))
        outs = [(first, (2, size, width), BF)] + [(full((size, width)), (size, width), BF)] * 2
        scratch = [pltpu.VMEM((size, width), BF)]
    else:
        outs = [(pl.BlockSpec((1, size, width), lambda i, which: (i, 0, 0)), (n, size, width), BF)]
        scratch = []
    got = call(
        partial(weigh_kernel, split), "weigh", (n,),
        [wide] * 4 + [full((rows, width))] * 4 + [pl.BlockSpec((8, part), along)] * 2
        + [full((8, width))] * 2,
        outs, scratch,
        cost=(8 * rows * width * ff, 26_000_000, 0), ahead=1,
    )(which, *hid, *du, *dy, *x, *bias, *small)
    return got if split else got[0]


def unproject_kernel(*refs):
    one_ref, two_ref, *w_refs = refs[: GROUPS + 2]
    x_ref, dh_ref, vec_ref, out_ref = refs[GROUPS + 2 :]
    part = x_ref.shape[1] // GROUPS
    da = None
    for r, w in enumerate(w_refs):
        got = dot((one_ref, two_ref)[r // 2][r % 2], w[:, : 3 * part], 1, 1)
        da = got if da is None else da + got
    unit, inverse = normalize(x_ref[...].astype(F32))
    out_ref[...] = dh_ref[...] + normalize_back(da, unit, inverse, vec_ref[0:1])


def unproject(grads, weights, x, dh, vec):
    count, width = x.shape
    part = width // GROUPS
    rows = min(256, count)
    w = pl.BlockSpec((width, 640), lambda i: (0, 0), pipeline_mode=pl.Buffered(1))
    return call(
        unproject_kernel, "unproject", (count // rows,),
        [chunk((2, rows, 3 * part), 1)] * 2 + [w] * GROUPS
        + [chunk((rows, width)), chunk((rows, width)), full((8, width))],
        [(chunk((rows, width)), (count, width), F32)],
        cost=(6 * count * width * width, 20_000_000, 0),
    )(*grads, *weights, x, dh, vec)[0]


def add(a, b):
    return (a.astype(F32) + b.astype(F32)).astype(BF)


class Place:
    def __init__(self, mesh):
        self.n_dp = mesh.shape["dp"]
        self.n_e = mesh.shape["expert"]
        self.staged = self.n_dp == 4 and self.n_e == 8
        if not self.staged:
            return
        dev = lambda x, c, z, y: (x * 2 + c) * 8 + z * 2 + y
        every = [
            (x, c, z, y) for x in range(2) for c in range(2) for z in range(4) for y in range(2)
        ]
        to = lambda move: [(dev(*p), dev(*move(*p))) for p in every]
        self.core = to(lambda x, c, z, y: (x, 1 - c, z, y))
        self.x = to(lambda x, c, z, y: (1 - x, c, z, y))
        self.y = to(lambda x, c, z, y: (x, c, z, 1 - y))
        self.z = [to(lambda x, c, z, y, k=k: (x, c, z ^ k, y)) for k in range(1, 4)]

    def tables(self):
        r = jnp.arange(4, dtype=jnp.int32)
        i = jnp.arange(8, dtype=jnp.int32)
        if not self.staged:
            return r, i, r
        d, e = lax.axis_index("dp"), lax.axis_index("expert")
        z, y = e // 2, e % 2
        weighed = d ^ jnp.where(r < 2, 3 - 2 * r, 6 - 2 * r)
        return d ^ r, (z ^ i % 4) * 2 + (y ^ i // 4), weighed

    def move(self, array, way):
        return lax.ppermute(array, BOTH, way)


def whole_of(have):
    n_dp, n_e = lax.axis_size("dp"), lax.axis_size("expert")
    rows, cols = have.shape[1:]
    have = have.reshape(n_dp, n_e, rows, cols).transpose(1, 2, 0, 3)
    return have.reshape(n_e * rows, n_dp * cols)


def gather_all(array):
    return whole_of(lax.all_gather(array, BOTH, axis=0, tiled=False))


def scatter_all(array):
    n_dp, n_e = lax.axis_size("dp"), lax.axis_size("expert")
    rows, cols = array.shape[0] // n_e, array.shape[1] // n_dp
    parts = array.reshape(n_e, rows, n_dp, cols).transpose(2, 0, 1, 3)
    parts = parts.reshape(n_dp * n_e, rows, cols)
    return lax.psum_scatter(parts, BOTH, scatter_dimension=0, tiled=False)


def fetch(place, table, weights, out_weights, vectors, filler):
    barrier = lax.optimization_barrier
    stacked = jnp.stack(vectors)
    pad = 64 - len(vectors)
    if place.staged:
        rows = out_weights.shape[0]
        extra = jnp.concatenate([stacked.T, jnp.zeros((rows, pad), BF)], axis=1)
        shard = jnp.concatenate([*weights, extra], axis=1)
        own = jnp.stack([shard] + [place.move(shard, way) for way in place.z])
        own, out_weights = barrier((own, out_weights))
        got = place.move(own, place.y)
        out_own = jnp.stack([out_weights] + [place.move(out_weights, way) for way in place.z])
        got, filler, out_own = barrier((got, filler, out_own))
        near = assemble(table, own, got)
        across = place.move(near, place.x)
        far = place.move(near, place.core)
        return (near, far, across), (out_own, place.move(out_own, place.y)), filler
    vecs = lax.all_gather(stacked, "expert", axis=1, tiled=True)
    width = vecs.shape[1]
    extra = jnp.concatenate([vecs, jnp.zeros((pad, width), BF)]).T
    extra = jnp.broadcast_to(extra[None], (GROUPS, width, 64))
    by_group = lambda w: gather_all(w).reshape(width, GROUPS, -1).transpose(1, 0, 2)
    grouped = jnp.concatenate([*(by_group(w) for w in weights), extra], axis=2)
    out = by_group(out_weights)
    return [grouped[i] for i in range(GROUPS)], [out[i] for i in range(GROUPS)], filler


def reduce_y(place, keep, send):
    got = place.move(send, place.y)
    return keep[0].astype(F32) + got[0].astype(F32), [add(keep[k], got[k]) for k in range(1, 4)]


def reduce_z(place, sends):
    return [place.move(part, way) for part, way in zip(sends, place.z)]


def columns_of(place, total, count):
    cols = (SLAB - 128) // 4
    parts = [total[:, i : i + cols] for i in (0, cols, 2 * cols, 640)]
    vecs = total[:, 576 : 576 + 8].T
    vecs = vecs + place.move(vecs, place.core)
    vecs = vecs + place.move(vecs, place.x)
    return parts, [vecs[i] for i in range(count)]


def reduce_plain(slabs, count):
    slabs = jnp.stack(slabs)
    width = slabs.shape[1]
    part = width // GROUPS
    parts = []
    for at in (0, part, 2 * part, 640):
        grad = slabs[:, :, at : at + part].transpose(1, 0, 2).reshape(width, width)
        parts.append(scatter_all(grad).astype(F32))
    vecs = jnp.sum(slabs[:, :, 576 : 576 + count].astype(F32), axis=0).T
    vecs = lax.psum_scatter(vecs, "expert", scatter_dimension=1, tiled=True)
    vecs = lax.psum(vecs, "dp")
    return parts, [vecs[i] for i in range(count)]


def shards(
    place,
    block_entries,
    assignments,
    positions_within,
    specialist_quotas,
    standardize_one_scale,
    standardize_one_shift,
    asking_weights,
    asking_shift,
    lookup_weights,
    content_weights,
    content_shift,
    context_mixing_weights,
    context_mixing_shift,
    standardize_two_scale,
    standardize_two_shift,
    gating_prototypes,
    specialist_widen_weights,
    specialist_widen_shift,
    specialist_contract_weights,
    specialist_contract_shift,
    upstream_adjoint,
):
    count, width = block_entries.shape
    experts = specialist_quotas.shape[0]
    cap = count // experts
    n_dp = place.n_dp
    order, table, weighed = place.tables()
    barrier = lax.optimization_barrier

    chosen = assignments[:, None] == lax.broadcasted_iota(jnp.int32, (count, experts), 1)
    limit = jnp.sum(jnp.where(chosen, specialist_quotas[None, :], 0), axis=1)
    kept = positions_within < limit
    target = jnp.where(kept, assignments * cap + positions_within, count)
    late = positions_within >= cap // 2
    halved = jnp.where(late, positions_within + (count - cap) // 2, positions_within)
    halved = jnp.where(kept, assignments * (cap // 2) + halved, count)

    def exchange(rows):
        sent = rows.reshape(experts, -1, width)
        got = lax.all_to_all(sent, "expert", split_axis=0, concat_axis=0, tiled=True)
        return got.reshape(rows.shape)

    weights, out, sent_g = fetch(
        place,
        table,
        (asking_weights, lookup_weights, content_weights),
        context_mixing_weights,
        (
            standardize_one_scale,
            standardize_one_shift,
            asking_shift,
            content_shift,
            context_mixing_shift,
            standardize_two_scale,
            standardize_two_shift,
        ),
        dispatch(target, upstream_adjoint),
    )

    sent_g, first = barrier((sent_g, weights[1]))
    weights = (weights[0], first, *weights[2:])
    rows_g = exchange(sent_g).reshape(experts, 2, cap // 2, width)

    *before, low_in, vec = attend(0, order, weights[:2], x=block_entries)
    if place.staged:
        before, out = barrier((before, out))
        out_near = assemble(table, *out)
        before, across, out_near = barrier((before, weights[2], out_near))
        weights = (*weights[:2], across, place.move(across, place.core))
        out_across = place.move(out_near, place.x)
        out = (out_near, place.move(out_near, place.core))
    qkv, ctx, lse = attend(1, order, weights[2:], low=low_in, vec=vec, before=before)
    ctx, rows_g = barrier((ctx, rows_g))
    if place.staged:
        ctx, out_across = barrier((ctx, out_across))
        out += (out_across, place.move(out_across, place.core))
    h1, whole_o, sent_one, sent_two = mix(order, block_entries, ctx, out, vec, halved)

    x_one = exchange(sent_one)
    x_one, sent_two = barrier((x_one, sent_two))
    x_two = exchange(sent_two)
    matrices = (
        specialist_widen_weights[0], specialist_widen_shift, specialist_contract_weights[0],
        specialist_contract_shift, gating_prototypes,
    )
    gy, dm_one, dy_one, hid_one, du_one, dbin_one, small_one = expert(
        0, x_one, rows_g, *matrices, None
    )
    x_two, dm_one = barrier((x_two, dm_one))
    dm_one = exchange(dm_one)
    gy, dm_two, dy_two, hid_two, du_two, dbin_two, small_two = expert(
        1, x_two, rows_g, *matrices, gy
    )
    dm_one, dm_two, hid_two = barrier((dm_one, dm_two, hid_two))
    dm_two = exchange(dm_two)
    sides = (
        (hid_one, hid_two), (du_one, du_two), (dy_one, dy_two), (x_one, x_two),
        (dbin_one, dbin_two), (small_one, small_two),
    )
    if place.staged:
        grads_far, grads_across, grads = weigh(
            weighed, n_dp, True, *sides
        )
        grads_far, gy, dm_two = barrier((grads_far, gy, dm_two))
        came_far = place.move(grads_far, place.core)
        crossing = add(grads_across, came_far[0])
        crossing, h1 = barrier((crossing, h1))
        came = place.move(crossing, place.x)
    else:
        grads = weigh(jnp.arange(n_dp, dtype=jnp.int32), n_dp, False, *sides)
        grads = lax.psum_scatter(grads, "dp", scatter_dimension=0, tiled=False)
    gy = exchange(gy.reshape(count, width))

    dh1, dctx, grad_o, two = unmix(
        order, h1, upstream_adjoint, dm_one, dm_two, halved, ctx, whole_o, vec
    )
    back = lambda half, dctx: attend_back(
        half, order, table, qkv, ctx, dctx, lse, low_in, grad_o, weights[2 * half : 2 * half + 2],
        two,
    )
    if place.staged:
        far, keep, send, *more = back(1, dctx)
        more = [place.move(m, place.core) for m in more]
        far, gy = barrier((far, gy))
        output = finish(h1, target, gy)
        send = add(send, more[1])
        dctx, output, send = barrier((dctx, output, send))
        across, sends = reduce_y(place, add(keep, more[0]), send)
        near, keep, send, *more = back(0, dctx)
        near, sends = barrier((near, sends))
        more = [place.move(m, place.core) for m in more]
        got = reduce_z(place, sends)
        send, keep = add(send, more[1]), add(keep, more[0])
        near, send = barrier((near, send))
        got_y = place.move(send, place.y)
        input_grad = unproject((near, far), weights, block_entries, dh1, vec)
        got, input_grad = barrier((got, input_grad))
        across = (across + sum(g.astype(F32) for g in got)).astype(BF)
        across = place.move(across, place.x)
        got, input_grad, came = barrier((got_y, input_grad, came))
        total = keep[0].astype(F32) + got[0].astype(F32)
        got = reduce_z(place, [add(keep[k], got[k]) for k in range(1, 4)])
        pick = lambda at: sum(
            a[at : at + width].astype(F32) for a in (grads, came_far[1], came)
        )
        got, grads, across = barrier((got, [pick(0), pick(width), pick(2 * width)], across))
        total += across.astype(F32)
        total += sum(g.astype(F32) for g in got)
        (sum_q, sum_k, sum_v, sum_o), small = columns_of(place, total, 7)
    else:
        parts = [back(half, dctx) for half in range(2)]
        (sum_q, sum_k, sum_v, sum_o), small = reduce_plain(
            [
                jnp.concatenate(p[1 + 2 * g : 3 + 2 * g]).reshape(width, SLAB)
                for p in parts
                for g in range(2)
            ],
            7,
        )
        input_grad = unproject([p[0] for p in parts], weights, block_entries, dh1, vec)
        output = finish(h1, target, gy)

        part = (grads.shape[0] - 16) // 2
        grads = [grads[:part], grads[part : 2 * part].T, grads[2 * part :]]
        grads = [g.astype(F32) for g in grads]

    grad_out, grad_in, rest = grads
    part = grad_out.shape[0]
    own = lax.axis_index("dp") * (width // n_dp)
    grad_bin = rest[0:1, :part]
    grad_bout = lax.dynamic_slice(rest[1:2], (0, own), (1, width // n_dp))
    grad_centers = rest[2:3]
    return (
        output,
        input_grad,
        small[0],
        small[1],
        sum_q,
        small[2],
        sum_k,
        sum_v,
        small[3],
        sum_o,
        small[4],
        small[5],
        small[6],
        grad_centers,
        grad_in[None],
        grad_bin,
        grad_out[None],
        grad_bout,
    )


def solution(mesh):
    placed = (
        P(("dp", "expert"), None),
        P(("dp", "expert")),
        P(("dp", "expert")),
        P(),
        P("expert"),
        P("expert"),
        P("expert", "dp"),
        P("expert"),
        P("expert", "dp"),
        P("expert", "dp"),
        P("expert"),
        P("expert", "dp"),
        P("expert"),
        P("expert"),
        P("expert"),
        P("expert", None),
        P("expert", None, None),
        P("expert", None),
        P("expert", None, None),
        P("expert", None),
        P(("dp", "expert"), None),
    )
    return jax.shard_map(
        partial(shards, Place(mesh)),
        mesh=mesh,
        in_specs=placed,
        out_specs=(
            P(("dp", "expert"), None),
            P(("dp", "expert"), None),
            P("expert"),
            P("expert"),
            P("expert", "dp"),
            P("expert"),
            P("expert", "dp"),
            P("expert", "dp"),
            P("expert"),
            P("expert", "dp"),
            P("expert"),
            P("expert"),
            P("expert"),
            P("expert", None),
            P("expert", None, "dp"),
            P("expert", "dp"),
            P("expert", "dp", None),
            P("expert", "dp"),
        ),
        check_vma=False,
    )
```

```python
from functools import partial

import jax
import jax.numpy as jnp
from jax import lax
from jax.experimental import pallas as pl
from jax.experimental.pallas import tpu as pltpu
from jax.sharding import PartitionSpec as P

HEADS = 12
HEAD_DIM = 64
SEQ_LEN = 1024
GROUPS = 4

EPSILON = 1e-05
MASKED = -1e30
FAR = 1024
BOTH = ("dp", "expert")
BF = jnp.bfloat16
F32 = jnp.float32


def dot(left, right, left_dim, right_dim):
    return lax.dot_general(
        left, right, (((left_dim,), (right_dim,)), ((), ())), preferred_element_type=F32
    )


def normalize(values):
    center = jnp.mean(values, axis=-1, keepdims=True)
    centered = values - center
    inverse = lax.rsqrt(jnp.mean(centered * centered, axis=-1, keepdims=True) + EPSILON)
    return (centered * inverse, inverse)


def normalize_back(grad, normed, inverse, gain):
    scaled = grad * gain
    return inverse * (
        scaled
        - jnp.mean(scaled, axis=-1, keepdims=True)
        - normed * jnp.mean(scaled * normed, axis=-1, keepdims=True)
    )


def call(
    kernel, name, grid, in_specs, outs, scratch=(), vmem=60, cost=(0, 0, 0), ahead=0, **more
):
    return pl.pallas_call(
        kernel,
        name=name,
        grid_spec=pltpu.PrefetchScalarGridSpec(
            num_scalar_prefetch=ahead,
            grid=grid,
            in_specs=in_specs,
            out_specs=[o[0] for o in outs],
            scratch_shapes=list(scratch),
        ),
        out_shape=[jax.ShapeDtypeStruct(o[1], o[2]) for o in outs],
        compiler_params=pltpu.CompilerParams(vmem_limit_bytes=vmem << 20),
        cost_estimate=pl.CostEstimate(
            flops=cost[0], bytes_accessed=cost[1], transcendentals=cost[2]
        ),
        **more,
    )


def full(shape):
    return pl.BlockSpec(
        shape, lambda *_: (0,) * len(shape), pipeline_mode=pl.Buffered(1)
    )


SCALARS = pl.BlockSpec(memory_space=pltpu.SMEM)
PLACED = pl.BlockSpec(memory_space=pl.ANY)


def assemble_kernel(table, own_ref, got_ref, out_ref, sems):
    rows = own_ref.shape[1]
    copies = []
    for i in range(8):
        src = (own_ref, got_ref)[i // 4].at[i % 4]
        at = pl.multiple_of(rows * table[i], 32)
        copies.append(pltpu.make_async_copy(src, out_ref.at[pl.ds(at, rows)], sems.at[i]))
    for c in copies:
        c.start()
    for c in copies:
        c.wait()


def assemble(table, own, got):
    rows, cols = own.shape[1:]
    return call(
        assemble_kernel, "assemble", (1,), [SCALARS, PLACED, PLACED],
        [(full((8 * rows, cols)), (8 * rows, cols), BF)],
        [pltpu.SemaphoreType.DMA((8,))],
        cost=(0, 4 * rows * cols * 8, 0),
    )(table, own, got)[0]


def chunk(shape, axis=0):
    return pl.BlockSpec(shape, lambda i: tuple(i if a == axis else 0 for a in range(len(shape))))


def attend_kernel(half, order, *refs):
    if half:
        low_ref, vec_ref, w_one, w_two = refs[:4]
        qkv_ref, ctx_ref, lse_ref = refs[7:]
    else:
        x_ref, w_one, w_two, qkv_ref, ctx_ref, lse_ref, low_ref, vec_ref = refs
    step = pl.program_id(0)
    count, width = low_ref.shape
    part = width // GROUPS
    if not half:

        @pl.when(step == 0)
        def _():
            vec_ref[...] = w_one[:, 512:640].astype(F32).T[64:72]
            for at in range(0, count, 256):
                unit, _ = normalize(x_ref[at : at + 256].astype(F32))
                low_ref[at : at + 256] = (unit * vec_ref[0:1] + vec_ref[1:2]).astype(BF)

    zero = jnp.zeros((1, part), F32)
    bias_q = bias_v = zero
    for n in range(GROUPS):
        here = order[2 * half + step] == n
        bias_q = jnp.where(here, vec_ref[2:3, part * n : part * n + part], bias_q)
        bias_v = jnp.where(here, vec_ref[3:4, part * n : part * n + part], bias_v)
    bias = jnp.concatenate([bias_q, zero, bias_v], axis=1)
    w = jnp.where(step == 0, w_one[...], w_two[...])[:, : 3 * part]
    for at in range(0, count, 512):
        qkv_ref[0, at : at + 512] = (dot(low_ref[at : at + 512], w, 1, 0) + bias).astype(BF)
    for base in range(0, count, SEQ_LEN):
        block = min(512, SEQ_LEN)
        for h in range(part // HEAD_DIM):
            at = h * HEAD_DIM
            v = qkv_ref[0, base : base + SEQ_LEN, 2 * part + at : 2 * part + at + HEAD_DIM].T
            for start in range(0, SEQ_LEN, block):
                stop = start + block
                q = qkv_ref[0, base + start : base + stop, at : at + HEAD_DIM] * BF(HEAD_DIM**-0.5)
                k = qkv_ref[0, base : base + stop, part + at : part + at + HEAD_DIM]
                row = lax.broadcasted_iota(jnp.int32, (stop, block), 0)
                col = lax.broadcasted_iota(jnp.int32, (stop, block), 1) + start
                scores = jnp.where(row <= col, dot(k, q, 1, 1), MASKED)
                top = jnp.max(scores, axis=0, keepdims=True)
                probs = jnp.exp(scores - top)
                total = jnp.sum(probs, axis=0, keepdims=True)
                out = dot(v[:, :stop], probs.astype(BF), 1, 0) / total
                ctx_ref[0, base + start : base + stop, at : at + HEAD_DIM] = out.T.astype(BF)
                lse_ref[0, h : h + 1, base + start : base + stop] = top + jnp.log(total)


def attend(half, order, weights, x=None, low=None, vec=None, before=()):
    count, width = (low if half else x).shape
    part = width // GROUPS
    at = lambda g: (2 * half + g, 0, 0)
    outs = [
        (pl.BlockSpec((1, count, 3 * part), at), (GROUPS, count, 3 * part), BF),
        (pl.BlockSpec((1, count, part), at), (GROUPS, count, part), BF),
        (pl.BlockSpec((1, 8, count), at), (GROUPS, 8, count), F32),
    ]
    w = [pl.BlockSpec((width, 640), lambda g: (0, 0), pipeline_mode=pl.Buffered(1))] * 2
    if half:
        ins, args = [full((count, width)), full((8, width))] + w + [PLACED] * 3, (low, vec)
    else:
        outs += [(full((count, width)), (count, width), BF), (full((8, width)), (8, width), F32)]
        ins, args = [full((count, width))] + w, (x,)
    return call(
        partial(attend_kernel, half), "attend", (2,), [SCALARS] + ins, outs,
        cost=(12_000_000_000, 8_000_000, 4_000_000),
        input_output_aliases={5 + i: i for i in range(len(before))},
    )(order, *args, *weights, *before)


def attend_back_kernel(half, order, table, *refs):
    qkv_ref, ctx_ref, dctx_ref, lse_ref, low_ref, w_one, w_two, two_ref = refs[:8]
    if half:
        o_refs, refs = refs[8:10], refs[2:]
    out_ref, *slabs, dq_ref, stage, sems = refs[8:]
    step = pl.program_id(0)
    count, width = low_ref.shape
    part = width // GROUPS
    inner = (ctx_ref[0].astype(F32) * dctx_ref[0].astype(F32)).T
    block = min(256, SEQ_LEN)
    for base in range(0, count, SEQ_LEN):
        last = base + SEQ_LEN
        for h in range(part // HEAD_DIM):
            at = h * HEAD_DIM
            q = qkv_ref[0, base:last, at : at + HEAD_DIM] * BF(HEAD_DIM**-0.5)
            do = dctx_ref[0, base:last, at : at + HEAD_DIM]
            turned = qkv_ref[0, base:last, part + at : part + at + HEAD_DIM].T
            row_dot = jnp.sum(inner[at : at + HEAD_DIM, base:last], axis=0, keepdims=True)
            for start in range(0, SEQ_LEN, block):
                stop = start + block
                rows = slice(base + start, base + stop)
                k = qkv_ref[0, rows, part + at : part + at + HEAD_DIM]
                v = qkv_ref[0, rows, 2 * part + at : 2 * part + at + HEAD_DIM]
                row = lax.broadcasted_iota(jnp.int32, (block, SEQ_LEN - start), 0)
                col = lax.broadcasted_iota(jnp.int32, (block, SEQ_LEN - start), 1)
                lse = lse_ref[0, h : h + 1, base + start : last]
                probs = jnp.where(row <= col, jnp.exp(dot(k, q[start:], 1, 1) - lse), 0.0)
                dscores = (probs * (dot(v, do[start:], 1, 1) - row_dot[:, start:])).astype(BF)
                dk = dot(dscores, q[start:], 1, 0)
                dv = dot(probs.astype(BF), do[start:], 1, 0)
                dq = dot(turned[:, start:stop], dscores, 1, 0)
                if start:
                    dq_ref[:, start:] += dq
                else:
                    dq_ref[...] = dq
                out_ref[0, rows, part + at : part + at + HEAD_DIM] = dk.astype(BF)
                out_ref[0, rows, 2 * part + at : 2 * part + at + HEAD_DIM] = dv.astype(BF)
            out_ref[0, base:last, at : at + HEAD_DIM] = (dq_ref[...].T * HEAD_DIM**-0.5).astype(BF)
    sums = jnp.sum(out_ref[0].astype(F32), axis=0, keepdims=True)
    grad = dot(low_ref[...], out_ref[0], 0, 0)
    w = jnp.where(step == 0, w_one[...], w_two[...]).astype(F32)
    shift = jnp.sum(w[:, : 3 * part] * sums, axis=-1, keepdims=True)
    gain = jnp.sum(w[:, : 3 * part] * grad, axis=-1, keepdims=True)
    gain = (gain - w[:, 577:578] * shift) / w[:, 576:577]
    row = lax.broadcasted_iota(jnp.int32, (width, part), 0) - order[2 * half + step] * part
    here = row == lax.broadcasted_iota(jnp.int32, (width, part), 1)
    columns = [gain, shift] + [
        jnp.sum(jnp.where(here, sums[:, at : at + part], 0.0), axis=-1, keepdims=True)
        for at in (0, 2 * part)
    ]
    lane = lax.broadcasted_iota(jnp.int32, (width, 64), 1)
    vecs = jnp.zeros((width, 64), F32)
    if not half:
        more = jnp.concatenate([two_ref[...], jnp.zeros((120, width), F32)]).T[:, :64]
        vecs = jnp.where(step == 0, more, vecs)
    for i, column in enumerate(columns):
        vecs = jnp.where(lane == i, column, vecs)
    stage[:, : 3 * part] = grad.astype(BF)
    stage[:, 3 * part : 640] = vecs.astype(BF)
    if half:
        stage[:, 640:] = jnp.concatenate([o_refs[0][0], o_refs[1][0]], axis=1)
    rows = width // 8
    for g in range(2):

        @pl.when(step == g)
        def _(g=g):
            copies = []
            for i in range(8):
                src = stage.at[pl.ds(pl.multiple_of(rows * table[i], 32), rows)]
                copies.append(
                    pltpu.make_async_copy(src, slabs[2 * g + i // 4].at[i % 4], sems.at[i])
                )
            for c in copies:
                c.start()
            for c in copies:
                c.wait()


def attend_back(half, order, table, qkv, ctx, dctx, lse, low, o_part, weights, two):
    groups, count, part = qkv.shape
    part //= 3
    width = low.shape[1]
    at = lambda g, *_: (2 * half + g, 0, 0)
    cols = FAR if half else 640
    slab = (PLACED, (4, width // 8, cols), BF)
    o_specs = [
        pl.BlockSpec((1, width, part), lambda g, order, table, b=b: (order[b + g], 0, 0))
        for b in ((2, 0) if half else ())
    ]
    return call(
        partial(attend_back_kernel, half), "attend_back", (2,),
        [
            pl.BlockSpec((1, count, 3 * part), at),
            pl.BlockSpec((1, count, part), at),
            pl.BlockSpec((1, count, part), at),
            pl.BlockSpec((1, 8, count), at),
            full((count, width)),
        ]
        + [pl.BlockSpec((width, 640), lambda *_: (0, 0), pipeline_mode=pl.Buffered(1))] * 2
        + [full((8, width))] + o_specs,
        [(pl.BlockSpec((1, count, 3 * part), lambda g, *_: (g, 0, 0)), (2, count, 3 * part), BF)]
        + [slab] * 4,
        [
            pltpu.VMEM((HEAD_DIM, SEQ_LEN), F32),
            pltpu.VMEM((width, cols), BF),
            pltpu.SemaphoreType.DMA((8,)),
        ],
        cost=(24_000_000_000, 14_000_000, 4_000_000), ahead=2,
    )(order, table, qkv, ctx, dctx, lse, low, *weights, two, *[o_part] * len(o_specs))


def dispatch_kernel(target_ref, rows_ref, out_ref):
    count = rows_ref.shape[0]
    for at in range(0, count, 256):
        slot = lax.broadcasted_iota(jnp.int32, (256, count), 0) + at
        picks = (target_ref[...] == slot).astype(F32).astype(BF)
        out_ref[at : at + 256] = dot(picks, rows_ref[...], 1, 0).astype(BF)


def dispatch(target, rows):
    count, width = rows.shape
    return call(
        dispatch_kernel, "dispatch", (1,),
        [full((1, count)), full((count, width))],
        [(full((count, width)), (count, width), BF)],
        cost=(2 * count * count * width, 3_000_000, 0),
    )(target.reshape(1, count), rows)[0]


def mix_kernel(order, x_ref, ctx_ref, vec_ref, target_ref, *refs):
    wo_refs, (h_ref, whole_ref, *sent, low_ref) = refs[:GROUPS], refs[GROUPS:]
    rows, width = x_ref.shape
    count = low_ref.shape[0]
    part = width // GROUPS
    step = pl.program_id(0)

    @pl.when(step == 0)
    def _():
        for q in range(GROUPS):
            at = pl.ds(pl.multiple_of(order[q] * part, 64), part)
            pieces = [wo[at, :] for wo in wo_refs]
            for n in range(GROUPS):
                piece = pieces[0]
                for r in range(1, GROUPS):
                    piece = jnp.where(order[r] == n, pieces[r], piece)
                whole_ref[q * part : q * part + part, n * part : n * part + part] = piece

    h = x_ref[...].astype(F32) + vec_ref[4:5]
    for r in range(GROUPS):
        h += dot(ctx_ref[r], whole_ref[r * part : r * part + part], 1, 0)
    h_ref[...] = h
    unit, _ = normalize(h)
    low_ref[pl.ds(pl.multiple_of(step * rows, 256), rows)] = (
        unit * vec_ref[5:6] + vec_ref[6:7]
    ).astype(BF)

    @pl.when(step == pl.num_programs(0) - 1)
    def _():
        for half in range(2):
            for at in range(0, count // 2, 256):
                index = lax.broadcasted_iota(jnp.int32, (256, count), 0) + (half * count // 2 + at)
                picks = (target_ref[...] == index).astype(F32).astype(BF)
                sent[half][at : at + 256] = dot(picks, low_ref[...], 1, 0).astype(BF)


def mix(order, x, ctx, weights, vec, target):
    count, width = x.shape
    part = width // GROUPS
    rows = min(256, count)
    return call(
        mix_kernel, "mix", (count // rows,),
        [SCALARS, chunk((rows, width)), chunk((GROUPS, rows, part), 1), full((8, width)),
         full((1, count))] + [full((width, part))] * GROUPS,
        [
            (chunk((rows, width)), (count, width), F32),
            (full((width, width)), (width, width), BF),
            (full((count // 2, width)), (count // 2, width), BF),
            (full((count // 2, width)), (count // 2, width), BF),
        ],
        [pltpu.VMEM((count, width), BF)],
        cost=(2 * count * width * (width + count), 12_000_000, 0),
    )(order, x, ctx, vec, target.reshape(1, count), *weights)


def unmix_kernel(
    order, h_ref, g_ref, dm_one, dm_two, target_ref, ctx_ref, whole_ref, vec_ref,
    dh_ref, dctx_ref, grad_ref, sum_ref, total_ref,
):
    rows, width = h_ref.shape
    part = width // GROUPS
    step = pl.program_id(0)
    dm = None
    for half, sent in enumerate((dm_one, dm_two)):
        index = lax.broadcasted_iota(jnp.int32, (rows, sent.shape[0]), 1) + half * sent.shape[0]
        picks = (target_ref[...] == index).astype(F32).astype(BF)
        got = dot(picks, sent[...], 1, 0)
        dm = got if dm is None else dm + got
    unit, inverse = normalize(h_ref[...])
    dh = g_ref[...].astype(F32) + normalize_back(dm, unit, inverse, vec_ref[5:6])
    dh_ref[...] = dh
    low = dh.astype(BF)
    sums = [
        jnp.sum(term, axis=0, keepdims=True) for term in (low.astype(F32), dm * unit, dm)
    ]
    zeros = jnp.zeros((1, width), F32)
    sums = jnp.concatenate([zeros] * 4 + sums + [zeros])
    for r in range(GROUPS):
        dctx_ref[r] = dot(low, whole_ref[r * part : r * part + part], 1, 1).astype(BF)
    grads = [dot(ctx_ref[q], low, 0, 0) for q in range(GROUPS)]

    @pl.when(step == 0)
    def _():
        sum_ref[...] = sums
        for q in range(GROUPS):
            total_ref[q] = grads[q]

    @pl.when(step > 0)
    def _():
        sum_ref[...] += sums
        for q in range(GROUPS):
            total_ref[q] += grads[q]

    @pl.when(step == pl.num_programs(0) - 1)
    def _():
        for q in range(GROUPS):
            grad = total_ref[q].astype(BF)
            at = pl.ds(pl.multiple_of(order[q] * part, 64), part)
            for n in range(GROUPS):
                grad_ref[n, at, :] = grad[:, n * part : n * part + part]


def unmix(order, h, g, dm_one, dm_two, target, ctx, whole, vec):
    count, width = h.shape
    part = width // GROUPS
    rows = min(256, count)
    half = full((count // 2, width))
    by_rows, by_ctx = chunk((rows, width)), chunk((GROUPS, rows, part), 1)
    return call(
        unmix_kernel, "unmix", (count // rows,),
        [SCALARS, by_rows, by_rows, half, half, chunk((rows, 1)), by_ctx, full((width, width)),
         full((8, width))],
        [
            (by_rows, (count, width), F32),
            (by_ctx, (GROUPS, count, part), BF),
            (full((GROUPS, width, part)), (GROUPS, width, part), BF),
            (full((8, width)), (8, width), F32),
        ],
        [pltpu.VMEM((GROUPS, part, width), F32)],
        cost=(2 * count * width * (2 * width + count), 20_000_000, 0),
    )(order, h, g, dm_one, dm_two, target.reshape(count, 1), ctx, whole, vec)


def finish_kernel(h_ref, target_ref, gy_ref, out_ref):
    slot = lax.broadcasted_iota(jnp.int32, (h_ref.shape[0], gy_ref.shape[0]), 1)
    picks = (target_ref[...] == slot).astype(F32).astype(BF)
    out_ref[...] = (h_ref[...] + dot(picks, gy_ref[...], 1, 0)).astype(BF)


def finish(h, target, gy):
    count, width = h.shape
    rows = min(256, count)
    return call(
        finish_kernel, "finish", (count // rows,),
        [chunk((rows, width)), chunk((rows, 1)), full((count, width))],
        [(chunk((rows, width)), (count, width), BF)],
        cost=(2 * count * count * width, 6_000_000, 0),
    )(h, target.reshape(count, 1), gy)[0]


def gelu_pair(v):
    cdf = 0.5 + 0.5 * lax.erf(v * 0.5**0.5)
    return v * cdf, cdf + v * jnp.exp(-0.5 * v * v) * (0.5 / jnp.pi) ** 0.5


def expert_kernel(
    x_ref, g_ref, win_ref, bin_ref, wout_ref, bout_ref, center_ref, _,
    gy_ref, dm_ref, dy_ref, hid_ref, du_ref, dbin_ref, small_ref,
    y_acc, dm_acc, gate_ref, gates,
):
    step = pl.program_id(0)
    rows, width = x_ref.shape

    @pl.when(step == 0)
    def _():
        z = jnp.sum(x_ref[...].astype(F32) * center_ref[...].astype(F32), axis=-1, keepdims=True)
        gate = 1.0 / (1.0 + jnp.exp(-z))
        gate_ref[...] = jnp.broadcast_to(gate, gate_ref.shape)
        dy_ref[...] = (gate * g_ref[...].reshape(rows, width).astype(F32)).astype(BF)

    act, slope = gelu_pair(dot(x_ref[...], win_ref[...], 1, 0) + bin_ref[...].astype(F32))
    hid = act.astype(BF)
    hid_ref[...] = hid
    y = dot(hid, wout_ref[...], 1, 0)
    du = (dot(dy_ref[...], wout_ref[...], 1, 1) * slope).astype(BF)
    du_ref[...] = du
    dbin_ref[...] = jnp.broadcast_to(
        jnp.sum(du.astype(F32), axis=0, keepdims=True), dbin_ref.shape
    )
    dm = dot(du, win_ref[...], 1, 1)

    @pl.when(step == 0)
    def _():
        y_acc[...] = y
        dm_acc[...] = dm

    @pl.when(step > 0)
    def _():
        y_acc[...] += y
        dm_acc[...] += dm

    @pl.when(step == pl.num_programs(0) - 1)
    def _():
        gate = gate_ref[:, :1]
        g = g_ref[...].reshape(rows, width).astype(F32)
        y = (y_acc[...] + bout_ref[...].astype(F32)).astype(BF).astype(F32)
        gy_ref[...] = (gate * y).astype(BF).reshape(gy_ref.shape)
        dz = gate * (1.0 - gate) * jnp.sum(g * y, axis=-1, keepdims=True)
        dm_ref[...] = (dm_acc[...] + dz * center_ref[...].astype(F32)).astype(BF)
        small_ref[0:1, :] = jnp.sum(dy_ref[...].astype(F32), axis=0, keepdims=True)
        small_ref[1:2, :] = jnp.sum(dz * x_ref[...].astype(F32), axis=0, keepdims=True)


def expert(half, x, g, win, bias_in, wout, bias_out, center, gy):
    rows, width = x.shape
    ff = win.shape[1]
    step = min(1024, ff)
    along = lambda i: (0, i)
    side = pl.BlockSpec(
        (g.shape[0], 1) + g.shape[2:], lambda i: (0, half, 0, 0), pipeline_mode=pl.Buffered(1)
    )
    return call(
        expert_kernel, "expert", (ff // step,),
        [
            full((rows, width)),
            side,
            pl.BlockSpec((width, step), along),
            pl.BlockSpec((1, step), along),
            pl.BlockSpec((step, width), lambda i: (i, 0)),
            full((1, width)),
            full((1, width)),
            PLACED,
        ],
        [
            (side, g.shape, BF),
            (full((rows, width)), (rows, width), BF),
            (full((rows, width)), (rows, width), BF),
            (pl.BlockSpec((rows, step), along), (rows, ff), BF),
            (pl.BlockSpec((rows, step), along), (rows, ff), BF),
            (pl.BlockSpec((8, step), along), (8, ff), F32),
            (full((8, width)), (8, width), F32),
        ],
        [
            pltpu.VMEM((rows, width), F32),
            pltpu.VMEM((rows, width), F32),
            pltpu.VMEM((rows, 128), F32),
            pltpu.SMEM((1,), jnp.int32),
        ],
        cost=(8 * rows * width * ff, 22_000_000, 2 * rows * ff),
        input_output_aliases={} if gy is None else {7: 0},
    )(x, g, win, bias_in, wout, bias_out, center, x if gy is None else gy)


def weigh_kernel(split, which, *refs):
    hid, du, dy, x, bias, small = (refs[i : i + 2] for i in range(0, 12, 2))
    ff = hid[0].shape[1]
    width = dy[0].shape[1]
    step = pl.program_id(0)
    small = small[0][...] + small[1][...]
    row = lax.broadcasted_iota(jnp.int32, (16, width), 0)
    bias = (bias[0][...] + bias[1][...])[0:1]
    if ff < width:
        bias = jnp.concatenate([bias, jnp.zeros((1, width - ff), F32)], axis=1)
    rest = jnp.where(row == 0, bias, 0.0)
    rest = jnp.where(row == 1, small[0:1], rest)
    rest = jnp.where(row == 2, small[1:2], rest)

    def pair(i):
        rows, cols = (x, du) if split else (du, x)
        return rows[i][...], cols[i][...]

    def put(out):
        out[:ff] = (dot(hid[0][...], dy[0][...], 0, 0) + dot(hid[1][...], dy[1][...], 0, 0)).astype(BF)
        out[ff : 2 * ff] = (
            dot(*pair(0), 0, 0) + dot(*pair(1), 0, 0)
        ).astype(BF)
        out[2 * ff :] = rest.astype(BF)

    if not split:
        put(refs[12].at[0])
        return
    for late, out in enumerate(refs[12:]):

        @pl.when(step // 2 == late)
        def _(out=out):
            put(out.at[0])


def weigh(which, n, split, hid, du, dy, x, bias, small):
    rows, ff = hid[0].shape
    width = dy[0].shape[1]
    part = ff // n
    size = 2 * part + 16
    along = lambda i, which: (0, which[i])
    wide = pl.BlockSpec((rows, part), along)
    if split:
        first = pl.BlockSpec((1, size, width), lambda i, which: (jnp.minimum(i, 1), 0, 0))
        last = pl.BlockSpec((1, size, width), lambda i, which: (jnp.maximum(i - 2, 0), 0, 0))
        outs = [(first, (2, size, width), BF), (last, (2, size, width), BF)]
    else:
        outs = [(pl.BlockSpec((1, size, width), lambda i, which: (i, 0, 0)), (n, size, width), BF)]
    got = call(
        partial(weigh_kernel, split), "weigh", (n,),
        [wide] * 4 + [full((rows, width))] * 4 + [pl.BlockSpec((8, part), along)] * 2
        + [full((8, width))] * 2,
        outs, cost=(8 * rows * width * ff, 26_000_000, 0), ahead=1,
    )(which, *hid, *du, *dy, *x, *bias, *small)
    return got if split else got[0]


def unproject_kernel(*refs):
    one_ref, two_ref, *w_refs = refs[: GROUPS + 2]
    x_ref, dh_ref, vec_ref, out_ref = refs[GROUPS + 2 :]
    part = x_ref.shape[1] // GROUPS
    da = None
    for r, w in enumerate(w_refs):
        got = dot((one_ref, two_ref)[r // 2][r % 2], w[:, : 3 * part], 1, 1)
        da = got if da is None else da + got
    unit, inverse = normalize(x_ref[...].astype(F32))
    out_ref[...] = dh_ref[...] + normalize_back(da, unit, inverse, vec_ref[0:1])


def unproject(grads, weights, x, dh, vec):
    count, width = x.shape
    part = width // GROUPS
    rows = min(256, count)
    w = pl.BlockSpec((width, 640), lambda i: (0, 0), pipeline_mode=pl.Buffered(1))
    return call(
        unproject_kernel, "unproject", (count // rows,),
        [chunk((2, rows, 3 * part), 1)] * 2 + [w] * GROUPS
        + [chunk((rows, width)), chunk((rows, width)), full((8, width))],
        [(chunk((rows, width)), (count, width), F32)],
        cost=(6 * count * width * width, 20_000_000, 0),
    )(*grads, *weights, x, dh, vec)[0]


def add(a, b):
    return (a.astype(F32) + b.astype(F32)).astype(BF)


class Place:
    def __init__(self, mesh):
        self.n_dp = mesh.shape["dp"]
        self.n_e = mesh.shape["expert"]
        self.staged = self.n_dp == 4 and self.n_e == 8
        if not self.staged:
            return
        dev = lambda x, c, z, y: (x * 2 + c) * 8 + z * 2 + y
        every = [
            (x, c, z, y) for x in range(2) for c in range(2) for z in range(4) for y in range(2)
        ]
        to = lambda move: [(dev(*p), dev(*move(*p))) for p in every]
        self.core = to(lambda x, c, z, y: (x, 1 - c, z, y))
        self.x = to(lambda x, c, z, y: (1 - x, c, z, y))
        self.y = to(lambda x, c, z, y: (x, c, z, 1 - y))
        self.z = [to(lambda x, c, z, y, k=k: (x, c, z ^ k, y)) for k in range(1, 4)]

    def tables(self):
        r = jnp.arange(4, dtype=jnp.int32)
        i = jnp.arange(8, dtype=jnp.int32)
        if not self.staged:
            return r, i, r
        d, e = lax.axis_index("dp"), lax.axis_index("expert")
        z, y = e // 2, e % 2
        weighed = d ^ jnp.where(r < 2, 3 - 2 * r, 6 - 2 * r)
        return d ^ r, (z ^ i % 4) * 2 + (y ^ i // 4), weighed

    def move(self, array, way):
        return lax.ppermute(array, BOTH, way)


def whole_of(have):
    n_dp, n_e = lax.axis_size("dp"), lax.axis_size("expert")
    rows, cols = have.shape[1:]
    have = have.reshape(n_dp, n_e, rows, cols).transpose(1, 2, 0, 3)
    return have.reshape(n_e * rows, n_dp * cols)


def gather_all(array):
    return whole_of(lax.all_gather(array, BOTH, axis=0, tiled=False))


def scatter_all(array):
    n_dp, n_e = lax.axis_size("dp"), lax.axis_size("expert")
    rows, cols = array.shape[0] // n_e, array.shape[1] // n_dp
    parts = array.reshape(n_e, rows, n_dp, cols).transpose(2, 0, 1, 3)
    parts = parts.reshape(n_dp * n_e, rows, cols)
    return lax.psum_scatter(parts, BOTH, scatter_dimension=0, tiled=False)


def fetch(place, table, weights, out_weights, vectors, filler):
    barrier = lax.optimization_barrier
    stacked = jnp.stack(vectors)
    pad = 64 - len(vectors)
    if place.staged:
        rows = out_weights.shape[0]
        extra = jnp.concatenate([stacked.T, jnp.zeros((rows, pad), BF)], axis=1)
        shard = jnp.concatenate([*weights, extra], axis=1)
        own = jnp.stack([shard] + [place.move(shard, way) for way in place.z])
        own, out_weights, filler = barrier((own, out_weights, filler))
        got = place.move(own, place.y)
        out_own = jnp.stack([out_weights] + [place.move(out_weights, way) for way in place.z])
        got, out_own = barrier((got, out_own))
        near = assemble(table, own, got)
        across = place.move(near, place.x)
        far = place.move(near, place.core)
        return (near, far, across), (out_own, place.move(out_own, place.y)), filler
    vecs = lax.all_gather(stacked, "expert", axis=1, tiled=True)
    width = vecs.shape[1]
    extra = jnp.concatenate([vecs, jnp.zeros((pad, width), BF)]).T
    extra = jnp.broadcast_to(extra[None], (GROUPS, width, 64))
    by_group = lambda w: gather_all(w).reshape(width, GROUPS, -1).transpose(1, 0, 2)
    grouped = jnp.concatenate([*(by_group(w) for w in weights), extra], axis=2)
    out = by_group(out_weights)
    return [grouped[i] for i in range(GROUPS)], [out[i] for i in range(GROUPS)], filler


def reduce_y(place, keep, send):
    got = place.move(send, place.y)
    return keep[0].astype(F32) + got[0].astype(F32), [add(keep[k], got[k]) for k in range(1, 4)]


def reduce_z(place, sends):
    return [place.move(part, way) for part, way in zip(sends, place.z)]


def columns_of(place, total, count):
    cols = (FAR - 640) // 2
    parts = [total[:, i * cols : (i + 1) * cols] for i in range(3)]
    vecs = total[:, 576 : 576 + 8].T
    vecs = vecs + place.move(vecs, place.core)
    vecs = vecs + place.move(vecs, place.x)
    return parts, [vecs[i] for i in range(count)]


def reduce_plain(near, far, count):
    slabs = jnp.stack([a[:, :640] for a in (*near, *far)])
    width = slabs.shape[1]
    part = width // GROUPS
    whole = lambda array: array.transpose(1, 0, 2).reshape(width, width)
    parts = [whole(slabs[:, :, i * part : (i + 1) * part]) for i in range(3)]
    parts.append(whole(jnp.stack([far[0][:, -part:], far[1][:, -part:]] + [a[:, 640:-part] for a in far])))
    parts = [scatter_all(p).astype(F32) for p in parts]
    vecs = jnp.sum(slabs[:, :, 576 : 576 + count].astype(F32), axis=0).T
    vecs = lax.psum_scatter(vecs, "expert", scatter_dimension=1, tiled=True)
    vecs = lax.psum(vecs, "dp")
    return parts, [vecs[i] for i in range(count)]


def shards(
    place,
    block_entries,
    assignments,
    positions_within,
    specialist_quotas,
    standardize_one_scale,
    standardize_one_shift,
    asking_weights,
    asking_shift,
    lookup_weights,
    content_weights,
    content_shift,
    context_mixing_weights,
    context_mixing_shift,
    standardize_two_scale,
    standardize_two_shift,
    gating_prototypes,
    specialist_widen_weights,
    specialist_widen_shift,
    specialist_contract_weights,
    specialist_contract_shift,
    upstream_adjoint,
):
    count, width = block_entries.shape
    experts = specialist_quotas.shape[0]
    cap = count // experts
    n_dp = place.n_dp
    order, table, weighed = place.tables()
    barrier = lax.optimization_barrier

    chosen = assignments[:, None] == lax.broadcasted_iota(jnp.int32, (count, experts), 1)
    limit = jnp.sum(jnp.where(chosen, specialist_quotas[None, :], 0), axis=1)
    kept = positions_within < limit
    target = jnp.where(kept, assignments * cap + positions_within, count)
    late = positions_within >= cap // 2
    halved = jnp.where(late, positions_within + (count - cap) // 2, positions_within)
    halved = jnp.where(kept, assignments * (cap // 2) + halved, count)

    def exchange(rows):
        sent = rows.reshape(experts, -1, width)
        got = lax.all_to_all(sent, "expert", split_axis=0, concat_axis=0, tiled=True)
        return got.reshape(rows.shape)

    weights, out, sent_g = fetch(
        place,
        table,
        (asking_weights, lookup_weights, content_weights),
        context_mixing_weights,
        (
            standardize_one_scale,
            standardize_one_shift,
            asking_shift,
            content_shift,
            context_mixing_shift,
            standardize_two_scale,
            standardize_two_shift,
        ),
        dispatch(target, upstream_adjoint),
    )

    sent_g, first = barrier((sent_g, weights[1]))
    weights = (weights[0], first, *weights[2:])
    rows_g = exchange(sent_g).reshape(experts, 2, cap // 2, width)

    *before, low_in, vec = attend(0, order, weights[:2], x=block_entries)
    if place.staged:
        before, out = barrier((before, out))
        out_near = assemble(table, *out)
        before, across, out_near = barrier((before, weights[2], out_near))
        weights = (*weights[:2], across, place.move(across, place.core))
        out_across = place.move(out_near, place.x)
        out = (out_near, place.move(out_near, place.core))
    qkv, ctx, lse = attend(1, order, weights[2:], low=low_in, vec=vec, before=before)
    ctx, rows_g = barrier((ctx, rows_g))
    if place.staged:
        ctx, out_across = barrier((ctx, out_across))
        out += (out_across, place.move(out_across, place.core))
    h1, whole_o, sent_one, sent_two = mix(order, block_entries, ctx, out, vec, halved)

    x_one = exchange(sent_one)
    x_two = exchange(sent_two)
    matrices = (
        specialist_widen_weights[0], specialist_widen_shift, specialist_contract_weights[0],
        specialist_contract_shift, gating_prototypes,
    )
    gy, dm_one, dy_one, hid_one, du_one, dbin_one, small_one = expert(
        0, x_one, rows_g, *matrices, None
    )
    x_two, dm_one = barrier((x_two, dm_one))
    dm_one = exchange(dm_one)
    gy, dm_two, dy_two, hid_two, du_two, dbin_two, small_two = expert(
        1, x_two, rows_g, *matrices, gy
    )
    dm_one, dm_two, hid_two = barrier((dm_one, dm_two, hid_two))
    dm_two = exchange(dm_two)
    sides = (
        (hid_one, hid_two), (du_one, du_two), (dy_one, dy_two), (x_one, x_two),
        (dbin_one, dbin_two), (small_one, small_two),
    )
    if place.staged:
        grads_far, grads = weigh(
            weighed, n_dp, True, *sides
        )
        grads_far, gy, dm_two = barrier((grads_far, gy, dm_two))
        came_far = place.move(grads_far, place.core)
        crossing = add(grads[0], came_far[0])
        crossing, h1 = barrier((crossing, h1))
        came = place.move(crossing, place.x)
    else:
        grads = weigh(jnp.arange(n_dp, dtype=jnp.int32), n_dp, False, *sides)
        grads = lax.psum_scatter(grads, "dp", scatter_dimension=0, tiled=False)
    gy = exchange(gy.reshape(count, width))

    dh1, dctx, grad_o, two = unmix(
        order, h1, upstream_adjoint, dm_one, dm_two, halved, ctx, whole_o, vec
    )
    back = lambda half, dctx: attend_back(
        half, order, table, qkv, ctx, dctx, lse, low_in, grad_o, weights[2 * half : 2 * half + 2],
        two,
    )
    if place.staged:
        far, keep, send, *more = back(1, dctx)
        more = [place.move(m, place.core) for m in more]
        far, gy = barrier((far, gy))
        output = finish(h1, target, gy)
        send = add(send, more[1])
        dctx, output, send = barrier((dctx, output, send))
        across, sends = reduce_y(place, add(keep, more[0]), send)
        near, keep, send, *more = back(0, dctx)
        near, keep, send, more, across, sends = barrier((near, keep, send, more, across, sends))
        more = [place.move(m, place.core) for m in more]
        got = reduce_z(place, sends)
        send, keep = add(send, more[1]), add(keep, more[0])
        near, send, keep = barrier((near, send, keep))
        got_y = place.move(send, place.y)
        input_grad = unproject((near, far), weights, block_entries, dh1, vec)
        got_far = got
        got, input_grad, came, got_far = barrier((got_y, input_grad, came, got_far))
        sum_o = across + sum(g.astype(F32) for g in got_far)
        cols = width // GROUPS
        across = place.move(sum_o[:, :-cols].astype(BF), place.x)
        total = keep[0].astype(F32) + got[0].astype(F32)
        got = reduce_z(place, [add(keep[k], got[k]) for k in range(1, 4)])
        pick = lambda at: sum(
            a[at : at + width].astype(F32) for a in (grads[1], came_far[1], came)
        )
        got, grads, across = barrier((got, [pick(0), pick(width), pick(2 * width)], across))
        total += across[:, :640].astype(F32)
        sum_o = sum_o[:, -cols:] + across[:, 640:].astype(F32)
        total += sum(g.astype(F32) for g in got)
        (sum_q, sum_k, sum_v), small = columns_of(place, total, 7)
    else:
        parts = [back(half, dctx) for half in range(2)]
        slabs = [
            [jnp.concatenate(p[1 + 2 * g : 3 + 2 * g]).reshape(width, -1) for g in range(2)]
            for p in parts
        ]
        (sum_q, sum_k, sum_v, sum_o), small = reduce_plain(*slabs, 7)
        input_grad = unproject([p[0] for p in parts], weights, block_entries, dh1, vec)
        output = finish(h1, target, gy)

        part = (grads.shape[0] - 16) // 2
        grads = [grads[:part], grads[part : 2 * part].T, grads[2 * part :]]
        grads = [g.astype(F32) for g in grads]

    grad_out, grad_in, rest = grads
    part = grad_out.shape[0]
    own = lax.axis_index("dp") * (width // n_dp)
    grad_bin = rest[0:1, :part]
    grad_bout = lax.dynamic_slice(rest[1:2], (0, own), (1, width // n_dp))
    grad_centers = rest[2:3]
    return (
        output,
        input_grad,
        small[0],
        small[1],
        sum_q,
        small[2],
        sum_k,
        sum_v,
        small[3],
        sum_o,
        small[4],
        small[5],
        small[6],
        grad_centers,
        grad_in[None],
        grad_bin,
        grad_out[None],
        grad_bout,
    )


def solution(mesh):
    placed = (
        P(("dp", "expert"), None),
        P(("dp", "expert")),
        P(("dp", "expert")),
        P(),
        P("expert"),
        P("expert"),
        P("expert", "dp"),
        P("expert"),
        P("expert", "dp"),
        P("expert", "dp"),
        P("expert"),
        P("expert", "dp"),
        P("expert"),
        P("expert"),
        P("expert"),
        P("expert", None),
        P("expert", None, None),
        P("expert", None),
        P("expert", None, None),
        P("expert", None),
        P(("dp", "expert"), None),
    )
    return jax.shard_map(
        partial(shards, Place(mesh)),
        mesh=mesh,
        in_specs=placed,
        out_specs=(
            P(("dp", "expert"), None),
            P(("dp", "expert"), None),
            P("expert"),
            P("expert"),
            P("expert", "dp"),
            P("expert"),
            P("expert", "dp"),
            P("expert", "dp"),
            P("expert"),
            P("expert", "dp"),
            P("expert"),
            P("expert"),
            P("expert"),
            P("expert", None),
            P("expert", None, "dp"),
            P("expert", "dp"),
            P("expert", "dp", None),
            P("expert", "dp"),
        ),
        check_vma=False,
    )
```

```python
from functools import partial

import jax
import jax.numpy as jnp
from jax import lax
from jax.experimental import pallas as pl
from jax.experimental.pallas import tpu as pltpu
from jax.sharding import PartitionSpec as P

HEADS = 12
HEAD_DIM = 64
SEQ_LEN = 1024
GROUPS = 4

EPSILON = 1e-05
MASKED = -1e30
FAR = 1024
BOTH = ("dp", "expert")
BF = jnp.bfloat16
F32 = jnp.float32


def dot(left, right, left_dim, right_dim):
    return lax.dot_general(
        left, right, (((left_dim,), (right_dim,)), ((), ())), preferred_element_type=F32
    )


def normalize(values):
    center = jnp.mean(values, axis=-1, keepdims=True)
    centered = values - center
    inverse = lax.rsqrt(jnp.mean(centered * centered, axis=-1, keepdims=True) + EPSILON)
    return (centered * inverse, inverse)


def normalize_back(grad, normed, inverse, gain):
    scaled = grad * gain
    return inverse * (
        scaled
        - jnp.mean(scaled, axis=-1, keepdims=True)
        - normed * jnp.mean(scaled * normed, axis=-1, keepdims=True)
    )


def call(
    kernel, name, grid, in_specs, outs, scratch=(), vmem=60, cost=(0, 0, 0), ahead=0, **more
):
    return pl.pallas_call(
        kernel,
        name=name,
        grid_spec=pltpu.PrefetchScalarGridSpec(
            num_scalar_prefetch=ahead,
            grid=grid,
            in_specs=in_specs,
            out_specs=[o[0] for o in outs],
            scratch_shapes=list(scratch),
        ),
        out_shape=[jax.ShapeDtypeStruct(o[1], o[2]) for o in outs],
        compiler_params=pltpu.CompilerParams(vmem_limit_bytes=vmem << 20),
        cost_estimate=pl.CostEstimate(
            flops=cost[0], bytes_accessed=cost[1], transcendentals=cost[2]
        ),
        **more,
    )


def full(shape):
    return pl.BlockSpec(
        shape, lambda *_: (0,) * len(shape), pipeline_mode=pl.Buffered(1)
    )


SCALARS = pl.BlockSpec(memory_space=pltpu.SMEM)
PLACED = pl.BlockSpec(memory_space=pl.ANY)


def assemble_kernel(table, own_ref, got_ref, out_ref, sems):
    rows = own_ref.shape[1]
    copies = []
    for i in range(8):
        src = (own_ref, got_ref)[i // 4].at[i % 4]
        at = pl.multiple_of(rows * table[i], 32)
        copies.append(pltpu.make_async_copy(src, out_ref.at[pl.ds(at, rows)], sems.at[i]))
    for c in copies:
        c.start()
    for c in copies:
        c.wait()


def assemble(table, own, got):
    rows, cols = own.shape[1:]
    return call(
        assemble_kernel, "assemble", (1,), [SCALARS, PLACED, PLACED],
        [(full((8 * rows, cols)), (8 * rows, cols), BF)],
        [pltpu.SemaphoreType.DMA((8,))],
        cost=(0, 4 * rows * cols * 8, 0),
    )(table, own, got)[0]


def chunk(shape, axis=0):
    return pl.BlockSpec(shape, lambda i: tuple(i if a == axis else 0 for a in range(len(shape))))


def attend_kernel(half, order, *refs):
    if half:
        low_ref, vec_ref, w_one, w_two = refs[:4]
        qkv_ref, ctx_ref, lse_ref = refs[7:]
    else:
        x_ref, w_one, w_two, qkv_ref, ctx_ref, lse_ref, low_ref, vec_ref = refs
    step = pl.program_id(0)
    count, width = low_ref.shape
    part = width // GROUPS
    if not half:

        @pl.when(step == 0)
        def _():
            vec_ref[...] = w_one[:, 512:640].astype(F32).T[64:72]
            for at in range(0, count, 256):
                unit, _ = normalize(x_ref[at : at + 256].astype(F32))
                low_ref[at : at + 256] = (unit * vec_ref[0:1] + vec_ref[1:2]).astype(BF)

    zero = jnp.zeros((1, part), F32)
    bias_q = bias_v = zero
    for n in range(GROUPS):
        here = order[2 * half + step] == n
        bias_q = jnp.where(here, vec_ref[2:3, part * n : part * n + part], bias_q)
        bias_v = jnp.where(here, vec_ref[3:4, part * n : part * n + part], bias_v)
    bias = jnp.concatenate([bias_q, zero, bias_v], axis=1)
    w = jnp.where(step == 0, w_one[...], w_two[...])[:, : 3 * part]
    for at in range(0, count, 512):
        qkv_ref[0, at : at + 512] = (dot(low_ref[at : at + 512], w, 1, 0) + bias).astype(BF)
    for base in range(0, count, SEQ_LEN):
        block = min(512, SEQ_LEN)
        for h in range(part // HEAD_DIM):
            at = h * HEAD_DIM
            v = qkv_ref[0, base : base + SEQ_LEN, 2 * part + at : 2 * part + at + HEAD_DIM].T
            for start in range(0, SEQ_LEN, block):
                stop = start + block
                q = qkv_ref[0, base + start : base + stop, at : at + HEAD_DIM] * BF(HEAD_DIM**-0.5)
                k = qkv_ref[0, base : base + stop, part + at : part + at + HEAD_DIM]
                row = lax.broadcasted_iota(jnp.int32, (stop, block), 0)
                col = lax.broadcasted_iota(jnp.int32, (stop, block), 1) + start
                scores = jnp.where(row <= col, dot(k, q, 1, 1), MASKED)
                top = jnp.max(scores, axis=0, keepdims=True)
                probs = jnp.exp(scores - top)
                total = jnp.sum(probs, axis=0, keepdims=True)
                out = dot(v[:, :stop], probs.astype(BF), 1, 0) / total
                ctx_ref[0, base + start : base + stop, at : at + HEAD_DIM] = out.T.astype(BF)
                lse_ref[0, h : h + 1, base + start : base + stop] = top + jnp.log(total)


def attend(half, order, weights, x=None, low=None, vec=None, before=()):
    count, width = (low if half else x).shape
    part = width // GROUPS
    at = lambda g: (2 * half + g, 0, 0)
    outs = [
        (pl.BlockSpec((1, count, 3 * part), at), (GROUPS, count, 3 * part), BF),
        (pl.BlockSpec((1, count, part), at), (GROUPS, count, part), BF),
        (pl.BlockSpec((1, 8, count), at), (GROUPS, 8, count), F32),
    ]
    w = [pl.BlockSpec((width, 640), lambda g: (0, 0), pipeline_mode=pl.Buffered(1))] * 2
    if half:
        ins, args = [full((count, width)), full((8, width))] + w + [PLACED] * 3, (low, vec)
    else:
        outs += [(full((count, width)), (count, width), BF), (full((8, width)), (8, width), F32)]
        ins, args = [full((count, width))] + w, (x,)
    return call(
        partial(attend_kernel, half), "attend", (2,), [SCALARS] + ins, outs,
        cost=(12_000_000_000, 8_000_000, 4_000_000),
        input_output_aliases={5 + i: i for i in range(len(before))},
    )(order, *args, *weights, *before)


def attend_back_kernel(half, order, table, *refs):
    qkv_ref, ctx_ref, dctx_ref, lse_ref, low_ref, w_one, w_two, two_ref = refs[:8]
    if half:
        o_refs, refs = refs[8:10], refs[2:]
    out_ref, *slabs, dq_ref, stage, sems = refs[8:]
    step = pl.program_id(0)
    count, width = low_ref.shape
    part = width // GROUPS
    inner = (ctx_ref[0].astype(F32) * dctx_ref[0].astype(F32)).T
    block = min(256, SEQ_LEN)
    for base in range(0, count, SEQ_LEN):
        last = base + SEQ_LEN
        for h in range(part // HEAD_DIM):
            at = h * HEAD_DIM
            q = qkv_ref[0, base:last, at : at + HEAD_DIM] * BF(HEAD_DIM**-0.5)
            do = dctx_ref[0, base:last, at : at + HEAD_DIM]
            turned = qkv_ref[0, base:last, part + at : part + at + HEAD_DIM].T
            row_dot = jnp.sum(inner[at : at + HEAD_DIM, base:last], axis=0, keepdims=True)
            for start in range(0, SEQ_LEN, block):
                stop = start + block
                rows = slice(base + start, base + stop)
                k = qkv_ref[0, rows, part + at : part + at + HEAD_DIM]
                v = qkv_ref[0, rows, 2 * part + at : 2 * part + at + HEAD_DIM]
                row = lax.broadcasted_iota(jnp.int32, (block, SEQ_LEN - start), 0)
                col = lax.broadcasted_iota(jnp.int32, (block, SEQ_LEN - start), 1)
                lse = lse_ref[0, h : h + 1, base + start : last]
                probs = jnp.where(row <= col, jnp.exp(dot(k, q[start:], 1, 1) - lse), 0.0)
                dscores = (probs * (dot(v, do[start:], 1, 1) - row_dot[:, start:])).astype(BF)
                dk = dot(dscores, q[start:], 1, 0)
                dv = dot(probs.astype(BF), do[start:], 1, 0)
                dq = dot(turned[:, start:stop], dscores, 1, 0)
                if start:
                    dq_ref[:, start:] += dq
                else:
                    dq_ref[...] = dq
                out_ref[0, rows, part + at : part + at + HEAD_DIM] = dk.astype(BF)
                out_ref[0, rows, 2 * part + at : 2 * part + at + HEAD_DIM] = dv.astype(BF)
            out_ref[0, base:last, at : at + HEAD_DIM] = (dq_ref[...].T * HEAD_DIM**-0.5).astype(BF)
    sums = jnp.sum(out_ref[0].astype(F32), axis=0, keepdims=True)
    grad = dot(low_ref[...], out_ref[0], 0, 0)
    w = jnp.where(step == 0, w_one[...], w_two[...]).astype(F32)
    shift = jnp.sum(w[:, : 3 * part] * sums, axis=-1, keepdims=True)
    gain = jnp.sum(w[:, : 3 * part] * grad, axis=-1, keepdims=True)
    gain = (gain - w[:, 577:578] * shift) / w[:, 576:577]
    row = lax.broadcasted_iota(jnp.int32, (width, part), 0) - order[2 * half + step] * part
    here = row == lax.broadcasted_iota(jnp.int32, (width, part), 1)
    columns = [gain, shift] + [
        jnp.sum(jnp.where(here, sums[:, at : at + part], 0.0), axis=-1, keepdims=True)
        for at in (0, 2 * part)
    ]
    lane = lax.broadcasted_iota(jnp.int32, (width, 64), 1)
    vecs = jnp.zeros((width, 64), F32)
    if not half:
        more = jnp.concatenate([two_ref[...], jnp.zeros((120, width), F32)]).T[:, :64]
        vecs = jnp.where(step == 0, more, vecs)
    for i, column in enumerate(columns):
        vecs = jnp.where(lane == i, column, vecs)
    stage[:, : 3 * part] = grad.astype(BF)
    stage[:, 3 * part : 640] = vecs.astype(BF)
    if half:
        stage[:, 640:] = jnp.concatenate([o_refs[0][0], o_refs[1][0]], axis=1)
    rows = width // 8
    for g in range(2):

        @pl.when(step == g)
        def _(g=g):
            copies = []
            for i in range(8):
                src = stage.at[pl.ds(pl.multiple_of(rows * table[i], 32), rows)]
                dst = slabs[2].at[i] if g else slabs[i // 4].at[i % 4]
                copies.append(pltpu.make_async_copy(src, dst, sems.at[i]))
            for c in copies:
                c.start()
            for c in copies:
                c.wait()


def attend_back(half, order, table, qkv, ctx, dctx, lse, low, o_part, weights, two):
    groups, count, part = qkv.shape
    part //= 3
    width = low.shape[1]
    at = lambda g, *_: (2 * half + g, 0, 0)
    cols = FAR if half else 640
    slabs = [(PLACED, (n, width // 8, cols), BF) for n in (4, 4, 8)]
    o_specs = [
        pl.BlockSpec((1, width, part), lambda g, order, table, b=b: (order[b + g], 0, 0))
        for b in ((2, 0) if half else ())
    ]
    return call(
        partial(attend_back_kernel, half), "attend_back", (2,),
        [
            pl.BlockSpec((1, count, 3 * part), at),
            pl.BlockSpec((1, count, part), at),
            pl.BlockSpec((1, count, part), at),
            pl.BlockSpec((1, 8, count), at),
            full((count, width)),
        ]
        + [pl.BlockSpec((width, 640), lambda *_: (0, 0), pipeline_mode=pl.Buffered(1))] * 2
        + [full((8, width))] + o_specs,
        [(pl.BlockSpec((1, count, 3 * part), lambda g, *_: (g, 0, 0)), (2, count, 3 * part), BF)]
        + slabs,
        [
            pltpu.VMEM((HEAD_DIM, SEQ_LEN), F32),
            pltpu.VMEM((width, cols), BF),
            pltpu.SemaphoreType.DMA((8,)),
        ],
        cost=(24_000_000_000, 14_000_000, 4_000_000), ahead=2,
    )(order, table, qkv, ctx, dctx, lse, low, *weights, two, *[o_part] * len(o_specs))


def dispatch_kernel(first, target_ref, rows_ref, out_ref):
    count = rows_ref.shape[0]
    for at in range(0, out_ref.shape[0], 256):
        slot = lax.broadcasted_iota(jnp.int32, (256, count), 0) + (first + at)
        picks = (target_ref[...] == slot).astype(F32).astype(BF)
        out_ref[at : at + 256] = dot(picks, rows_ref[...], 1, 0).astype(BF)


def dispatch(target, rows, first=0):
    count, width = rows.shape
    slots = count - first
    return call(
        partial(dispatch_kernel, first), "dispatch", (1,),
        [full((1, count)), full((count, width))],
        [(full((slots, width)), (slots, width), BF)],
        cost=(2 * count * count * width, 3_000_000, 0),
    )(target.reshape(1, count), rows)[0]


def mix_kernel(order, x_ref, ctx_ref, vec_ref, target_ref, *refs):
    wo_refs, (h_ref, whole_ref, low_ref, sent_ref) = refs[:GROUPS], refs[GROUPS:]
    rows, width = x_ref.shape
    count = low_ref.shape[0]
    part = width // GROUPS
    step = pl.program_id(0)

    @pl.when(step == 0)
    def _():
        for q in range(GROUPS):
            at = pl.ds(pl.multiple_of(order[q] * part, 64), part)
            pieces = [wo[at, :] for wo in wo_refs]
            for n in range(GROUPS):
                piece = pieces[0]
                for r in range(1, GROUPS):
                    piece = jnp.where(order[r] == n, pieces[r], piece)
                whole_ref[q * part : q * part + part, n * part : n * part + part] = piece

    h = x_ref[...].astype(F32) + vec_ref[4:5]
    for r in range(GROUPS):
        h += dot(ctx_ref[r], whole_ref[r * part : r * part + part], 1, 0)
    h_ref[...] = h
    unit, _ = normalize(h)
    low_ref[pl.ds(pl.multiple_of(step * rows, 256), rows)] = (
        unit * vec_ref[5:6] + vec_ref[6:7]
    ).astype(BF)

    @pl.when(step == pl.num_programs(0) - 1)
    def _():
        for at in range(0, count // 2, 256):
            index = lax.broadcasted_iota(jnp.int32, (256, count), 0) + at
            picks = (target_ref[...] == index).astype(F32).astype(BF)
            sent_ref[at : at + 256] = dot(picks, low_ref[...], 1, 0).astype(BF)


def mix(order, x, ctx, weights, vec, target):
    count, width = x.shape
    part = width // GROUPS
    rows = min(256, count)
    return call(
        mix_kernel, "mix", (count // rows,),
        [SCALARS, chunk((rows, width)), chunk((GROUPS, rows, part), 1), full((8, width)),
         full((1, count))] + [full((width, part))] * GROUPS,
        [
            (chunk((rows, width)), (count, width), F32),
            (full((width, width)), (width, width), BF),
            (full((count, width)), (count, width), BF),
            (full((count // 2, width)), (count // 2, width), BF),
        ],
        cost=(2 * count * width * (width + count), 12_000_000, 0),
    )(order, x, ctx, vec, target.reshape(1, count), *weights)


def unmix_kernel(
    order, h_ref, g_ref, dm_one, dm_two, target_ref, ctx_ref, whole_ref, vec_ref,
    dh_ref, dctx_ref, grad_ref, sum_ref, total_ref,
):
    rows, width = h_ref.shape
    part = width // GROUPS
    step = pl.program_id(0)
    dm = None
    for half, sent in enumerate((dm_one, dm_two)):
        index = lax.broadcasted_iota(jnp.int32, (rows, sent.shape[0]), 1) + half * sent.shape[0]
        picks = (target_ref[...] == index).astype(F32).astype(BF)
        got = dot(picks, sent[...], 1, 0)
        dm = got if dm is None else dm + got
    unit, inverse = normalize(h_ref[...])
    dh = g_ref[...].astype(F32) + normalize_back(dm, unit, inverse, vec_ref[5:6])
    dh_ref[...] = dh
    low = dh.astype(BF)
    sums = [
        jnp.sum(term, axis=0, keepdims=True) for term in (low.astype(F32), dm * unit, dm)
    ]
    zeros = jnp.zeros((1, width), F32)
    sums = jnp.concatenate([zeros] * 4 + sums + [zeros])
    for r in range(GROUPS):
        dctx_ref[r] = dot(low, whole_ref[r * part : r * part + part], 1, 1).astype(BF)
    grads = [dot(ctx_ref[q], low, 0, 0) for q in range(GROUPS)]

    @pl.when(step == 0)
    def _():
        sum_ref[...] = sums
        for q in range(GROUPS):
            total_ref[q] = grads[q]

    @pl.when(step > 0)
    def _():
        sum_ref[...] += sums
        for q in range(GROUPS):
            total_ref[q] += grads[q]

    @pl.when(step == pl.num_programs(0) - 1)
    def _():
        for q in range(GROUPS):
            grad = total_ref[q].astype(BF)
            at = pl.ds(pl.multiple_of(order[q] * part, 64), part)
            for n in range(GROUPS):
                grad_ref[n, at, :] = grad[:, n * part : n * part + part]


def unmix(order, h, g, dm_one, dm_two, target, ctx, whole, vec):
    count, width = h.shape
    part = width // GROUPS
    rows = min(256, count)
    half = full((count // 2, width))
    by_rows, by_ctx = chunk((rows, width)), chunk((GROUPS, rows, part), 1)
    return call(
        unmix_kernel, "unmix", (count // rows,),
        [SCALARS, by_rows, by_rows, half, half, chunk((rows, 1)), by_ctx, full((width, width)),
         full((8, width))],
        [
            (by_rows, (count, width), F32),
            (by_ctx, (GROUPS, count, part), BF),
            (full((GROUPS, width, part)), (GROUPS, width, part), BF),
            (full((8, width)), (8, width), F32),
        ],
        [pltpu.VMEM((GROUPS, part, width), F32)],
        cost=(2 * count * width * (2 * width + count), 20_000_000, 0),
    )(order, h, g, dm_one, dm_two, target.reshape(count, 1), ctx, whole, vec)


def finish_kernel(h_ref, target_ref, gy_ref, out_ref):
    slot = lax.broadcasted_iota(jnp.int32, (h_ref.shape[0], gy_ref.shape[0]), 1)
    picks = (target_ref[...] == slot).astype(F32).astype(BF)
    out_ref[...] = (h_ref[...] + dot(picks, gy_ref[...], 1, 0)).astype(BF)


def finish(h, target, gy):
    count, width = h.shape
    rows = min(256, count)
    return call(
        finish_kernel, "finish", (count // rows,),
        [chunk((rows, width)), chunk((rows, 1)), full((count, width))],
        [(chunk((rows, width)), (count, width), BF)],
        cost=(2 * count * count * width, 6_000_000, 0),
    )(h, target.reshape(count, 1), gy)[0]


def gelu_pair(v):
    cdf = 0.5 + 0.5 * lax.erf(v * 0.5**0.5)
    return v * cdf, cdf + v * jnp.exp(-0.5 * v * v) * (0.5 / jnp.pi) ** 0.5


def expert_kernel(
    x_ref, g_ref, win_ref, bin_ref, wout_ref, bout_ref, center_ref, _,
    gy_ref, dm_ref, dy_ref, hid_ref, du_ref, dbin_ref, small_ref,
    y_acc, dm_acc, gate_ref, gates,
):
    step = pl.program_id(0)
    rows, width = x_ref.shape

    @pl.when(step == 0)
    def _():
        z = jnp.sum(x_ref[...].astype(F32) * center_ref[...].astype(F32), axis=-1, keepdims=True)
        gate = 1.0 / (1.0 + jnp.exp(-z))
        gate_ref[...] = jnp.broadcast_to(gate, gate_ref.shape)
        dy_ref[...] = (gate * g_ref[...].reshape(rows, width).astype(F32)).astype(BF)

    act, slope = gelu_pair(dot(x_ref[...], win_ref[...], 1, 0) + bin_ref[...].astype(F32))
    hid = act.astype(BF)
    hid_ref[...] = hid
    y = dot(hid, wout_ref[...], 1, 0)
    du = (dot(dy_ref[...], wout_ref[...], 1, 1) * slope).astype(BF)
    du_ref[...] = du
    dbin_ref[...] = jnp.broadcast_to(
        jnp.sum(du.astype(F32), axis=0, keepdims=True), dbin_ref.shape
    )
    dm = dot(du, win_ref[...], 1, 1)

    @pl.when(step == 0)
    def _():
        y_acc[...] = y
        dm_acc[...] = dm

    @pl.when(step > 0)
    def _():
        y_acc[...] += y
        dm_acc[...] += dm

    @pl.when(step == pl.num_programs(0) - 1)
    def _():
        gate = gate_ref[:, :1]
        g = g_ref[...].reshape(rows, width).astype(F32)
        y = (y_acc[...] + bout_ref[...].astype(F32)).astype(BF).astype(F32)
        gy_ref[...] = (gate * y).astype(BF).reshape(gy_ref.shape)
        dz = gate * (1.0 - gate) * jnp.sum(g * y, axis=-1, keepdims=True)
        dm_ref[...] = (dm_acc[...] + dz * center_ref[...].astype(F32)).astype(BF)
        small_ref[0:1, :] = jnp.sum(dy_ref[...].astype(F32), axis=0, keepdims=True)
        small_ref[1:2, :] = jnp.sum(dz * x_ref[...].astype(F32), axis=0, keepdims=True)


def expert(half, x, g, win, bias_in, wout, bias_out, center, gy):
    rows, width = x.shape
    ff = win.shape[1]
    step = min(1024, ff)
    along = lambda i: (0, i)
    side = pl.BlockSpec(
        (g.shape[0], 1) + g.shape[2:], lambda i: (0, half, 0, 0), pipeline_mode=pl.Buffered(1)
    )
    return call(
        expert_kernel, "expert", (ff // step,),
        [
            full((rows, width)),
            side,
            pl.BlockSpec((width, step), along),
            pl.BlockSpec((1, step), along),
            pl.BlockSpec((step, width), lambda i: (i, 0)),
            full((1, width)),
            full((1, width)),
            PLACED,
        ],
        [
            (side, g.shape, BF),
            (full((rows, width)), (rows, width), BF),
            (full((rows, width)), (rows, width), BF),
            (pl.BlockSpec((rows, step), along), (rows, ff), BF),
            (pl.BlockSpec((rows, step), along), (rows, ff), BF),
            (pl.BlockSpec((8, step), along), (8, ff), F32),
            (full((8, width)), (8, width), F32),
        ],
        [
            pltpu.VMEM((rows, width), F32),
            pltpu.VMEM((rows, width), F32),
            pltpu.VMEM((rows, 128), F32),
            pltpu.SMEM((1,), jnp.int32),
        ],
        cost=(8 * rows * width * ff, 22_000_000, 2 * rows * ff),
        input_output_aliases={} if gy is None else {7: 0},
    )(x, g, win, bias_in, wout, bias_out, center, x if gy is None else gy)


def weigh_kernel(split, which, *refs):
    hid, du, dy, x, bias, small = (refs[i : i + 2] for i in range(0, 12, 2))
    ff = hid[0].shape[1]
    width = dy[0].shape[1]
    step = pl.program_id(0)
    small = small[0][...] + small[1][...]
    row = lax.broadcasted_iota(jnp.int32, (16, width), 0)
    bias = (bias[0][...] + bias[1][...])[0:1]
    if ff < width:
        bias = jnp.concatenate([bias, jnp.zeros((1, width - ff), F32)], axis=1)
    rest = jnp.where(row == 0, bias, 0.0)
    rest = jnp.where(row == 1, small[0:1], rest)
    rest = jnp.where(row == 2, small[1:2], rest)

    def pair(i):
        rows, cols = (x, du) if split else (du, x)
        return rows[i][...], cols[i][...]

    def put(out):
        out[:ff] = (dot(hid[0][...], dy[0][...], 0, 0) + dot(hid[1][...], dy[1][...], 0, 0)).astype(BF)
        out[ff : 2 * ff] = (
            dot(*pair(0), 0, 0) + dot(*pair(1), 0, 0)
        ).astype(BF)
        out[2 * ff :] = rest.astype(BF)

    if not split:
        put(refs[12].at[0])
        return
    for late, out in enumerate(refs[12:]):

        @pl.when(step // 2 == late)
        def _(out=out):
            put(out.at[0])


def weigh(which, n, split, hid, du, dy, x, bias, small):
    rows, ff = hid[0].shape
    width = dy[0].shape[1]
    part = ff // n
    size = 2 * part + 16
    along = lambda i, which: (0, which[i])
    wide = pl.BlockSpec((rows, part), along)
    if split:
        first = pl.BlockSpec((1, size, width), lambda i, which: (jnp.minimum(i, 1), 0, 0))
        last = pl.BlockSpec((1, size, width), lambda i, which: (jnp.maximum(i - 2, 0), 0, 0))
        outs = [(first, (2, size, width), BF), (last, (2, size, width), BF)]
    else:
        outs = [(pl.BlockSpec((1, size, width), lambda i, which: (i, 0, 0)), (n, size, width), BF)]
    got = call(
        partial(weigh_kernel, split), "weigh", (n,),
        [wide] * 4 + [full((rows, width))] * 4 + [pl.BlockSpec((8, part), along)] * 2
        + [full((8, width))] * 2,
        outs, cost=(8 * rows * width * ff, 26_000_000, 0), ahead=1,
    )(which, *hid, *du, *dy, *x, *bias, *small)
    return got if split else got[0]


def unproject_kernel(*refs):
    one_ref, two_ref, *w_refs = refs[: GROUPS + 2]
    x_ref, dh_ref, vec_ref, out_ref = refs[GROUPS + 2 :]
    part = x_ref.shape[1] // GROUPS
    da = None
    for r, w in enumerate(w_refs):
        got = dot((one_ref, two_ref)[r // 2][r % 2], w[:, : 3 * part], 1, 1)
        da = got if da is None else da + got
    unit, inverse = normalize(x_ref[...].astype(F32))
    out_ref[...] = dh_ref[...] + normalize_back(da, unit, inverse, vec_ref[0:1])


def unproject(grads, weights, x, dh, vec):
    count, width = x.shape
    part = width // GROUPS
    rows = min(256, count)
    w = pl.BlockSpec((width, 640), lambda i: (0, 0), pipeline_mode=pl.Buffered(1))
    return call(
        unproject_kernel, "unproject", (count // rows,),
        [chunk((2, rows, 3 * part), 1)] * 2 + [w] * GROUPS
        + [chunk((rows, width)), chunk((rows, width)), full((8, width))],
        [(chunk((rows, width)), (count, width), F32)],
        cost=(6 * count * width * width, 20_000_000, 0),
    )(*grads, *weights, x, dh, vec)[0]


def add(a, b):
    return (a.astype(F32) + b.astype(F32)).astype(BF)


class Place:
    def __init__(self, mesh):
        self.n_dp = mesh.shape["dp"]
        self.n_e = mesh.shape["expert"]
        self.staged = self.n_dp == 4 and self.n_e == 8
        if not self.staged:
            return
        dev = lambda x, c, z, y: (x * 2 + c) * 8 + z * 2 + y
        every = [
            (x, c, z, y) for x in range(2) for c in range(2) for z in range(4) for y in range(2)
        ]
        to = lambda move: [(dev(*p), dev(*move(*p))) for p in every]
        self.core = to(lambda x, c, z, y: (x, 1 - c, z, y))
        self.x = to(lambda x, c, z, y: (1 - x, c, z, y))
        self.across = to(lambda x, c, z, y: (1 - x, 1 - c, z, y))
        self.y = to(lambda x, c, z, y: (x, c, z, 1 - y))
        self.z = [to(lambda x, c, z, y, k=k: (x, c, z ^ k, y)) for k in range(1, 4)]

    def tables(self):
        r = jnp.arange(4, dtype=jnp.int32)
        i = jnp.arange(8, dtype=jnp.int32)
        if not self.staged:
            return r, i, r
        d, e = lax.axis_index("dp"), lax.axis_index("expert")
        z, y = e // 2, e % 2
        weighed = d ^ jnp.where(r < 2, 3 - 2 * r, 6 - 2 * r)
        return d ^ r, (z ^ i % 4) * 2 + (y ^ i // 4), weighed

    def move(self, array, way):
        return lax.ppermute(array, BOTH, way)


def whole_of(have):
    n_dp, n_e = lax.axis_size("dp"), lax.axis_size("expert")
    rows, cols = have.shape[1:]
    have = have.reshape(n_dp, n_e, rows, cols).transpose(1, 2, 0, 3)
    return have.reshape(n_e * rows, n_dp * cols)


def gather_all(array):
    return whole_of(lax.all_gather(array, BOTH, axis=0, tiled=False))


def scatter_all(array):
    n_dp, n_e = lax.axis_size("dp"), lax.axis_size("expert")
    rows, cols = array.shape[0] // n_e, array.shape[1] // n_dp
    parts = array.reshape(n_e, rows, n_dp, cols).transpose(2, 0, 1, 3)
    parts = parts.reshape(n_dp * n_e, rows, cols)
    return lax.psum_scatter(parts, BOTH, scatter_dimension=0, tiled=False)


def fetch(place, table, weights, out_weights, vectors, filler):
    barrier = lax.optimization_barrier
    stacked = jnp.stack(vectors)
    pad = 64 - len(vectors)
    if place.staged:
        rows = out_weights.shape[0]
        extra = jnp.concatenate([stacked.T, jnp.zeros((rows, pad), BF)], axis=1)
        shard = jnp.concatenate([*weights, extra], axis=1)
        own = jnp.stack([shard] + [place.move(shard, way) for way in place.z])
        own, out_weights, filler = barrier((own, out_weights, filler))
        got = place.move(own, place.y)
        out_own = jnp.stack([out_weights] + [place.move(out_weights, way) for way in place.z])
        got, out_own = barrier((got, out_own))
        near = assemble(table, own, got)
        across = place.move(near, place.x)
        far = place.move(near, place.core)
        return (near, far, across), (out_own, place.move(out_own, place.y)), filler
    vecs = lax.all_gather(stacked, "expert", axis=1, tiled=True)
    width = vecs.shape[1]
    extra = jnp.concatenate([vecs, jnp.zeros((pad, width), BF)]).T
    extra = jnp.broadcast_to(extra[None], (GROUPS, width, 64))
    by_group = lambda w: gather_all(w).reshape(width, GROUPS, -1).transpose(1, 0, 2)
    grouped = jnp.concatenate([*(by_group(w) for w in weights), extra], axis=2)
    out = by_group(out_weights)
    return [grouped[i] for i in range(GROUPS)], [out[i] for i in range(GROUPS)], filler


def reduce_y(place, keep, send):
    got = place.move(send, place.y)
    return keep[0].astype(F32) + got[0].astype(F32), [add(keep[k], got[k]) for k in range(1, 4)]


def reduce_z(place, sends):
    return [place.move(part, way) for part, way in zip(sends, place.z)]


def columns_of(place, total, count):
    cols = (FAR - 640) // 2
    parts = [total[:, i * cols : (i + 1) * cols] for i in range(3)]
    vecs = total[:, 576 : 576 + 8].T
    vecs = vecs + sum(place.move(vecs, way) for way in (place.core, place.x, place.across))
    return parts, [vecs[i] for i in range(count)]


def reduce_plain(near, far, count):
    slabs = jnp.stack([a[:, :640] for a in (*near, *far)])
    width = slabs.shape[1]
    part = width // GROUPS
    whole = lambda array: array.transpose(1, 0, 2).reshape(width, width)
    parts = [whole(slabs[:, :, i * part : (i + 1) * part]) for i in range(3)]
    parts.append(whole(jnp.stack([far[0][:, -part:], far[1][:, -part:]] + [a[:, 640:-part] for a in far])))
    parts = [scatter_all(p).astype(F32) for p in parts]
    vecs = jnp.sum(slabs[:, :, 576 : 576 + count].astype(F32), axis=0).T
    vecs = lax.psum_scatter(vecs, "expert", scatter_dimension=1, tiled=True)
    vecs = lax.psum(vecs, "dp")
    return parts, [vecs[i] for i in range(count)]


def shards(
    place,
    block_entries,
    assignments,
    positions_within,
    specialist_quotas,
    standardize_one_scale,
    standardize_one_shift,
    asking_weights,
    asking_shift,
    lookup_weights,
    content_weights,
    content_shift,
    context_mixing_weights,
    context_mixing_shift,
    standardize_two_scale,
    standardize_two_shift,
    gating_prototypes,
    specialist_widen_weights,
    specialist_widen_shift,
    specialist_contract_weights,
    specialist_contract_shift,
    upstream_adjoint,
):
    count, width = block_entries.shape
    experts = specialist_quotas.shape[0]
    cap = count // experts
    n_dp = place.n_dp
    order, table, weighed = place.tables()
    barrier = lax.optimization_barrier

    chosen = assignments[:, None] == lax.broadcasted_iota(jnp.int32, (count, experts), 1)
    limit = jnp.sum(jnp.where(chosen, specialist_quotas[None, :], 0), axis=1)
    kept = positions_within < limit
    target = jnp.where(kept, assignments * cap + positions_within, count)
    late = positions_within >= cap // 2
    halved = jnp.where(late, positions_within + (count - cap) // 2, positions_within)
    halved = jnp.where(kept, assignments * (cap // 2) + halved, count)

    def exchange(rows):
        sent = rows.reshape(experts, -1, width)
        got = lax.all_to_all(sent, "expert", split_axis=0, concat_axis=0, tiled=True)
        return got.reshape(rows.shape)

    weights, out, sent_g = fetch(
        place,
        table,
        (asking_weights, lookup_weights, content_weights),
        context_mixing_weights,
        (
            standardize_one_scale,
            standardize_one_shift,
            asking_shift,
            content_shift,
            context_mixing_shift,
            standardize_two_scale,
            standardize_two_shift,
        ),
        dispatch(target, upstream_adjoint),
    )

    sent_g, first = barrier((sent_g, weights[1]))
    weights = (weights[0], first, *weights[2:])
    rows_g = exchange(sent_g).reshape(experts, 2, cap // 2, width)

    *before, low_in, vec = attend(0, order, weights[:2], x=block_entries)
    if place.staged:
        before, out = barrier((before, out))
        out_near = assemble(table, *out)
        before, across, out_near = barrier((before, weights[2], out_near))
        weights = (*weights[:2], across, place.move(across, place.core))
        out_across = place.move(out_near, place.x)
        out = (out_near, place.move(out_near, place.core))
    qkv, ctx, lse = attend(1, order, weights[2:], low=low_in, vec=vec, before=before)
    ctx, rows_g = barrier((ctx, rows_g))
    if place.staged:
        ctx, out_across = barrier((ctx, out_across))
        out += (out_across, place.move(out_across, place.core))
    h1, whole_o, low_mid, sent_one = mix(order, block_entries, ctx, out, vec, halved)

    sent_two = dispatch(halved, low_mid, count // 2)
    x_one, sent_two = barrier((exchange(sent_one), sent_two))
    x_two = exchange(sent_two)
    matrices = (
        specialist_widen_weights[0], specialist_widen_shift, specialist_contract_weights[0],
        specialist_contract_shift, gating_prototypes,
    )
    gy, dm_one, dy_one, hid_one, du_one, dbin_one, small_one = expert(
        0, x_one, rows_g, *matrices, None
    )
    x_two, dm_one = barrier((x_two, dm_one))
    dm_one = exchange(dm_one)
    gy, dm_two, dy_two, hid_two, du_two, dbin_two, small_two = expert(
        1, x_two, rows_g, *matrices, gy
    )
    dm_one, dm_two, hid_two = barrier((dm_one, dm_two, hid_two))
    dm_two = exchange(dm_two)
    sides = (
        (hid_one, hid_two), (du_one, du_two), (dy_one, dy_two), (x_one, x_two),
        (dbin_one, dbin_two), (small_one, small_two),
    )
    if place.staged:
        grads_far, grads = weigh(
            weighed, n_dp, True, *sides
        )
        grads_far, gy, dm_two = barrier((grads_far, gy, dm_two))
        came_far = place.move(grads_far, place.core)
        crossing = add(grads[0], came_far[0])
    else:
        grads = weigh(jnp.arange(n_dp, dtype=jnp.int32), n_dp, False, *sides)
        grads = lax.psum_scatter(grads, "dp", scatter_dimension=0, tiled=False)
    gy = exchange(gy.reshape(count, width))

    dh1, dctx, grad_o, two = unmix(
        order, h1, upstream_adjoint, dm_one, dm_two, halved, ctx, whole_o, vec
    )
    back = lambda half, dctx: attend_back(
        half, order, table, qkv, ctx, dctx, lse, low_in, grad_o, weights[2 * half : 2 * half + 2],
        two,
    )
    if place.staged:
        dctx, crossing = barrier((dctx, crossing))
        came = place.move(crossing, place.x)
        far, keep, send, more = back(1, dctx)
        more = place.move(more, place.core)
        far, gy = barrier((far, gy))
        output = finish(h1, target, gy)
        send = add(send, more[4:])
        dctx, output, send = barrier((dctx, output, send))
        across, sends = reduce_y(place, add(keep, more[:4]), send)
        near, keep, send, more = back(0, dctx)
        near, keep, send, more, across, sends = barrier((near, keep, send, more, across, sends))
        more = place.move(more, place.core)
        got = reduce_z(place, sends)
        send, keep = add(send, more[4:]), add(keep, more[:4])
        near, send, keep = barrier((near, send, keep))
        got_y = place.move(send, place.y)
        input_grad = unproject((near, far), weights, block_entries, dh1, vec)
        got_far = got
        got, input_grad, came = barrier((got_y, input_grad, came))
        total = keep[0].astype(F32) + got[0].astype(F32)
        got = reduce_z(place, [add(keep[k], got[k]) for k in range(1, 4)])
        got_far, came, input_grad = barrier((got_far, came, input_grad))
        sum_o = across + sum(g.astype(F32) for g in got_far)
        cols = width // GROUPS
        across = place.move(sum_o[:, :-cols].astype(BF), place.x)
        pick = lambda at: sum(
            a[at : at + width].astype(F32) for a in (grads[1], came_far[1], came)
        )
        got, grads, across = barrier((got, [pick(0), pick(width), pick(2 * width)], across))
        total += across[:, :640].astype(F32)
        sum_o = sum_o[:, -cols:] + across[:, 640:].astype(F32)
        total += sum(g.astype(F32) for g in got)
        (sum_q, sum_k, sum_v), small = columns_of(place, total, 7)
    else:
        parts = [back(half, dctx) for half in range(2)]
        slabs = [
            [jnp.concatenate(p[1:3]).reshape(width, -1), p[3].reshape(width, -1)]
            for p in parts
        ]
        (sum_q, sum_k, sum_v, sum_o), small = reduce_plain(*slabs, 7)
        input_grad = unproject([p[0] for p in parts], weights, block_entries, dh1, vec)
        output = finish(h1, target, gy)

        part = (grads.shape[0] - 16) // 2
        grads = [grads[:part], grads[part : 2 * part].T, grads[2 * part :]]
        grads = [g.astype(F32) for g in grads]

    grad_out, grad_in, rest = grads
    part = grad_out.shape[0]
    own = lax.axis_index("dp") * (width // n_dp)
    grad_bin = rest[0:1, :part]
    grad_bout = lax.dynamic_slice(rest[1:2], (0, own), (1, width // n_dp))
    grad_centers = rest[2:3]
    return (
        output,
        input_grad,
        small[0],
        small[1],
        sum_q,
        small[2],
        sum_k,
        sum_v,
        small[3],
        sum_o,
        small[4],
        small[5],
        small[6],
        grad_centers,
        grad_in[None],
        grad_bin,
        grad_out[None],
        grad_bout,
    )


def solution(mesh):
    placed = (
        P(("dp", "expert"), None),
        P(("dp", "expert")),
        P(("dp", "expert")),
        P(),
        P("expert"),
        P("expert"),
        P("expert", "dp"),
        P("expert"),
        P("expert", "dp"),
        P("expert", "dp"),
        P("expert"),
        P("expert", "dp"),
        P("expert"),
        P("expert"),
        P("expert"),
        P("expert", None),
        P("expert", None, None),
        P("expert", None),
        P("expert", None, None),
        P("expert", None),
        P(("dp", "expert"), None),
    )
    return jax.shard_map(
        partial(shards, Place(mesh)),
        mesh=mesh,
        in_specs=placed,
        out_specs=(
            P(("dp", "expert"), None),
            P(("dp", "expert"), None),
            P("expert"),
            P("expert"),
            P("expert", "dp"),
            P("expert"),
            P("expert", "dp"),
            P("expert", "dp"),
            P("expert"),
            P("expert", "dp"),
            P("expert"),
            P("expert"),
            P("expert"),
            P("expert", None),
            P("expert", None, "dp"),
            P("expert", "dp"),
            P("expert", "dp", None),
            P("expert", "dp"),
        ),
        check_vma=False,
    )
```

```python
from functools import partial

import jax
import jax.numpy as jnp
from jax import lax
from jax.experimental import pallas as pl
from jax.experimental.pallas import tpu as pltpu
from jax.sharding import PartitionSpec as P

HEADS = 12
HEAD_DIM = 64
SEQ_LEN = 1024
GROUPS = 4

EPSILON = 1e-05
MASKED = -1e30
FAR = 1024
BOTH = ("dp", "expert")
BF = jnp.bfloat16
F32 = jnp.float32


def dot(left, right, left_dim, right_dim):
    return lax.dot_general(
        left, right, (((left_dim,), (right_dim,)), ((), ())), preferred_element_type=F32
    )


def normalize(values):
    center = jnp.mean(values, axis=-1, keepdims=True)
    centered = values - center
    inverse = lax.rsqrt(jnp.mean(centered * centered, axis=-1, keepdims=True) + EPSILON)
    return (centered * inverse, inverse)


def normalize_back(grad, normed, inverse, gain):
    scaled = grad * gain
    return inverse * (
        scaled
        - jnp.mean(scaled, axis=-1, keepdims=True)
        - normed * jnp.mean(scaled * normed, axis=-1, keepdims=True)
    )


def call(
    kernel, name, grid, in_specs, outs, scratch=(), vmem=60, cost=(0, 0, 0), ahead=0, **more
):
    return pl.pallas_call(
        kernel,
        name=name,
        grid_spec=pltpu.PrefetchScalarGridSpec(
            num_scalar_prefetch=ahead,
            grid=grid,
            in_specs=in_specs,
            out_specs=[o[0] for o in outs],
            scratch_shapes=list(scratch),
        ),
        out_shape=[jax.ShapeDtypeStruct(o[1], o[2]) for o in outs],
        compiler_params=pltpu.CompilerParams(vmem_limit_bytes=vmem << 20),
        cost_estimate=pl.CostEstimate(
            flops=cost[0], bytes_accessed=cost[1], transcendentals=cost[2]
        ),
        **more,
    )


def full(shape):
    return pl.BlockSpec(
        shape, lambda *_: (0,) * len(shape), pipeline_mode=pl.Buffered(1)
    )


SCALARS = pl.BlockSpec(memory_space=pltpu.SMEM)
PLACED = pl.BlockSpec(memory_space=pl.ANY)


def assemble_kernel(table, own_ref, got_ref, out_ref, sems):
    rows = own_ref.shape[1]
    copies = []
    for i in range(8):
        src = (own_ref, got_ref)[i // 4].at[i % 4]
        at = pl.multiple_of(rows * table[i], 32)
        copies.append(pltpu.make_async_copy(src, out_ref.at[pl.ds(at, rows)], sems.at[i]))
    for c in copies:
        c.start()
    for c in copies:
        c.wait()


def assemble(table, own, got):
    rows, cols = own.shape[1:]
    return call(
        assemble_kernel, "assemble", (1,), [SCALARS, PLACED, PLACED],
        [(full((8 * rows, cols)), (8 * rows, cols), BF)],
        [pltpu.SemaphoreType.DMA((8,))],
        cost=(0, 4 * rows * cols * 8, 0),
    )(table, own, got)[0]


def chunk(shape, axis=0):
    return pl.BlockSpec(shape, lambda i: tuple(i if a == axis else 0 for a in range(len(shape))))


def attend_kernel(half, order, *refs):
    if half:
        low_ref, vec_ref, w_one, w_two = refs[:4]
        qkv_ref, ctx_ref, lse_ref = refs[7:]
    else:
        x_ref, w_one, w_two, qkv_ref, ctx_ref, lse_ref, low_ref, vec_ref = refs
    step = pl.program_id(0)
    count, width = low_ref.shape
    part = width // GROUPS
    if not half:

        @pl.when(step == 0)
        def _():
            vec_ref[...] = w_one[:, 512:640].astype(F32).T[64:72]
            for at in range(0, count, 256):
                unit, _ = normalize(x_ref[at : at + 256].astype(F32))
                low_ref[at : at + 256] = (unit * vec_ref[0:1] + vec_ref[1:2]).astype(BF)

    zero = jnp.zeros((1, part), F32)
    bias_q = bias_v = zero
    for n in range(GROUPS):
        here = order[2 * half + step] == n
        bias_q = jnp.where(here, vec_ref[2:3, part * n : part * n + part], bias_q)
        bias_v = jnp.where(here, vec_ref[3:4, part * n : part * n + part], bias_v)
    bias = jnp.concatenate([bias_q, zero, bias_v], axis=1)
    w = jnp.where(step == 0, w_one[...], w_two[...])[:, : 3 * part]
    for at in range(0, count, 512):
        qkv_ref[0, at : at + 512] = (dot(low_ref[at : at + 512], w, 1, 0) + bias).astype(BF)
    for base in range(0, count, SEQ_LEN):
        block = min(512, SEQ_LEN)
        for h in range(part // HEAD_DIM):
            at = h * HEAD_DIM
            v = qkv_ref[0, base : base + SEQ_LEN, 2 * part + at : 2 * part + at + HEAD_DIM].T
            for start in range(0, SEQ_LEN, block):
                stop = start + block
                q = qkv_ref[0, base + start : base + stop, at : at + HEAD_DIM] * BF(HEAD_DIM**-0.5)
                k = qkv_ref[0, base : base + stop, part + at : part + at + HEAD_DIM]
                row = lax.broadcasted_iota(jnp.int32, (stop, block), 0)
                col = lax.broadcasted_iota(jnp.int32, (stop, block), 1) + start
                scores = jnp.where(row <= col, dot(k, q, 1, 1), MASKED)
                top = jnp.max(scores, axis=0, keepdims=True)
                probs = jnp.exp(scores - top)
                total = jnp.sum(probs, axis=0, keepdims=True)
                out = dot(v[:, :stop], probs.astype(BF), 1, 0) / total
                ctx_ref[0, base + start : base + stop, at : at + HEAD_DIM] = out.T.astype(BF)
                lse_ref[0, h : h + 1, base + start : base + stop] = top + jnp.log(total)


def attend(half, order, weights, x=None, low=None, vec=None, before=()):
    count, width = (low if half else x).shape
    part = width // GROUPS
    at = lambda g: (2 * half + g, 0, 0)
    outs = [
        (pl.BlockSpec((1, count, 3 * part), at), (GROUPS, count, 3 * part), BF),
        (pl.BlockSpec((1, count, part), at), (GROUPS, count, part), BF),
        (pl.BlockSpec((1, 8, count), at), (GROUPS, 8, count), F32),
    ]
    w = [pl.BlockSpec((width, 640), lambda g: (0, 0), pipeline_mode=pl.Buffered(1))] * 2
    if half:
        ins, args = [full((count, width)), full((8, width))] + w + [PLACED] * 3, (low, vec)
    else:
        outs += [(full((count, width)), (count, width), BF), (full((8, width)), (8, width), F32)]
        ins, args = [full((count, width))] + w, (x,)
    return call(
        partial(attend_kernel, half), "attend", (2,), [SCALARS] + ins, outs,
        cost=(12_000_000_000, 8_000_000, 4_000_000),
        input_output_aliases={5 + i: i for i in range(len(before))},
    )(order, *args, *weights, *before)


def attend_back_kernel(half, order, table, *refs):
    qkv_ref, ctx_ref, dctx_ref, lse_ref, low_ref, w_one, w_two, two_ref = refs[:8]
    if half:
        o_refs, refs = refs[8:10], refs[2:]
    out_ref, *slabs, dq_ref, stage, sems = refs[8:]
    step = pl.program_id(0)
    count, width = low_ref.shape
    part = width // GROUPS
    inner = (ctx_ref[0].astype(F32) * dctx_ref[0].astype(F32)).T
    block = min(256, SEQ_LEN)
    for base in range(0, count, SEQ_LEN):
        last = base + SEQ_LEN
        for h in range(part // HEAD_DIM):
            at = h * HEAD_DIM
            q = qkv_ref[0, base:last, at : at + HEAD_DIM] * BF(HEAD_DIM**-0.5)
            do = dctx_ref[0, base:last, at : at + HEAD_DIM]
            turned = qkv_ref[0, base:last, part + at : part + at + HEAD_DIM].T
            row_dot = jnp.sum(inner[at : at + HEAD_DIM, base:last], axis=0, keepdims=True)
            for start in range(0, SEQ_LEN, block):
                stop = start + block
                rows = slice(base + start, base + stop)
                k = qkv_ref[0, rows, part + at : part + at + HEAD_DIM]
                v = qkv_ref[0, rows, 2 * part + at : 2 * part + at + HEAD_DIM]
                row = lax.broadcasted_iota(jnp.int32, (block, SEQ_LEN - start), 0)
                col = lax.broadcasted_iota(jnp.int32, (block, SEQ_LEN - start), 1)
                lse = lse_ref[0, h : h + 1, base + start : last]
                probs = jnp.where(row <= col, jnp.exp(dot(k, q[start:], 1, 1) - lse), 0.0)
                dscores = (probs * (dot(v, do[start:], 1, 1) - row_dot[:, start:])).astype(BF)
                dk = dot(dscores, q[start:], 1, 0)
                dv = dot(probs.astype(BF), do[start:], 1, 0)
                dq = dot(turned[:, start:stop], dscores, 1, 0)
                if start:
                    dq_ref[:, start:] += dq
                else:
                    dq_ref[...] = dq
                out_ref[0, rows, part + at : part + at + HEAD_DIM] = dk.astype(BF)
                out_ref[0, rows, 2 * part + at : 2 * part + at + HEAD_DIM] = dv.astype(BF)
            out_ref[0, base:last, at : at + HEAD_DIM] = (dq_ref[...].T * HEAD_DIM**-0.5).astype(BF)
    sums = jnp.sum(out_ref[0].astype(F32), axis=0, keepdims=True)
    grad = dot(low_ref[...], out_ref[0], 0, 0)
    w = jnp.where(step == 0, w_one[...], w_two[...]).astype(F32)
    shift = jnp.sum(w[:, : 3 * part] * sums, axis=-1, keepdims=True)
    gain = jnp.sum(w[:, : 3 * part] * grad, axis=-1, keepdims=True)
    gain = (gain - w[:, 577:578] * shift) / w[:, 576:577]
    row = lax.broadcasted_iota(jnp.int32, (width, part), 0) - order[2 * half + step] * part
    here = row == lax.broadcasted_iota(jnp.int32, (width, part), 1)
    columns = [gain, shift] + [
        jnp.sum(jnp.where(here, sums[:, at : at + part], 0.0), axis=-1, keepdims=True)
        for at in (0, 2 * part)
    ]
    lane = lax.broadcasted_iota(jnp.int32, (width, 64), 1)
    vecs = jnp.zeros((width, 64), F32)
    if not half:
        more = jnp.concatenate([two_ref[...], jnp.zeros((120, width), F32)]).T[:, :64]
        vecs = jnp.where(step == 0, more, vecs)
    for i, column in enumerate(columns):
        vecs = jnp.where(lane == i, column, vecs)
    stage[:, : 3 * part] = grad.astype(BF)
    stage[:, 3 * part : 640] = vecs.astype(BF)
    if half:
        stage[:, 640:] = jnp.concatenate([o_refs[0][0], o_refs[1][0]], axis=1)
    rows = width // 8
    for g in range(2):

        @pl.when(step == g)
        def _(g=g):
            copies = []
            for i in range(8):
                src = stage.at[pl.ds(pl.multiple_of(rows * table[i], 32), rows)]
                dst = slabs[2].at[i] if g else slabs[i // 4].at[i % 4]
                copies.append(pltpu.make_async_copy(src, dst, sems.at[i]))
            for c in copies:
                c.start()
            for c in copies:
                c.wait()


def attend_back(half, order, table, qkv, ctx, dctx, lse, low, o_part, weights, two):
    groups, count, part = qkv.shape
    part //= 3
    width = low.shape[1]
    at = lambda g, *_: (2 * half + g, 0, 0)
    cols = FAR if half else 640
    slabs = [(PLACED, (n, width // 8, cols), BF) for n in (4, 4, 8)]
    o_specs = [
        pl.BlockSpec((1, width, part), lambda g, order, table, b=b: (order[b + g], 0, 0))
        for b in ((2, 0) if half else ())
    ]
    return call(
        partial(attend_back_kernel, half), "attend_back", (2,),
        [
            pl.BlockSpec((1, count, 3 * part), at),
            pl.BlockSpec((1, count, part), at),
            pl.BlockSpec((1, count, part), at),
            pl.BlockSpec((1, 8, count), at),
            full((count, width)),
        ]
        + [pl.BlockSpec((width, 640), lambda *_: (0, 0), pipeline_mode=pl.Buffered(1))] * 2
        + [full((8, width))] + o_specs,
        [(pl.BlockSpec((1, count, 3 * part), lambda g, *_: (g, 0, 0)), (2, count, 3 * part), BF)]
        + slabs,
        [
            pltpu.VMEM((HEAD_DIM, SEQ_LEN), F32),
            pltpu.VMEM((width, cols), BF),
            pltpu.SemaphoreType.DMA((8,)),
        ],
        cost=(24_000_000_000, 14_000_000, 4_000_000), ahead=2,
    )(order, table, qkv, ctx, dctx, lse, low, *weights, two, *[o_part] * len(o_specs))


def dispatch_kernel(first, target_ref, rows_ref, out_ref):
    count = rows_ref.shape[0]
    for at in range(0, out_ref.shape[0], 256):
        slot = lax.broadcasted_iota(jnp.int32, (256, count), 0) + (first + at)
        picks = (target_ref[...] == slot).astype(F32).astype(BF)
        out_ref[at : at + 256] = dot(picks, rows_ref[...], 1, 0).astype(BF)


def dispatch(target, rows, first=0):
    count, width = rows.shape
    slots = count - first
    return call(
        partial(dispatch_kernel, first), "dispatch", (1,),
        [full((1, count)), full((count, width))],
        [(full((slots, width)), (slots, width), BF)],
        cost=(2 * count * count * width, 3_000_000, 0),
    )(target.reshape(1, count), rows)[0]


def column(row_ref):
    row = row_ref[...].astype(F32)
    return jnp.broadcast_to(row, (8, row.shape[1])).T[:, :1].astype(jnp.int32)


def mix_kernel(order, slab, x_ref, ctx_ref, vec_ref, target_ref, *refs):
    wo_refs, (h_ref, whole_ref, low_ref, sent_ref) = refs[:GROUPS], refs[GROUPS:]
    rows, width = x_ref.shape
    count = low_ref.shape[0]
    part = width // GROUPS
    step = pl.program_id(0)

    @pl.when(step == 0)
    def _():
        for q in range(GROUPS):
            first, second = slab[2 * order[q]], slab[2 * order[q] + 1]
            pieces = [jnp.concatenate([wo[first], wo[second]]) for wo in wo_refs]
            for n in range(GROUPS):
                piece = pieces[0]
                for r in range(1, GROUPS):
                    piece = jnp.where(order[r] == n, pieces[r], piece)
                whole_ref[q * part : q * part + part, n * part : n * part + part] = piece

    h = x_ref[...].astype(F32) + vec_ref[4:5]
    for r in range(GROUPS):
        h += dot(ctx_ref[r], whole_ref[r * part : r * part + part], 1, 0)
    h_ref[...] = h
    unit, _ = normalize(h)
    low_ref[pl.ds(pl.multiple_of(step * rows, 256), rows)] = (
        unit * vec_ref[5:6] + vec_ref[6:7]
    ).astype(BF)

    @pl.when(step == pl.num_programs(0) - 1)
    def _():
        for at in range(0, count // 2, 256):
            index = lax.broadcasted_iota(jnp.int32, (256, count), 0) + at
            picks = (target_ref[...] == index).astype(F32).astype(BF)
            sent_ref[at : at + 256] = dot(picks, low_ref[...], 1, 0).astype(BF)


def mix(order, slab, x, ctx, weights, vec, target):
    count, width = x.shape
    part = width // GROUPS
    rows = min(256, count)
    return call(
        mix_kernel, "mix", (count // rows,),
        [SCALARS, SCALARS, chunk((rows, width)), chunk((GROUPS, rows, part), 1), full((8, width)),
         full((1, count))] + [full((8, width // 8, part))] * GROUPS,
        [
            (chunk((rows, width)), (count, width), F32),
            (full((width, width)), (width, width), BF),
            (full((count, width)), (count, width), BF),
            (full((count // 2, width)), (count // 2, width), BF),
        ],
        cost=(2 * count * width * (width + count), 12_000_000, 0),
    )(order, slab, x, ctx, vec, target.reshape(1, count), *weights)


def unmix_kernel(
    order, h_ref, g_ref, dm_one, dm_two, target_ref, ctx_ref, whole_ref, vec_ref,
    dh_ref, dctx_ref, grad_ref, sum_ref, total_ref,
):
    rows, width = h_ref.shape
    part = width // GROUPS
    step = pl.program_id(0)
    dm = None
    target = column(target_ref)
    for half, sent in enumerate((dm_one, dm_two)):
        index = lax.broadcasted_iota(jnp.int32, (rows, sent.shape[0]), 1) + half * sent.shape[0]
        picks = (target == index).astype(F32).astype(BF)
        got = dot(picks, sent[...], 1, 0)
        dm = got if dm is None else dm + got
    unit, inverse = normalize(h_ref[...])
    dh = g_ref[...].astype(F32) + normalize_back(dm, unit, inverse, vec_ref[5:6])
    dh_ref[...] = dh
    low = dh.astype(BF)
    sums = [
        jnp.sum(term, axis=0, keepdims=True) for term in (low.astype(F32), dm * unit, dm)
    ]
    zeros = jnp.zeros((1, width), F32)
    sums = jnp.concatenate([zeros] * 4 + sums + [zeros])
    for r in range(GROUPS):
        dctx_ref[r] = dot(low, whole_ref[r * part : r * part + part], 1, 1).astype(BF)
    grads = [dot(ctx_ref[q], low, 0, 0) for q in range(GROUPS)]

    @pl.when(step == 0)
    def _():
        sum_ref[...] = sums
        for q in range(GROUPS):
            total_ref[q] = grads[q]

    @pl.when(step > 0)
    def _():
        sum_ref[...] += sums
        for q in range(GROUPS):
            total_ref[q] += grads[q]

    @pl.when(step == pl.num_programs(0) - 1)
    def _():
        for q in range(GROUPS):
            grad = total_ref[q].astype(BF)
            at = pl.ds(pl.multiple_of(order[q] * part, 64), part)
            for n in range(GROUPS):
                grad_ref[n, at, :] = grad[:, n * part : n * part + part]


def unmix(order, h, g, dm_one, dm_two, target, ctx, whole, vec):
    count, width = h.shape
    part = width // GROUPS
    rows = min(256, count)
    half = full((count // 2, width))
    by_rows, by_ctx = chunk((rows, width)), chunk((GROUPS, rows, part), 1)
    return call(
        unmix_kernel, "unmix", (count // rows,),
        [SCALARS, by_rows, by_rows, half, half, chunk((1, rows), 1), by_ctx, full((width, width)),
         full((8, width))],
        [
            (by_rows, (count, width), F32),
            (by_ctx, (GROUPS, count, part), BF),
            (full((GROUPS, width, part)), (GROUPS, width, part), BF),
            (full((8, width)), (8, width), F32),
        ],
        [pltpu.VMEM((GROUPS, part, width), F32)],
        cost=(2 * count * width * (2 * width + count), 20_000_000, 0),
    )(order, h, g, dm_one, dm_two, target.reshape(1, count), ctx, whole, vec)


def finish_kernel(h_ref, target_ref, gy_ref, out_ref):
    slot = lax.broadcasted_iota(jnp.int32, (h_ref.shape[0], gy_ref.shape[0]), 1)
    picks = (column(target_ref) == slot).astype(F32).astype(BF)
    out_ref[...] = (h_ref[...] + dot(picks, gy_ref[...], 1, 0)).astype(BF)


def finish(h, target, gy):
    count, width = h.shape
    rows = min(256, count)
    return call(
        finish_kernel, "finish", (count // rows,),
        [chunk((rows, width)), chunk((1, rows), 1), full((count, width))],
        [(chunk((rows, width)), (count, width), BF)],
        cost=(2 * count * count * width, 6_000_000, 0),
    )(h, target.reshape(1, count), gy)[0]


def gelu_pair(v):
    cdf = 0.5 + 0.5 * lax.erf(v * 0.5**0.5)
    return v * cdf, cdf + v * jnp.exp(-0.5 * v * v) * (0.5 / jnp.pi) ** 0.5


def expert_kernel(
    x_ref, g_ref, win_ref, bin_ref, wout_ref, bout_ref, center_ref, _,
    gy_ref, dm_ref, dy_ref, hid_ref, du_ref, dbin_ref, small_ref,
    y_acc, dm_acc, gate_ref, gates,
):
    step = pl.program_id(0)
    rows, width = x_ref.shape

    @pl.when(step == 0)
    def _():
        z = jnp.sum(x_ref[...].astype(F32) * center_ref[...].astype(F32), axis=-1, keepdims=True)
        gate = 1.0 / (1.0 + jnp.exp(-z))
        gate_ref[...] = jnp.broadcast_to(gate, gate_ref.shape)
        dy_ref[...] = (gate * g_ref[...].reshape(rows, width).astype(F32)).astype(BF)

    act, slope = gelu_pair(dot(x_ref[...], win_ref[...], 1, 0) + bin_ref[...].astype(F32))
    hid = act.astype(BF)
    hid_ref[...] = hid
    y = dot(hid, wout_ref[...], 1, 0)
    du = (dot(dy_ref[...], wout_ref[...], 1, 1) * slope).astype(BF)
    du_ref[...] = du
    dbin_ref[...] = jnp.broadcast_to(
        jnp.sum(du.astype(F32), axis=0, keepdims=True), dbin_ref.shape
    )
    dm = dot(du, win_ref[...], 1, 1)

    @pl.when(step == 0)
    def _():
        y_acc[...] = y
        dm_acc[...] = dm

    @pl.when(step > 0)
    def _():
        y_acc[...] += y
        dm_acc[...] += dm

    @pl.when(step == pl.num_programs(0) - 1)
    def _():
        gate = gate_ref[:, :1]
        g = g_ref[...].reshape(rows, width).astype(F32)
        y = (y_acc[...] + bout_ref[...].astype(F32)).astype(BF).astype(F32)
        gy_ref[...] = (gate * y).astype(BF).reshape(gy_ref.shape)
        dz = gate * (1.0 - gate) * jnp.sum(g * y, axis=-1, keepdims=True)
        dm_ref[...] = (dm_acc[...] + dz * center_ref[...].astype(F32)).astype(BF)
        small_ref[0:1, :] = jnp.sum(dy_ref[...].astype(F32), axis=0, keepdims=True)
        small_ref[1:2, :] = jnp.sum(dz * x_ref[...].astype(F32), axis=0, keepdims=True)


def expert(half, x, g, win, bias_in, wout, bias_out, center, gy):
    rows, width = x.shape
    ff = win.shape[1]
    step = min(1024, ff)
    along = lambda i: (0, i)
    side = pl.BlockSpec(
        (g.shape[0], 1) + g.shape[2:], lambda i: (0, half, 0, 0), pipeline_mode=pl.Buffered(1)
    )
    return call(
        expert_kernel, "expert", (ff // step,),
        [
            full((rows, width)),
            side,
            pl.BlockSpec((width, step), along),
            pl.BlockSpec((1, step), along),
            pl.BlockSpec((step, width), lambda i: (i, 0)),
            full((1, width)),
            full((1, width)),
            PLACED,
        ],
        [
            (side, g.shape, BF),
            (full((rows, width)), (rows, width), BF),
            (full((rows, width)), (rows, width), BF),
            (pl.BlockSpec((rows, step), along), (rows, ff), BF),
            (pl.BlockSpec((rows, step), along), (rows, ff), BF),
            (pl.BlockSpec((8, step), along), (8, ff), F32),
            (full((8, width)), (8, width), F32),
        ],
        [
            pltpu.VMEM((rows, width), F32),
            pltpu.VMEM((rows, width), F32),
            pltpu.VMEM((rows, 128), F32),
            pltpu.SMEM((1,), jnp.int32),
        ],
        cost=(8 * rows * width * ff, 22_000_000, 2 * rows * ff),
        input_output_aliases={} if gy is None else {7: 0},
    )(x, g, win, bias_in, wout, bias_out, center, x if gy is None else gy)


def weigh_kernel(split, which, *refs):
    hid, du, dy, x, bias, small = (refs[i : i + 2] for i in range(0, 12, 2))
    ff = hid[0].shape[1]
    width = dy[0].shape[1]
    step = pl.program_id(0)
    small = small[0][...] + small[1][...]
    row = lax.broadcasted_iota(jnp.int32, (16, width), 0)
    bias = (bias[0][...] + bias[1][...])[0:1]
    if ff < width:
        bias = jnp.concatenate([bias, jnp.zeros((1, width - ff), F32)], axis=1)
    rest = jnp.where(row == 0, bias, 0.0)
    rest = jnp.where(row == 1, small[0:1], rest)
    rest = jnp.where(row == 2, small[1:2], rest)

    def pair(i):
        rows, cols = (x, du) if split else (du, x)
        return rows[i][...], cols[i][...]

    def put(out):
        out[:ff] = (dot(hid[0][...], dy[0][...], 0, 0) + dot(hid[1][...], dy[1][...], 0, 0)).astype(BF)
        out[ff : 2 * ff] = (
            dot(*pair(0), 0, 0) + dot(*pair(1), 0, 0)
        ).astype(BF)
        out[2 * ff :] = rest.astype(BF)

    if not split:
        put(refs[12].at[0])
        return
    for late, out in enumerate(refs[12:]):

        @pl.when(step // 2 == late)
        def _(out=out):
            put(out.at[0])


def weigh(which, n, split, hid, du, dy, x, bias, small):
    rows, ff = hid[0].shape
    width = dy[0].shape[1]
    part = ff // n
    size = 2 * part + 16
    along = lambda i, which: (0, which[i])
    wide = pl.BlockSpec((rows, part), along)
    if split:
        first = pl.BlockSpec((1, size, width), lambda i, which: (jnp.minimum(i, 1), 0, 0))
        last = pl.BlockSpec((1, size, width), lambda i, which: (jnp.maximum(i - 2, 0), 0, 0))
        outs = [(first, (2, size, width), BF), (last, (2, size, width), BF)]
    else:
        outs = [(pl.BlockSpec((1, size, width), lambda i, which: (i, 0, 0)), (n, size, width), BF)]
    got = call(
        partial(weigh_kernel, split), "weigh", (n,),
        [wide] * 4 + [full((rows, width))] * 4 + [pl.BlockSpec((8, part), along)] * 2
        + [full((8, width))] * 2,
        outs, cost=(8 * rows * width * ff, 26_000_000, 0), ahead=1,
    )(which, *hid, *du, *dy, *x, *bias, *small)
    return got if split else got[0]


def unproject_kernel(*refs):
    one_ref, two_ref, *w_refs = refs[: GROUPS + 2]
    x_ref, dh_ref, vec_ref, out_ref = refs[GROUPS + 2 :]
    part = x_ref.shape[1] // GROUPS
    da = None
    for r, w in enumerate(w_refs):
        got = dot((one_ref, two_ref)[r // 2][r % 2], w[:, : 3 * part], 1, 1)
        da = got if da is None else da + got
    unit, inverse = normalize(x_ref[...].astype(F32))
    out_ref[...] = dh_ref[...] + normalize_back(da, unit, inverse, vec_ref[0:1])


def unproject(grads, weights, x, dh, vec):
    count, width = x.shape
    part = width // GROUPS
    rows = min(256, count)
    w = pl.BlockSpec((width, 640), lambda i: (0, 0), pipeline_mode=pl.Buffered(1))
    return call(
        unproject_kernel, "unproject", (count // rows,),
        [chunk((2, rows, 3 * part), 1)] * 2 + [w] * GROUPS
        + [chunk((rows, width)), chunk((rows, width)), full((8, width))],
        [(chunk((rows, width)), (count, width), F32)],
        cost=(6 * count * width * width, 20_000_000, 0),
    )(*grads, *weights, x, dh, vec)[0]


def add(a, b):
    return (a.astype(F32) + b.astype(F32)).astype(BF)


class Place:
    def __init__(self, mesh):
        self.n_dp = mesh.shape["dp"]
        self.n_e = mesh.shape["expert"]
        self.staged = self.n_dp == 4 and self.n_e == 8
        if not self.staged:
            return
        dev = lambda x, c, z, y: (x * 2 + c) * 8 + z * 2 + y
        every = [
            (x, c, z, y) for x in range(2) for c in range(2) for z in range(4) for y in range(2)
        ]
        to = lambda move: [(dev(*p), dev(*move(*p))) for p in every]
        self.core = to(lambda x, c, z, y: (x, 1 - c, z, y))
        self.x = to(lambda x, c, z, y: (1 - x, c, z, y))
        self.across = to(lambda x, c, z, y: (1 - x, 1 - c, z, y))
        self.y = to(lambda x, c, z, y: (x, c, z, 1 - y))
        self.z = [to(lambda x, c, z, y, k=k: (x, c, z ^ k, y)) for k in range(1, 4)]

    def tables(self):
        r = jnp.arange(4, dtype=jnp.int32)
        i = jnp.arange(8, dtype=jnp.int32)
        if not self.staged:
            return r, i, r, i
        d, e = lax.axis_index("dp"), lax.axis_index("expert")
        z, y = e // 2, e % 2
        weighed = d ^ jnp.where(r < 2, 3 - 2 * r, 6 - 2 * r)
        return d ^ r, (z ^ i % 4) * 2 + (y ^ i // 4), weighed, (y ^ i % 2) * 4 + (z ^ i // 2)

    def move(self, array, way):
        return lax.ppermute(array, BOTH, way)


def whole_of(have):
    n_dp, n_e = lax.axis_size("dp"), lax.axis_size("expert")
    rows, cols = have.shape[1:]
    have = have.reshape(n_dp, n_e, rows, cols).transpose(1, 2, 0, 3)
    return have.reshape(n_e * rows, n_dp * cols)


def gather_all(array):
    return whole_of(lax.all_gather(array, BOTH, axis=0, tiled=False))


def scatter_all(array):
    n_dp, n_e = lax.axis_size("dp"), lax.axis_size("expert")
    rows, cols = array.shape[0] // n_e, array.shape[1] // n_dp
    parts = array.reshape(n_e, rows, n_dp, cols).transpose(2, 0, 1, 3)
    parts = parts.reshape(n_dp * n_e, rows, cols)
    return lax.psum_scatter(parts, BOTH, scatter_dimension=0, tiled=False)


def fetch(place, table, weights, out_weights, vectors, filler):
    barrier = lax.optimization_barrier
    stacked = jnp.stack(vectors)
    pad = 64 - len(vectors)
    if place.staged:
        rows = out_weights.shape[0]
        extra = jnp.concatenate([stacked.T, jnp.zeros((rows, pad), BF)], axis=1)
        shard = jnp.concatenate([*weights, extra], axis=1)
        own = jnp.stack([shard] + [place.move(shard, way) for way in place.z])
        own, out_weights, filler = barrier((own, out_weights, filler))
        got = place.move(own, place.y)
        out_own = jnp.stack([out_weights] + [place.move(out_weights, way) for way in place.z])
        got, out_own = barrier((got, out_own))
        near = assemble(table, own, got)
        across = place.move(near, place.x)
        far = place.move(near, place.core)
        return (near, far, across), (out_own, place.move(out_own, place.y)), filler
    vecs = lax.all_gather(stacked, "expert", axis=1, tiled=True)
    width = vecs.shape[1]
    extra = jnp.concatenate([vecs, jnp.zeros((pad, width), BF)]).T
    extra = jnp.broadcast_to(extra[None], (GROUPS, width, 64))
    by_group = lambda w: gather_all(w).reshape(width, GROUPS, -1).transpose(1, 0, 2)
    grouped = jnp.concatenate([*(by_group(w) for w in weights), extra], axis=2)
    out = by_group(out_weights)
    out = out.reshape(GROUPS, 8, width // 8, -1)
    return [grouped[i] for i in range(GROUPS)], [out[i] for i in range(GROUPS)], filler


def reduce_y(place, keep, send):
    got = place.move(send, place.y)
    return keep[0].astype(F32) + got[0].astype(F32), [add(keep[k], got[k]) for k in range(1, 4)]


def reduce_z(place, sends):
    return [place.move(part, way) for part, way in zip(sends, place.z)]


def columns_of(place, total, count):
    cols = (FAR - 640) // 2
    parts = [total[:, i * cols : (i + 1) * cols] for i in range(3)]
    vecs = total[:, 576 : 576 + 8].T
    vecs = vecs + sum(place.move(vecs, way) for way in (place.core, place.x, place.across))
    return parts, [vecs[i] for i in range(count)]


def reduce_plain(near, far, count):
    slabs = jnp.stack([a[:, :640] for a in (*near, *far)])
    width = slabs.shape[1]
    part = width // GROUPS
    whole = lambda array: array.transpose(1, 0, 2).reshape(width, width)
    parts = [whole(slabs[:, :, i * part : (i + 1) * part]) for i in range(3)]
    parts.append(whole(jnp.stack([far[0][:, -part:], far[1][:, -part:]] + [a[:, 640:-part] for a in far])))
    parts = [scatter_all(p).astype(F32) for p in parts]
    vecs = jnp.sum(slabs[:, :, 576 : 576 + count].astype(F32), axis=0).T
    vecs = lax.psum_scatter(vecs, "expert", scatter_dimension=1, tiled=True)
    vecs = lax.psum(vecs, "dp")
    return parts, [vecs[i] for i in range(count)]


def shards(
    place,
    block_entries,
    assignments,
    positions_within,
    specialist_quotas,
    standardize_one_scale,
    standardize_one_shift,
    asking_weights,
    asking_shift,
    lookup_weights,
    content_weights,
    content_shift,
    context_mixing_weights,
    context_mixing_shift,
    standardize_two_scale,
    standardize_two_shift,
    gating_prototypes,
    specialist_widen_weights,
    specialist_widen_shift,
    specialist_contract_weights,
    specialist_contract_shift,
    upstream_adjoint,
):
    count, width = block_entries.shape
    experts = specialist_quotas.shape[0]
    cap = count // experts
    n_dp = place.n_dp
    order, table, weighed, place_of = place.tables()
    barrier = lax.optimization_barrier

    chosen = assignments[:, None] == lax.broadcasted_iota(jnp.int32, (count, experts), 1)
    limit = jnp.sum(jnp.where(chosen, specialist_quotas[None, :], 0), axis=1)
    kept = positions_within < limit
    target = jnp.where(kept, assignments * cap + positions_within, count)
    late = positions_within >= cap // 2
    halved = jnp.where(late, positions_within + (count - cap) // 2, positions_within)
    halved = jnp.where(kept, assignments * (cap // 2) + halved, count)

    def exchange(rows):
        sent = rows.reshape(experts, -1, width)
        got = lax.all_to_all(sent, "expert", split_axis=0, concat_axis=0, tiled=True)
        return got.reshape(rows.shape)

    weights, out, sent_g = fetch(
        place,
        table,
        (asking_weights, lookup_weights, content_weights),
        context_mixing_weights,
        (
            standardize_one_scale,
            standardize_one_shift,
            asking_shift,
            content_shift,
            context_mixing_shift,
            standardize_two_scale,
            standardize_two_shift,
        ),
        dispatch(target, upstream_adjoint),
    )

    sent_g, first = barrier((sent_g, weights[1]))
    weights = (weights[0], first, *weights[2:])
    rows_g = exchange(sent_g).reshape(experts, 2, cap // 2, width)

    *before, low_in, vec = attend(0, order, weights[:2], x=block_entries)
    if place.staged:
        before, out = barrier((before, out))
        out_near = jnp.concatenate(out)
        before, across, out_near = barrier((before, weights[2], out_near))
        weights = (*weights[:2], across, place.move(across, place.core))
        out_across = place.move(out_near, place.x)
        out = (out_near, place.move(out_near, place.core))
    qkv, ctx, lse = attend(1, order, weights[2:], low=low_in, vec=vec, before=before)
    ctx, rows_g = barrier((ctx, rows_g))
    if place.staged:
        ctx, out_across = barrier((ctx, out_across))
        out += (out_across, place.move(out_across, place.core))
    h1, whole_o, low_mid, sent_one = mix(order, place_of, block_entries, ctx, out, vec, halved)

    sent_two = dispatch(halved, low_mid, count // 2)
    x_one, sent_two = barrier((exchange(sent_one), sent_two))
    x_two = exchange(sent_two)
    matrices = (
        specialist_widen_weights[0], specialist_widen_shift, specialist_contract_weights[0],
        specialist_contract_shift, gating_prototypes,
    )
    gy, dm_one, dy_one, hid_one, du_one, dbin_one, small_one = expert(
        0, x_one, rows_g, *matrices, None
    )
    x_two, dm_one = barrier((x_two, dm_one))
    dm_one = exchange(dm_one)
    gy, dm_two, dy_two, hid_two, du_two, dbin_two, small_two = expert(
        1, x_two, rows_g, *matrices, gy
    )
    dm_one, dm_two, hid_two = barrier((dm_one, dm_two, hid_two))
    dm_two = exchange(dm_two)
    sides = (
        (hid_one, hid_two), (du_one, du_two), (dy_one, dy_two), (x_one, x_two),
        (dbin_one, dbin_two), (small_one, small_two),
    )
    if place.staged:
        grads_far, grads = weigh(
            weighed, n_dp, True, *sides
        )
        grads_far, gy, dm_two = barrier((grads_far, gy, dm_two))
        came_far = place.move(grads_far, place.core)
        crossing = add(grads[0], came_far[0])
    else:
        grads = weigh(jnp.arange(n_dp, dtype=jnp.int32), n_dp, False, *sides)
        grads = lax.psum_scatter(grads, "dp", scatter_dimension=0, tiled=False)
    gy = exchange(gy.reshape(count, width))

    dh1, dctx, grad_o, two = unmix(
        order, h1, upstream_adjoint, dm_one, dm_two, halved, ctx, whole_o, vec
    )
    back = lambda half, dctx: attend_back(
        half, order, table, qkv, ctx, dctx, lse, low_in, grad_o, weights[2 * half : 2 * half + 2],
        two,
    )
    if place.staged:
        dctx, crossing = barrier((dctx, crossing))
        came = place.move(crossing, place.x)
        far, keep, send, more = back(1, dctx)
        more = place.move(more, place.core)
        far, gy = barrier((far, gy))
        output = finish(h1, target, gy)
        send = add(send, more[4:])
        dctx, output, send = barrier((dctx, output, send))
        across, sends = reduce_y(place, add(keep, more[:4]), send)
        near, keep, send, more = back(0, dctx)
        near, keep, send, more, across, sends = barrier((near, keep, send, more, across, sends))
        more = place.move(more, place.core)
        got = reduce_z(place, sends)
        send, keep = add(send, more[4:]), add(keep, more[:4])
        near, send, keep = barrier((near, send, keep))
        got_y = place.move(send, place.y)
        input_grad = unproject((near, far), weights, block_entries, dh1, vec)
        got_far = got
        got, input_grad, came = barrier((got_y, input_grad, came))
        total = keep[0].astype(F32) + got[0].astype(F32)
        got = reduce_z(place, [add(keep[k], got[k]) for k in range(1, 4)])
        got_far, came, input_grad = barrier((got_far, came, input_grad))
        sum_o = across + sum(g.astype(F32) for g in got_far)
        cols = width // GROUPS
        across = place.move(sum_o[:, :-cols].astype(BF), place.x)
        pick = lambda at: sum(
            a[at : at + width].astype(F32) for a in (grads[1], came_far[1], came)
        )
        got, grads, across = barrier((got, [pick(0), pick(width), pick(2 * width)], across))
        total += across[:, :640].astype(F32)
        sum_o = sum_o[:, -cols:] + across[:, 640:].astype(F32)
        total += sum(g.astype(F32) for g in got)
        (sum_q, sum_k, sum_v), small = columns_of(place, total, 7)
    else:
        parts = [back(half, dctx) for half in range(2)]
        slabs = [
            [jnp.concatenate(p[1:3]).reshape(width, -1), p[3].reshape(width, -1)]
            for p in parts
        ]
        (sum_q, sum_k, sum_v, sum_o), small = reduce_plain(*slabs, 7)
        input_grad = unproject([p[0] for p in parts], weights, block_entries, dh1, vec)
        output = finish(h1, target, gy)

        part = (grads.shape[0] - 16) // 2
        grads = [grads[:part], grads[part : 2 * part].T, grads[2 * part :]]
        grads = [g.astype(F32) for g in grads]

    grad_out, grad_in, rest = grads
    part = grad_out.shape[0]
    own = lax.axis_index("dp") * (width // n_dp)
    grad_bin = rest[0:1, :part]
    grad_bout = lax.dynamic_slice(rest[1:2], (0, own), (1, width // n_dp))
    grad_centers = rest[2:3]
    return (
        output,
        input_grad,
        small[0],
        small[1],
        sum_q,
        small[2],
        sum_k,
        sum_v,
        small[3],
        sum_o,
        small[4],
        small[5],
        small[6],
        grad_centers,
        grad_in[None],
        grad_bin,
        grad_out[None],
        grad_bout,
    )


def solution(mesh):
    placed = (
        P(("dp", "expert"), None),
        P(("dp", "expert")),
        P(("dp", "expert")),
        P(),
        P("expert"),
        P("expert"),
        P("expert", "dp"),
        P("expert"),
        P("expert", "dp"),
        P("expert", "dp"),
        P("expert"),
        P("expert", "dp"),
        P("expert"),
        P("expert"),
        P("expert"),
        P("expert", None),
        P("expert", None, None),
        P("expert", None),
        P("expert", None, None),
        P("expert", None),
        P(("dp", "expert"), None),
    )
    return jax.shard_map(
        partial(shards, Place(mesh)),
        mesh=mesh,
        in_specs=placed,
        out_specs=(
            P(("dp", "expert"), None),
            P(("dp", "expert"), None),
            P("expert"),
            P("expert"),
            P("expert", "dp"),
            P("expert"),
            P("expert", "dp"),
            P("expert", "dp"),
            P("expert"),
            P("expert", "dp"),
            P("expert"),
            P("expert"),
            P("expert"),
            P("expert", None),
            P("expert", None, "dp"),
            P("expert", "dp"),
            P("expert", "dp", None),
            P("expert", "dp"),
        ),
        check_vma=False,
    )
```

```python
from functools import partial

import jax
import jax.numpy as jnp
from jax import lax
from jax.experimental import pallas as pl
from jax.experimental.pallas import tpu as pltpu
from jax.sharding import PartitionSpec as P

HEADS = 12
HEAD_DIM = 64
SEQ_LEN = 1024
GROUPS = 4

EPSILON = 1e-05
MASKED = -1e30
FAR = 1024
BOTH = ("dp", "expert")
BF = jnp.bfloat16
F32 = jnp.float32


def dot(left, right, left_dim, right_dim):
    return lax.dot_general(
        left, right, (((left_dim,), (right_dim,)), ((), ())), preferred_element_type=F32
    )


def normalize(values):
    center = jnp.mean(values, axis=-1, keepdims=True)
    centered = values - center
    inverse = lax.rsqrt(jnp.mean(centered * centered, axis=-1, keepdims=True) + EPSILON)
    return (centered * inverse, inverse)


def normalize_back(grad, normed, inverse, gain):
    scaled = grad * gain
    return inverse * (
        scaled
        - jnp.mean(scaled, axis=-1, keepdims=True)
        - normed * jnp.mean(scaled * normed, axis=-1, keepdims=True)
    )


def call(
    kernel, name, grid, in_specs, outs, scratch=(), vmem=60, cost=(0, 0, 0), ahead=0, **more
):
    return pl.pallas_call(
        kernel,
        name=name,
        grid_spec=pltpu.PrefetchScalarGridSpec(
            num_scalar_prefetch=ahead,
            grid=grid,
            in_specs=in_specs,
            out_specs=[o[0] for o in outs],
            scratch_shapes=list(scratch),
        ),
        out_shape=[jax.ShapeDtypeStruct(o[1], o[2]) for o in outs],
        compiler_params=pltpu.CompilerParams(vmem_limit_bytes=vmem << 20),
        cost_estimate=pl.CostEstimate(
            flops=cost[0], bytes_accessed=cost[1], transcendentals=cost[2]
        ),
        **more,
    )


def full(shape):
    return pl.BlockSpec(
        shape, lambda *_: (0,) * len(shape), pipeline_mode=pl.Buffered(1)
    )


SCALARS = pl.BlockSpec(memory_space=pltpu.SMEM)
PLACED = pl.BlockSpec(memory_space=pl.ANY)


def assemble_kernel(table, own_ref, got_ref, out_ref, sems):
    rows = own_ref.shape[1]
    copies = []
    for i in range(8):
        src = (own_ref, got_ref)[i // 4].at[i % 4]
        at = pl.multiple_of(rows * table[i], 32)
        copies.append(pltpu.make_async_copy(src, out_ref.at[pl.ds(at, rows)], sems.at[i]))
    for c in copies:
        c.start()
    for c in copies:
        c.wait()


def assemble(table, own, got):
    rows, cols = own.shape[1:]
    return call(
        assemble_kernel, "assemble", (1,), [SCALARS, PLACED, PLACED],
        [(full((8 * rows, cols)), (8 * rows, cols), BF)],
        [pltpu.SemaphoreType.DMA((8,))],
        cost=(0, 4 * rows * cols * 8, 0),
    )(table, own, got)[0]


def chunk(shape, axis=0):
    return pl.BlockSpec(shape, lambda i: tuple(i if a == axis else 0 for a in range(len(shape))))


def attend_kernel(half, order, *refs):
    if half:
        low_ref, vec_ref, w_one, w_two = refs[:4]
        qkv_ref, ctx_ref, lse_ref = refs[7:]
    else:
        x_ref, w_one, w_two, qkv_ref, ctx_ref, lse_ref, low_ref, vec_ref = refs
    step = pl.program_id(0)
    count, width = low_ref.shape
    part = width // GROUPS
    if not half:

        @pl.when(step == 0)
        def _():
            vec_ref[...] = w_one[:, 512:640].astype(F32).T[64:72]
            for at in range(0, count, 256):
                unit, _ = normalize(x_ref[at : at + 256].astype(F32))
                low_ref[at : at + 256] = (unit * vec_ref[0:1] + vec_ref[1:2]).astype(BF)

    zero = jnp.zeros((1, part), F32)
    bias_q = bias_v = zero
    for n in range(GROUPS):
        here = order[2 * half + step] == n
        bias_q = jnp.where(here, vec_ref[2:3, part * n : part * n + part], bias_q)
        bias_v = jnp.where(here, vec_ref[3:4, part * n : part * n + part], bias_v)
    bias = jnp.concatenate([bias_q, zero, bias_v], axis=1)
    w = jnp.where(step == 0, w_one[...], w_two[...])[:, : 3 * part]
    for at in range(0, count, 512):
        qkv_ref[0, at : at + 512] = (dot(low_ref[at : at + 512], w, 1, 0) + bias).astype(BF)
    for base in range(0, count, SEQ_LEN):
        block = min(1024, SEQ_LEN)
        for h in range(part // HEAD_DIM):
            at = h * HEAD_DIM
            v = qkv_ref[0, base : base + SEQ_LEN, 2 * part + at : 2 * part + at + HEAD_DIM].T
            for start in range(0, SEQ_LEN, block):
                stop = start + block
                q = qkv_ref[0, base + start : base + stop, at : at + HEAD_DIM] * BF(HEAD_DIM**-0.5)
                k = qkv_ref[0, base : base + stop, part + at : part + at + HEAD_DIM]
                row = lax.broadcasted_iota(jnp.int32, (stop, block), 0)
                col = lax.broadcasted_iota(jnp.int32, (stop, block), 1) + start
                scores = jnp.where(row <= col, dot(k, q, 1, 1), MASKED)
                top = jnp.max(scores, axis=0, keepdims=True)
                probs = jnp.exp(scores - top)
                total = jnp.sum(probs, axis=0, keepdims=True)
                out = dot(v[:, :stop], probs.astype(BF), 1, 0) / total
                ctx_ref[0, base + start : base + stop, at : at + HEAD_DIM] = out.T.astype(BF)
                lse_ref[0, h : h + 1, base + start : base + stop] = top + jnp.log(total)


def attend(half, order, weights, x=None, low=None, vec=None, before=()):
    count, width = (low if half else x).shape
    part = width // GROUPS
    at = lambda g: (2 * half + g, 0, 0)
    outs = [
        (pl.BlockSpec((1, count, 3 * part), at), (GROUPS, count, 3 * part), BF),
        (pl.BlockSpec((1, count, part), at), (GROUPS, count, part), BF),
        (pl.BlockSpec((1, 8, count), at), (GROUPS, 8, count), F32),
    ]
    w = [pl.BlockSpec((width, 640), lambda g: (0, 0), pipeline_mode=pl.Buffered(1))] * 2
    if half:
        ins, args = [full((count, width)), full((8, width))] + w + [PLACED] * 3, (low, vec)
    else:
        outs += [(full((count, width)), (count, width), BF), (full((8, width)), (8, width), F32)]
        ins, args = [full((count, width))] + w, (x,)
    return call(
        partial(attend_kernel, half), "attend", (2,), [SCALARS] + ins, outs,
        cost=(12_000_000_000, 8_000_000, 4_000_000),
        input_output_aliases={5 + i: i for i in range(len(before))},
    )(order, *args, *weights, *before)


def attend_back_kernel(half, order, table, *refs):
    qkv_ref, ctx_ref, dctx_ref, lse_ref, low_ref, w_one, w_two, two_ref = refs[:8]
    if half:
        o_refs, refs = refs[8:10], refs[2:]
    out_ref, *slabs, dq_ref, stage, sems = refs[8:]
    step = pl.program_id(0)
    count, width = low_ref.shape
    part = width // GROUPS
    inner = (ctx_ref[0].astype(F32) * dctx_ref[0].astype(F32)).T
    block = min(256, SEQ_LEN)
    for base in range(0, count, SEQ_LEN):
        last = base + SEQ_LEN
        for h in range(part // HEAD_DIM):
            at = h * HEAD_DIM
            q = qkv_ref[0, base:last, at : at + HEAD_DIM] * BF(HEAD_DIM**-0.5)
            do = dctx_ref[0, base:last, at : at + HEAD_DIM]
            turned = qkv_ref[0, base:last, part + at : part + at + HEAD_DIM].T
            row_dot = jnp.sum(inner[at : at + HEAD_DIM, base:last], axis=0, keepdims=True)
            for start in range(0, SEQ_LEN, block):
                stop = start + block
                rows = slice(base + start, base + stop)
                k = qkv_ref[0, rows, part + at : part + at + HEAD_DIM]
                v = qkv_ref[0, rows, 2 * part + at : 2 * part + at + HEAD_DIM]
                row = lax.broadcasted_iota(jnp.int32, (block, SEQ_LEN - start), 0)
                col = lax.broadcasted_iota(jnp.int32, (block, SEQ_LEN - start), 1)
                lse = lse_ref[0, h : h + 1, base + start : last]
                probs = jnp.where(row <= col, jnp.exp(dot(k, q[start:], 1, 1) - lse), 0.0)
                dscores = (probs * (dot(v, do[start:], 1, 1) - row_dot[:, start:])).astype(BF)
                dk = dot(dscores, q[start:], 1, 0)
                dv = dot(probs.astype(BF), do[start:], 1, 0)
                dq = dot(turned[:, start:stop], dscores, 1, 0)
                if start:
                    dq_ref[:, start:] += dq
                else:
                    dq_ref[...] = dq
                out_ref[0, rows, part + at : part + at + HEAD_DIM] = dk.astype(BF)
                out_ref[0, rows, 2 * part + at : 2 * part + at + HEAD_DIM] = dv.astype(BF)
            out_ref[0, base:last, at : at + HEAD_DIM] = (dq_ref[...].T * HEAD_DIM**-0.5).astype(BF)
    sums = jnp.sum(out_ref[0].astype(F32), axis=0, keepdims=True)
    grad = dot(low_ref[...], out_ref[0], 0, 0)
    w = jnp.where(step == 0, w_one[...], w_two[...]).astype(F32)
    shift = jnp.sum(w[:, : 3 * part] * sums, axis=-1, keepdims=True)
    gain = jnp.sum(w[:, : 3 * part] * grad, axis=-1, keepdims=True)
    gain = (gain - w[:, 577:578] * shift) / w[:, 576:577]
    row = lax.broadcasted_iota(jnp.int32, (width, part), 0) - order[2 * half + step] * part
    here = row == lax.broadcasted_iota(jnp.int32, (width, part), 1)
    columns = [gain, shift] + [
        jnp.sum(jnp.where(here, sums[:, at : at + part], 0.0), axis=-1, keepdims=True)
        for at in (0, 2 * part)
    ]
    lane = lax.broadcasted_iota(jnp.int32, (width, 64), 1)
    vecs = jnp.zeros((width, 64), F32)
    if not half:
        more = jnp.concatenate([two_ref[...], jnp.zeros((120, width), F32)]).T[:, :64]
        vecs = jnp.where(step == 0, more, vecs)
    for i, column in enumerate(columns):
        vecs = jnp.where(lane == i, column, vecs)
    stage[:, : 3 * part] = grad.astype(BF)
    stage[:, 3 * part : 640] = vecs.astype(BF)
    if half:
        stage[:, 640:] = jnp.concatenate([o_refs[0][0], o_refs[1][0]], axis=1)
    rows = width // 8
    for g in range(2):

        @pl.when(step == g)
        def _(g=g):
            copies = []
            for i in range(8):
                src = stage.at[pl.ds(pl.multiple_of(rows * table[i], 32), rows)]
                dst = slabs[2].at[i] if g else slabs[i // 4].at[i % 4]
                copies.append(pltpu.make_async_copy(src, dst, sems.at[i]))
            for c in copies:
                c.start()
            for c in copies:
                c.wait()


def attend_back(half, order, table, qkv, ctx, dctx, lse, low, o_part, weights, two):
    groups, count, part = qkv.shape
    part //= 3
    width = low.shape[1]
    at = lambda g, *_: (2 * half + g, 0, 0)
    cols = FAR if half else 640
    slabs = [(PLACED, (n, width // 8, cols), BF) for n in (4, 4, 8)]
    o_specs = [
        pl.BlockSpec((1, width, part), lambda g, order, table, b=b: (order[b + g], 0, 0))
        for b in ((2, 0) if half else ())
    ]
    return call(
        partial(attend_back_kernel, half), "attend_back", (2,),
        [
            pl.BlockSpec((1, count, 3 * part), at),
            pl.BlockSpec((1, count, part), at),
            pl.BlockSpec((1, count, part), at),
            pl.BlockSpec((1, 8, count), at),
            full((count, width)),
        ]
        + [pl.BlockSpec((width, 640), lambda *_: (0, 0), pipeline_mode=pl.Buffered(1))] * 2
        + [full((8, width))] + o_specs,
        [(pl.BlockSpec((1, count, 3 * part), lambda g, *_: (g, 0, 0)), (2, count, 3 * part), BF)]
        + slabs,
        [
            pltpu.VMEM((HEAD_DIM, SEQ_LEN), F32),
            pltpu.VMEM((width, cols), BF),
            pltpu.SemaphoreType.DMA((8,)),
        ],
        cost=(24_000_000_000, 14_000_000, 4_000_000), ahead=2,
    )(order, table, qkv, ctx, dctx, lse, low, *weights, two, *[o_part] * len(o_specs))


def dispatch_kernel(first, target_ref, rows_ref, out_ref):
    count = rows_ref.shape[0]
    for at in range(0, out_ref.shape[0], 256):
        slot = lax.broadcasted_iota(jnp.int32, (256, count), 0) + (first + at)
        picks = (target_ref[...] == slot).astype(F32).astype(BF)
        out_ref[at : at + 256] = dot(picks, rows_ref[...], 1, 0).astype(BF)


def dispatch(target, rows, first=0):
    count, width = rows.shape
    slots = count - first
    return call(
        partial(dispatch_kernel, first), "dispatch", (1,),
        [full((1, count)), full((count, width))],
        [(full((slots, width)), (slots, width), BF)],
        cost=(2 * count * count * width, 3_000_000, 0),
    )(target.reshape(1, count), rows)[0]


def column(row_ref):
    row = row_ref[...].astype(F32)
    return jnp.broadcast_to(row, (8, row.shape[1])).T[:, :1].astype(jnp.int32)


def mix_kernel(order, slab, x_ref, ctx_ref, vec_ref, target_ref, *refs):
    wo_refs, (h_ref, whole_ref, low_ref, sent_ref) = refs[:GROUPS], refs[GROUPS:]
    rows, width = x_ref.shape
    count = low_ref.shape[0]
    part = width // GROUPS
    step = pl.program_id(0)

    @pl.when(step == 0)
    def _():
        for q in range(GROUPS):
            first, second = slab[2 * order[q]], slab[2 * order[q] + 1]
            pieces = [jnp.concatenate([wo[first], wo[second]]) for wo in wo_refs]
            for n in range(GROUPS):
                piece = pieces[0]
                for r in range(1, GROUPS):
                    piece = jnp.where(order[r] == n, pieces[r], piece)
                whole_ref[q * part : q * part + part, n * part : n * part + part] = piece

    h = x_ref[...].astype(F32) + vec_ref[4:5]
    for r in range(GROUPS):
        h += dot(ctx_ref[r], whole_ref[r * part : r * part + part], 1, 0)
    h_ref[...] = h
    unit, _ = normalize(h)
    low_ref[pl.ds(pl.multiple_of(step * rows, 256), rows)] = (
        unit * vec_ref[5:6] + vec_ref[6:7]
    ).astype(BF)

    @pl.when(step == pl.num_programs(0) - 1)
    def _():
        for at in range(0, count // 2, 256):
            index = lax.broadcasted_iota(jnp.int32, (256, count), 0) + at
            picks = (target_ref[...] == index).astype(F32).astype(BF)
            sent_ref[at : at + 256] = dot(picks, low_ref[...], 1, 0).astype(BF)


def mix(order, slab, x, ctx, weights, vec, target):
    count, width = x.shape
    part = width // GROUPS
    rows = min(256, count)
    return call(
        mix_kernel, "mix", (count // rows,),
        [SCALARS, SCALARS, chunk((rows, width)), chunk((GROUPS, rows, part), 1), full((8, width)),
         full((1, count))] + [full((8, width // 8, part))] * GROUPS,
        [
            (chunk((rows, width)), (count, width), F32),
            (full((width, width)), (width, width), BF),
            (full((count, width)), (count, width), BF),
            (full((count // 2, width)), (count // 2, width), BF),
        ],
        cost=(2 * count * width * (width + count), 12_000_000, 0),
    )(order, slab, x, ctx, vec, target.reshape(1, count), *weights)


def unmix_kernel(
    order, h_ref, g_ref, dm_one, dm_two, target_ref, ctx_ref, whole_ref, vec_ref,
    dh_ref, dctx_ref, grad_ref, sum_ref, total_ref,
):
    rows, width = h_ref.shape
    part = width // GROUPS
    step = pl.program_id(0)
    dm = None
    target = column(target_ref)
    for half, sent in enumerate((dm_one, dm_two)):
        index = lax.broadcasted_iota(jnp.int32, (rows, sent.shape[0]), 1) + half * sent.shape[0]
        picks = (target == index).astype(F32).astype(BF)
        got = dot(picks, sent[...], 1, 0)
        dm = got if dm is None else dm + got
    unit, inverse = normalize(h_ref[...])
    dh = g_ref[...].astype(F32) + normalize_back(dm, unit, inverse, vec_ref[5:6])
    low = dh.astype(BF)
    dh_ref[...] = low
    sums = [
        jnp.sum(term, axis=0, keepdims=True) for term in (low.astype(F32), dm * unit, dm)
    ]
    zeros = jnp.zeros((1, width), F32)
    sums = jnp.concatenate([zeros] * 4 + sums + [zeros])
    for r in range(GROUPS):
        dctx_ref[r] = dot(low, whole_ref[r * part : r * part + part], 1, 1).astype(BF)
    grads = [dot(ctx_ref[q], low, 0, 0) for q in range(GROUPS)]

    @pl.when(step == 0)
    def _():
        sum_ref[...] = sums
        for q in range(GROUPS):
            total_ref[q] = grads[q]

    @pl.when(step > 0)
    def _():
        sum_ref[...] += sums
        for q in range(GROUPS):
            total_ref[q] += grads[q]

    @pl.when(step == pl.num_programs(0) - 1)
    def _():
        for q in range(GROUPS):
            grad = total_ref[q].astype(BF)
            at = pl.ds(pl.multiple_of(order[q] * part, 64), part)
            for n in range(GROUPS):
                grad_ref[n, at, :] = grad[:, n * part : n * part + part]


def unmix(order, h, g, dm_one, dm_two, target, ctx, whole, vec):
    count, width = h.shape
    part = width // GROUPS
    rows = min(256, count)
    half = full((count // 2, width))
    by_rows, by_ctx = chunk((rows, width)), chunk((GROUPS, rows, part), 1)
    return call(
        unmix_kernel, "unmix", (count // rows,),
        [SCALARS, by_rows, by_rows, half, half, chunk((1, rows), 1), by_ctx, full((width, width)),
         full((8, width))],
        [
            (by_rows, (count, width), BF),
            (by_ctx, (GROUPS, count, part), BF),
            (full((GROUPS, width, part)), (GROUPS, width, part), BF),
            (full((8, width)), (8, width), F32),
        ],
        [pltpu.VMEM((GROUPS, part, width), F32)],
        cost=(2 * count * width * (2 * width + count), 20_000_000, 0),
    )(order, h, g, dm_one, dm_two, target.reshape(1, count), ctx, whole, vec)


def finish_kernel(h_ref, target_ref, gy_ref, out_ref):
    slot = lax.broadcasted_iota(jnp.int32, (h_ref.shape[0], gy_ref.shape[0]), 1)
    picks = (column(target_ref) == slot).astype(F32).astype(BF)
    out_ref[...] = (h_ref[...] + dot(picks, gy_ref[...], 1, 0)).astype(BF)


def finish(h, target, gy):
    count, width = h.shape
    rows = min(256, count)
    return call(
        finish_kernel, "finish", (count // rows,),
        [chunk((rows, width)), chunk((1, rows), 1), full((count, width))],
        [(chunk((rows, width)), (count, width), BF)],
        cost=(2 * count * count * width, 6_000_000, 0),
    )(h, target.reshape(1, count), gy)[0]


def gelu_pair(v):
    cdf = 0.5 + 0.5 * lax.erf(v * 0.5**0.5)
    return v * cdf, cdf + v * jnp.exp(-0.5 * v * v) * (0.5 / jnp.pi) ** 0.5


def expert_kernel(
    x_ref, g_ref, win_ref, bin_ref, wout_ref, bout_ref, center_ref, _,
    gy_ref, dm_ref, dy_ref, hid_ref, du_ref, dbin_ref, small_ref,
    y_acc, dm_acc, gate_ref, gates,
):
    step = pl.program_id(0)
    rows, width = x_ref.shape

    @pl.when(step == 0)
    def _():
        z = jnp.sum(x_ref[...].astype(F32) * center_ref[...].astype(F32), axis=-1, keepdims=True)
        gate = 1.0 / (1.0 + jnp.exp(-z))
        gate_ref[...] = jnp.broadcast_to(gate, gate_ref.shape)
        dy_ref[...] = (gate * g_ref[...].reshape(rows, width).astype(F32)).astype(BF)

    act, slope = gelu_pair(dot(x_ref[...], win_ref[...], 1, 0) + bin_ref[...].astype(F32))
    hid = act.astype(BF)
    hid_ref[...] = hid
    y = dot(hid, wout_ref[...], 1, 0)
    du = (dot(dy_ref[...], wout_ref[...], 1, 1) * slope).astype(BF)
    du_ref[...] = du
    dbin_ref[...] = jnp.broadcast_to(
        jnp.sum(du.astype(F32), axis=0, keepdims=True), dbin_ref.shape
    )
    dm = dot(du, win_ref[...], 1, 1)

    @pl.when(step == 0)
    def _():
        y_acc[...] = y
        dm_acc[...] = dm

    @pl.when(step > 0)
    def _():
        y_acc[...] += y
        dm_acc[...] += dm

    @pl.when(step == pl.num_programs(0) - 1)
    def _():
        gate = gate_ref[:, :1]
        g = g_ref[...].reshape(rows, width).astype(F32)
        y = (y_acc[...] + bout_ref[...].astype(F32)).astype(BF).astype(F32)
        gy_ref[...] = (gate * y).astype(BF).reshape(gy_ref.shape)
        dz = gate * (1.0 - gate) * jnp.sum(g * y, axis=-1, keepdims=True)
        dm_ref[...] = (dm_acc[...] + dz * center_ref[...].astype(F32)).astype(BF)
        small_ref[0:1, :] = jnp.sum(dy_ref[...].astype(F32), axis=0, keepdims=True)
        small_ref[1:2, :] = jnp.sum(dz * x_ref[...].astype(F32), axis=0, keepdims=True)


def expert(half, x, g, win, bias_in, wout, bias_out, center, gy):
    rows, width = x.shape
    ff = win.shape[1]
    step = min(1024, ff)
    along = lambda i: (0, i)
    side = pl.BlockSpec(
        (g.shape[0], 1) + g.shape[2:], lambda i: (0, half, 0, 0), pipeline_mode=pl.Buffered(1)
    )
    return call(
        expert_kernel, "expert", (ff // step,),
        [
            full((rows, width)),
            side,
            pl.BlockSpec((width, step), along),
            pl.BlockSpec((1, step), along),
            pl.BlockSpec((step, width), lambda i: (i, 0)),
            full((1, width)),
            full((1, width)),
            PLACED,
        ],
        [
            (side, g.shape, BF),
            (full((rows, width)), (rows, width), BF),
            (full((rows, width)), (rows, width), BF),
            (pl.BlockSpec((rows, step), along), (rows, ff), BF),
            (pl.BlockSpec((rows, step), along), (rows, ff), BF),
            (pl.BlockSpec((8, step), along), (8, ff), F32),
            (full((8, width)), (8, width), F32),
        ],
        [
            pltpu.VMEM((rows, width), F32),
            pltpu.VMEM((rows, width), F32),
            pltpu.VMEM((rows, 128), F32),
            pltpu.SMEM((1,), jnp.int32),
        ],
        cost=(8 * rows * width * ff, 22_000_000, 2 * rows * ff),
        input_output_aliases={} if gy is None else {7: 0},
    )(x, g, win, bias_in, wout, bias_out, center, x if gy is None else gy)


def weigh_kernel(split, which, *refs):
    hid, du, dy, x, bias, small = (refs[i : i + 2] for i in range(0, 12, 2))
    ff = hid[0].shape[1]
    width = dy[0].shape[1]
    step = pl.program_id(0)
    small = small[0][...] + small[1][...]
    row = lax.broadcasted_iota(jnp.int32, (16, width), 0)
    bias = (bias[0][...] + bias[1][...])[0:1]
    if ff < width:
        bias = jnp.concatenate([bias, jnp.zeros((1, width - ff), F32)], axis=1)
    rest = jnp.where(row == 0, bias, 0.0)
    rest = jnp.where(row == 1, small[0:1], rest)
    rest = jnp.where(row == 2, small[1:2], rest)

    def pair(i):
        rows, cols = (x, du) if split else (du, x)
        return rows[i][...], cols[i][...]

    def put(out):
        out[:ff] = (dot(hid[0][...], dy[0][...], 0, 0) + dot(hid[1][...], dy[1][...], 0, 0)).astype(BF)
        out[ff : 2 * ff] = (
            dot(*pair(0), 0, 0) + dot(*pair(1), 0, 0)
        ).astype(BF)
        out[2 * ff :] = rest.astype(BF)

    if not split:
        put(refs[12].at[0])
        return
    for late, out in enumerate(refs[12:]):

        @pl.when(step // 2 == late)
        def _(out=out):
            put(out.at[0])


def weigh(which, n, split, hid, du, dy, x, bias, small):
    rows, ff = hid[0].shape
    width = dy[0].shape[1]
    part = ff // n
    size = 2 * part + 16
    along = lambda i, which: (0, which[i])
    wide = pl.BlockSpec((rows, part), along)
    if split:
        first = pl.BlockSpec((1, size, width), lambda i, which: (jnp.minimum(i, 1), 0, 0))
        last = pl.BlockSpec((1, size, width), lambda i, which: (jnp.maximum(i - 2, 0), 0, 0))
        outs = [(first, (2, size, width), BF), (last, (2, size, width), BF)]
    else:
        outs = [(pl.BlockSpec((1, size, width), lambda i, which: (i, 0, 0)), (n, size, width), BF)]
    got = call(
        partial(weigh_kernel, split), "weigh", (n,),
        [wide] * 4 + [full((rows, width))] * 4 + [pl.BlockSpec((8, part), along)] * 2
        + [full((8, width))] * 2,
        outs, cost=(8 * rows * width * ff, 26_000_000, 0), ahead=1,
    )(which, *hid, *du, *dy, *x, *bias, *small)
    return got if split else got[0]


def unproject_kernel(*refs):
    one_ref, two_ref, *w_refs = refs[: GROUPS + 2]
    x_ref, dh_ref, vec_ref, out_ref = refs[GROUPS + 2 :]
    part = x_ref.shape[1] // GROUPS
    da = None
    for r, w in enumerate(w_refs):
        got = dot((one_ref, two_ref)[r // 2][r % 2], w[:, : 3 * part], 1, 1)
        da = got if da is None else da + got
    unit, inverse = normalize(x_ref[...].astype(F32))
    out_ref[...] = dh_ref[...].astype(F32) + normalize_back(da, unit, inverse, vec_ref[0:1])


def unproject(grads, weights, x, dh, vec):
    count, width = x.shape
    part = width // GROUPS
    rows = min(256, count)
    w = pl.BlockSpec((width, 640), lambda i: (0, 0), pipeline_mode=pl.Buffered(1))
    return call(
        unproject_kernel, "unproject", (count // rows,),
        [chunk((2, rows, 3 * part), 1)] * 2 + [w] * GROUPS
        + [chunk((rows, width)), chunk((rows, width)), full((8, width))],
        [(chunk((rows, width)), (count, width), F32)],
        cost=(6 * count * width * width, 20_000_000, 0),
    )(*grads, *weights, x, dh, vec)[0]


def add(a, b):
    return (a.astype(F32) + b.astype(F32)).astype(BF)


class Place:
    def __init__(self, mesh):
        self.n_dp = mesh.shape["dp"]
        self.n_e = mesh.shape["expert"]
        self.staged = self.n_dp == 4 and self.n_e == 8
        if not self.staged:
            return
        dev = lambda x, c, z, y: (x * 2 + c) * 8 + z * 2 + y
        every = [
            (x, c, z, y) for x in range(2) for c in range(2) for z in range(4) for y in range(2)
        ]
        to = lambda move: [(dev(*p), dev(*move(*p))) for p in every]
        self.core = to(lambda x, c, z, y: (x, 1 - c, z, y))
        self.x = to(lambda x, c, z, y: (1 - x, c, z, y))
        self.across = to(lambda x, c, z, y: (1 - x, 1 - c, z, y))
        self.y = to(lambda x, c, z, y: (x, c, z, 1 - y))
        self.z = [to(lambda x, c, z, y, k=k: (x, c, z ^ k, y)) for k in range(1, 4)]

    def tables(self):
        r = jnp.arange(4, dtype=jnp.int32)
        i = jnp.arange(8, dtype=jnp.int32)
        if not self.staged:
            return r, i, r, i
        d, e = lax.axis_index("dp"), lax.axis_index("expert")
        z, y = e // 2, e % 2
        weighed = d ^ jnp.where(r < 2, 3 - 2 * r, 6 - 2 * r)
        return d ^ r, (z ^ i % 4) * 2 + (y ^ i // 4), weighed, (y ^ i % 2) * 4 + (z ^ i // 2)

    def move(self, array, way):
        return lax.ppermute(array, BOTH, way)


def whole_of(have):
    n_dp, n_e = lax.axis_size("dp"), lax.axis_size("expert")
    rows, cols = have.shape[1:]
    have = have.reshape(n_dp, n_e, rows, cols).transpose(1, 2, 0, 3)
    return have.reshape(n_e * rows, n_dp * cols)


def gather_all(array):
    return whole_of(lax.all_gather(array, BOTH, axis=0, tiled=False))


def scatter_all(array):
    n_dp, n_e = lax.axis_size("dp"), lax.axis_size("expert")
    rows, cols = array.shape[0] // n_e, array.shape[1] // n_dp
    parts = array.reshape(n_e, rows, n_dp, cols).transpose(2, 0, 1, 3)
    parts = parts.reshape(n_dp * n_e, rows, cols)
    return lax.psum_scatter(parts, BOTH, scatter_dimension=0, tiled=False)


def fetch(place, table, weights, out_weights, vectors, filler):
    barrier = lax.optimization_barrier
    stacked = jnp.stack(vectors)
    pad = 64 - len(vectors)
    if place.staged:
        rows = out_weights.shape[0]
        extra = jnp.concatenate([stacked.T, jnp.zeros((rows, pad), BF)], axis=1)
        shard = jnp.concatenate([*weights, extra], axis=1)
        own = jnp.stack([shard] + [place.move(shard, way) for way in place.z])
        own, out_weights, filler = barrier((own, out_weights, filler))
        got = place.move(own, place.y)
        out_own = jnp.stack([out_weights] + [place.move(out_weights, way) for way in place.z])
        got, out_own = barrier((got, out_own))
        near = assemble(table, own, got)
        across = place.move(near, place.x)
        far = place.move(near, place.core)
        return (near, far, across), (out_own, place.move(out_own, place.y)), filler
    vecs = lax.all_gather(stacked, "expert", axis=1, tiled=True)
    width = vecs.shape[1]
    extra = jnp.concatenate([vecs, jnp.zeros((pad, width), BF)]).T
    extra = jnp.broadcast_to(extra[None], (GROUPS, width, 64))
    by_group = lambda w: gather_all(w).reshape(width, GROUPS, -1).transpose(1, 0, 2)
    grouped = jnp.concatenate([*(by_group(w) for w in weights), extra], axis=2)
    out = by_group(out_weights)
    out = out.reshape(GROUPS, 8, width // 8, -1)
    return [grouped[i] for i in range(GROUPS)], [out[i] for i in range(GROUPS)], filler


def reduce_y(place, keep, send, cols):
    got = place.move(send, place.y)
    total = keep[0, :, :cols].astype(F32) + got[0, :, :cols].astype(F32)
    sends = [add(keep[k, :, :cols], got[k, :, :cols]) for k in range(1, 4)]
    return total, sends, add(keep[:, :, cols:], got[:, :, cols:])


def reduce_z(place, sends):
    return [place.move(part, way) for part, way in zip(sends, place.z)]


def columns_of(place, total, count):
    cols = (FAR - 640) // 2
    parts = [total[:, i * cols : (i + 1) * cols] for i in range(3)]
    vecs = total[:, 576 : 576 + 8].T
    vecs = vecs + sum(place.move(vecs, way) for way in (place.core, place.x, place.across))
    return parts, [vecs[i] for i in range(count)]


def reduce_plain(near, far, count):
    slabs = jnp.stack([a[:, :640] for a in (*near, *far)])
    width = slabs.shape[1]
    part = width // GROUPS
    whole = lambda array: array.transpose(1, 0, 2).reshape(width, width)
    parts = [whole(slabs[:, :, i * part : (i + 1) * part]) for i in range(3)]
    parts.append(whole(jnp.stack([far[0][:, -part:], far[1][:, -part:]] + [a[:, 640:-part] for a in far])))
    parts = [scatter_all(p).astype(F32) for p in parts]
    vecs = jnp.sum(slabs[:, :, 576 : 576 + count].astype(F32), axis=0).T
    vecs = lax.psum_scatter(vecs, "expert", scatter_dimension=1, tiled=True)
    vecs = lax.psum(vecs, "dp")
    return parts, [vecs[i] for i in range(count)]


def shards(
    place,
    block_entries,
    assignments,
    positions_within,
    specialist_quotas,
    standardize_one_scale,
    standardize_one_shift,
    asking_weights,
    asking_shift,
    lookup_weights,
    content_weights,
    content_shift,
    context_mixing_weights,
    context_mixing_shift,
    standardize_two_scale,
    standardize_two_shift,
    gating_prototypes,
    specialist_widen_weights,
    specialist_widen_shift,
    specialist_contract_weights,
    specialist_contract_shift,
    upstream_adjoint,
):
    count, width = block_entries.shape
    experts = specialist_quotas.shape[0]
    cap = count // experts
    n_dp = place.n_dp
    order, table, weighed, place_of = place.tables()
    barrier = lax.optimization_barrier

    chosen = assignments[:, None] == lax.broadcasted_iota(jnp.int32, (count, experts), 1)
    limit = jnp.sum(jnp.where(chosen, specialist_quotas[None, :], 0), axis=1)
    kept = positions_within < limit
    target = jnp.where(kept, assignments * cap + positions_within, count)
    late = positions_within >= cap // 2
    halved = jnp.where(late, positions_within + (count - cap) // 2, positions_within)
    halved = jnp.where(kept, assignments * (cap // 2) + halved, count)

    def exchange(rows):
        sent = rows.reshape(experts, -1, width)
        got = lax.all_to_all(sent, "expert", split_axis=0, concat_axis=0, tiled=True)
        return got.reshape(rows.shape)

    weights, out, sent_g = fetch(
        place,
        table,
        (asking_weights, lookup_weights, content_weights),
        context_mixing_weights,
        (
            standardize_one_scale,
            standardize_one_shift,
            asking_shift,
            content_shift,
            context_mixing_shift,
            standardize_two_scale,
            standardize_two_shift,
        ),
        dispatch(target, upstream_adjoint),
    )

    sent_g, first = barrier((sent_g, weights[1]))
    weights = (weights[0], first, *weights[2:])
    rows_g = exchange(sent_g).reshape(experts, 2, cap // 2, width)

    *before, low_in, vec = attend(0, order, weights[:2], x=block_entries)
    if place.staged:
        before, out = barrier((before, out))
        out_near = jnp.concatenate(out)
        before, across, out_near = barrier((before, weights[2], out_near))
        weights = (*weights[:2], across, place.move(across, place.core))
        out_across = place.move(out_near, place.x)
        out = (out_near, place.move(out_near, place.core))
    qkv, ctx, lse = attend(1, order, weights[2:], low=low_in, vec=vec, before=before)
    ctx, rows_g = barrier((ctx, rows_g))
    if place.staged:
        ctx, out_across = barrier((ctx, out_across))
        out += (out_across, place.move(out_across, place.core))
    h1, whole_o, low_mid, sent_one = mix(order, place_of, block_entries, ctx, out, vec, halved)

    sent_two = dispatch(halved, low_mid, count // 2)
    x_one, sent_two = barrier((exchange(sent_one), sent_two))
    x_two = exchange(sent_two)
    matrices = (
        specialist_widen_weights[0], specialist_widen_shift, specialist_contract_weights[0],
        specialist_contract_shift, gating_prototypes,
    )
    gy, dm_one, dy_one, hid_one, du_one, dbin_one, small_one = expert(
        0, x_one, rows_g, *matrices, None
    )
    x_two, dm_one = barrier((x_two, dm_one))
    dm_one = exchange(dm_one)
    gy, dm_two, dy_two, hid_two, du_two, dbin_two, small_two = expert(
        1, x_two, rows_g, *matrices, gy
    )
    dm_one, dm_two, hid_two = barrier((dm_one, dm_two, hid_two))
    dm_two = exchange(dm_two)
    sides = (
        (hid_one, hid_two), (du_one, du_two), (dy_one, dy_two), (x_one, x_two),
        (dbin_one, dbin_two), (small_one, small_two),
    )
    if place.staged:
        grads_far, grads = weigh(
            weighed, n_dp, True, *sides
        )
        grads_far, gy, dm_two = barrier((grads_far, gy, dm_two))
        came_far = place.move(grads_far, place.core)
        crossing = add(grads[0], came_far[0])
    else:
        grads = weigh(jnp.arange(n_dp, dtype=jnp.int32), n_dp, False, *sides)
        grads = lax.psum_scatter(grads, "dp", scatter_dimension=0, tiled=False)
    gy = exchange(gy.reshape(count, width))

    dh1, dctx, grad_o, two = unmix(
        order, h1, upstream_adjoint, dm_one, dm_two, halved, ctx, whole_o, vec
    )
    back = lambda half, dctx: attend_back(
        half, order, table, qkv, ctx, dctx, lse, low_in, grad_o, weights[2 * half : 2 * half + 2],
        two,
    )
    if place.staged:
        dctx, crossing = barrier((dctx, crossing))
        came = place.move(crossing, place.x)
        far, keep, send, more = back(1, dctx)
        more = place.move(more, place.core)
        far, gy = barrier((far, gy))
        output = finish(h1, target, gy)
        send = add(send, more[4:])
        dctx, output, send = barrier((dctx, output, send))
        cols = width // GROUPS
        across, sends, own_o = reduce_y(place, add(keep, more[:4]), send, FAR - cols)
        near, keep, send, more = back(0, dctx)
        near, keep, send, more, across, sends, own_o = barrier(
            (near, keep, send, more, across, sends, own_o)
        )
        more = place.move(more, place.core)
        got = reduce_z(place, sends)
        send, keep = add(send, more[4:]), add(keep, more[:4])
        near, send, keep = barrier((near, send, keep))
        got_y = place.move(send, place.y)
        input_grad = unproject((near, far), weights, block_entries, dh1, vec)
        got_far = got
        got, input_grad, came = barrier((got_y, input_grad, came))
        wide = lambda k, a: jnp.concatenate([a, own_o[k].astype(a.dtype)], axis=1)
        total = wide(0, keep[0].astype(F32) + got[0].astype(F32))
        got = reduce_z(place, [wide(k, add(keep[k], got[k])) for k in range(1, 4)])
        got_far, came, input_grad = barrier((got_far, came, input_grad))
        across = across + sum(g.astype(F32) for g in got_far)
        across = place.move(across.astype(BF), place.x)
        pick = lambda at: sum(
            a[at : at + width].astype(F32) for a in (grads[1], came_far[1], came)
        )
        got, grads, across = barrier((got, [pick(0), pick(width), pick(2 * width)], across))
        total += across.astype(F32)
        total += sum(g.astype(F32) for g in got)
        (sum_q, sum_k, sum_v), small = columns_of(place, total, 7)
        sum_o = total[:, 640:]
    else:
        parts = [back(half, dctx) for half in range(2)]
        slabs = [
            [jnp.concatenate(p[1:3]).reshape(width, -1), p[3].reshape(width, -1)]
            for p in parts
        ]
        (sum_q, sum_k, sum_v, sum_o), small = reduce_plain(*slabs, 7)
        input_grad = unproject([p[0] for p in parts], weights, block_entries, dh1, vec)
        output = finish(h1, target, gy)

        part = (grads.shape[0] - 16) // 2
        grads = [grads[:part], grads[part : 2 * part].T, grads[2 * part :]]
        grads = [g.astype(F32) for g in grads]

    grad_out, grad_in, rest = grads
    part = grad_out.shape[0]
    own = lax.axis_index("dp") * (width // n_dp)
    grad_bin = rest[0:1, :part]
    grad_bout = lax.dynamic_slice(rest[1:2], (0, own), (1, width // n_dp))
    grad_centers = rest[2:3]
    return (
        output,
        input_grad,
        small[0],
        small[1],
        sum_q,
        small[2],
        sum_k,
        sum_v,
        small[3],
        sum_o,
        small[4],
        small[5],
        small[6],
        grad_centers,
        grad_in[None],
        grad_bin,
        grad_out[None],
        grad_bout,
    )


def solution(mesh):
    placed = (
        P(("dp", "expert"), None),
        P(("dp", "expert")),
        P(("dp", "expert")),
        P(),
        P("expert"),
        P("expert"),
        P("expert", "dp"),
        P("expert"),
        P("expert", "dp"),
        P("expert", "dp"),
        P("expert"),
        P("expert", "dp"),
        P("expert"),
        P("expert"),
        P("expert"),
        P("expert", None),
        P("expert", None, None),
        P("expert", None),
        P("expert", None, None),
        P("expert", None),
        P(("dp", "expert"), None),
    )
    return jax.shard_map(
        partial(shards, Place(mesh)),
        mesh=mesh,
        in_specs=placed,
        out_specs=(
            P(("dp", "expert"), None),
            P(("dp", "expert"), None),
            P("expert"),
            P("expert"),
            P("expert", "dp"),
            P("expert"),
            P("expert", "dp"),
            P("expert", "dp"),
            P("expert"),
            P("expert", "dp"),
            P("expert"),
            P("expert"),
            P("expert"),
            P("expert", None),
            P("expert", None, "dp"),
            P("expert", "dp"),
            P("expert", "dp", None),
            P("expert", "dp"),
        ),
        check_vma=False,
    )
```

```python
from functools import partial

import jax
import jax.numpy as jnp
from jax import lax
from jax.experimental import pallas as pl
from jax.experimental.pallas import tpu as pltpu
from jax.sharding import PartitionSpec as P

HEADS = 12
HEAD_DIM = 64
SEQ_LEN = 1024
GROUPS = 4

EPSILON = 1e-05
MASKED = -1e30
FAR = 1024
BOTH = ("dp", "expert")
BF = jnp.bfloat16
F32 = jnp.float32


def dot(left, right, left_dim, right_dim):
    return lax.dot_general(
        left, right, (((left_dim,), (right_dim,)), ((), ())), preferred_element_type=F32
    )


def normalize(values):
    center = jnp.mean(values, axis=-1, keepdims=True)
    centered = values - center
    inverse = lax.rsqrt(jnp.mean(centered * centered, axis=-1, keepdims=True) + EPSILON)
    return (centered * inverse, inverse)


def normalize_back(grad, normed, inverse, gain):
    scaled = grad * gain
    return inverse * (
        scaled
        - jnp.mean(scaled, axis=-1, keepdims=True)
        - normed * jnp.mean(scaled * normed, axis=-1, keepdims=True)
    )


def call(
    kernel, name, grid, in_specs, outs, scratch=(), vmem=60, cost=(0, 0, 0), ahead=0, **more
):
    return pl.pallas_call(
        kernel,
        name=name,
        grid_spec=pltpu.PrefetchScalarGridSpec(
            num_scalar_prefetch=ahead,
            grid=grid,
            in_specs=in_specs,
            out_specs=[o[0] for o in outs],
            scratch_shapes=list(scratch),
        ),
        out_shape=[jax.ShapeDtypeStruct(o[1], o[2]) for o in outs],
        compiler_params=pltpu.CompilerParams(vmem_limit_bytes=vmem << 20),
        cost_estimate=pl.CostEstimate(
            flops=cost[0], bytes_accessed=cost[1], transcendentals=cost[2]
        ),
        **more,
    )


def full(shape):
    return pl.BlockSpec(
        shape, lambda *_: (0,) * len(shape), pipeline_mode=pl.Buffered(1)
    )


SCALARS = pl.BlockSpec(memory_space=pltpu.SMEM)
PLACED = pl.BlockSpec(memory_space=pl.ANY)


def assemble_kernel(table, own_ref, got_ref, out_ref, sems):
    rows = own_ref.shape[1]
    copies = []
    for i in range(8):
        src = (own_ref, got_ref)[i // 4].at[i % 4]
        at = pl.multiple_of(rows * table[i], 32)
        copies.append(pltpu.make_async_copy(src, out_ref.at[pl.ds(at, rows)], sems.at[i]))
    for c in copies:
        c.start()
    for c in copies:
        c.wait()


def assemble(table, own, got):
    rows, cols = own.shape[1:]
    return call(
        assemble_kernel, "assemble", (1,), [SCALARS, PLACED, PLACED],
        [(full((8 * rows, cols)), (8 * rows, cols), BF)],
        [pltpu.SemaphoreType.DMA((8,))],
        cost=(0, 4 * rows * cols * 8, 0),
    )(table, own, got)[0]


def chunk(shape, axis=0):
    return pl.BlockSpec(shape, lambda i: tuple(i if a == axis else 0 for a in range(len(shape))))


def attend_kernel(half, order, *refs):
    if half:
        low_ref, vec_ref, w_one, w_two = refs[:4]
        qkv_ref, ctx_ref, lse_ref = refs[7:]
    else:
        x_ref, w_one, w_two, qkv_ref, ctx_ref, lse_ref, low_ref, vec_ref = refs
    step = pl.program_id(0)
    count, width = low_ref.shape
    part = width // GROUPS
    if not half:

        @pl.when(step == 0)
        def _():
            vec_ref[...] = w_one[:, 512:640].astype(F32).T[64:72]
            for at in range(0, count, 256):
                unit, _ = normalize(x_ref[at : at + 256].astype(F32))
                low_ref[at : at + 256] = (unit * vec_ref[0:1] + vec_ref[1:2]).astype(BF)

    zero = jnp.zeros((1, part), F32)
    bias_q = bias_v = zero
    for n in range(GROUPS):
        here = order[2 * half + step] == n
        bias_q = jnp.where(here, vec_ref[2:3, part * n : part * n + part], bias_q)
        bias_v = jnp.where(here, vec_ref[3:4, part * n : part * n + part], bias_v)
    bias = jnp.concatenate([bias_q, zero, bias_v], axis=1)
    w = jnp.where(step == 0, w_one[...], w_two[...])[:, : 3 * part]
    for at in range(0, count, 512):
        qkv_ref[0, at : at + 512] = (dot(low_ref[at : at + 512], w, 1, 0) + bias).astype(BF)
    for base in range(0, count, SEQ_LEN):
        block = min(1024, SEQ_LEN)
        for h in range(part // HEAD_DIM):
            at = h * HEAD_DIM
            v = qkv_ref[0, base : base + SEQ_LEN, 2 * part + at : 2 * part + at + HEAD_DIM].T
            for start in range(0, SEQ_LEN, block):
                stop = start + block
                q = qkv_ref[0, base + start : base + stop, at : at + HEAD_DIM] * BF(HEAD_DIM**-0.5)
                k = qkv_ref[0, base : base + stop, part + at : part + at + HEAD_DIM]
                row = lax.broadcasted_iota(jnp.int32, (stop, block), 0)
                col = lax.broadcasted_iota(jnp.int32, (stop, block), 1) + start
                scores = jnp.where(row <= col, dot(k, q, 1, 1), MASKED)
                top = jnp.max(scores, axis=0, keepdims=True)
                probs = jnp.exp(scores - top)
                total = jnp.sum(probs, axis=0, keepdims=True)
                out = dot(v[:, :stop], probs.astype(BF), 1, 0) / total
                ctx_ref[0, base + start : base + stop, at : at + HEAD_DIM] = out.T.astype(BF)
                lse_ref[0, h : h + 1, base + start : base + stop] = top + jnp.log(total)


def attend(half, order, weights, x=None, low=None, vec=None, before=()):
    count, width = (low if half else x).shape
    part = width // GROUPS
    at = lambda g: (2 * half + g, 0, 0)
    outs = [
        (pl.BlockSpec((1, count, 3 * part), at), (GROUPS, count, 3 * part), BF),
        (pl.BlockSpec((1, count, part), at), (GROUPS, count, part), BF),
        (pl.BlockSpec((1, 8, count), at), (GROUPS, 8, count), F32),
    ]
    w = [pl.BlockSpec((width, 640), lambda g: (0, 0), pipeline_mode=pl.Buffered(1))] * 2
    if half:
        ins, args = [full((count, width)), full((8, width))] + w + [PLACED] * 3, (low, vec)
    else:
        outs += [(full((count, width)), (count, width), BF), (full((8, width)), (8, width), F32)]
        ins, args = [full((count, width))] + w, (x,)
    return call(
        partial(attend_kernel, half), "attend", (2,), [SCALARS] + ins, outs,
        cost=(12_000_000_000, 8_000_000, 4_000_000),
        input_output_aliases={5 + i: i for i in range(len(before))},
    )(order, *args, *weights, *before)


def attend_back_kernel(half, order, table, *refs):
    qkv_ref, ctx_ref, dctx_ref, lse_ref, low_ref, w_one, w_two, two_ref = refs[:8]
    if half:
        o_refs, refs = refs[8:10], refs[2:]
    out_ref, *slabs, dq_ref, stage, sems = refs[8:]
    step = pl.program_id(0)
    count, width = low_ref.shape
    part = width // GROUPS
    inner = (ctx_ref[0].astype(F32) * dctx_ref[0].astype(F32)).T
    block = min(256, SEQ_LEN)
    for base in range(0, count, SEQ_LEN):
        last = base + SEQ_LEN
        for h in range(part // HEAD_DIM):
            at = h * HEAD_DIM
            q = qkv_ref[0, base:last, at : at + HEAD_DIM] * BF(HEAD_DIM**-0.5)
            do = dctx_ref[0, base:last, at : at + HEAD_DIM]
            turned = qkv_ref[0, base:last, part + at : part + at + HEAD_DIM].T
            row_dot = jnp.sum(inner[at : at + HEAD_DIM, base:last], axis=0, keepdims=True)
            for start in range(0, SEQ_LEN, block):
                stop = start + block
                rows = slice(base + start, base + stop)
                k = qkv_ref[0, rows, part + at : part + at + HEAD_DIM]
                v = qkv_ref[0, rows, 2 * part + at : 2 * part + at + HEAD_DIM]
                row = lax.broadcasted_iota(jnp.int32, (block, SEQ_LEN - start), 0)
                col = lax.broadcasted_iota(jnp.int32, (block, SEQ_LEN - start), 1)
                lse = lse_ref[0, h : h + 1, base + start : last]
                probs = jnp.where(row <= col, jnp.exp(dot(k, q[start:], 1, 1) - lse), 0.0)
                dscores = (probs * (dot(v, do[start:], 1, 1) - row_dot[:, start:])).astype(BF)
                dk = dot(dscores, q[start:], 1, 0)
                dv = dot(probs.astype(BF), do[start:], 1, 0)
                dq = dot(turned[:, start:stop], dscores, 1, 0)
                if start:
                    dq_ref[:, start:] += dq
                else:
                    dq_ref[...] = dq
                out_ref[0, rows, part + at : part + at + HEAD_DIM] = dk.astype(BF)
                out_ref[0, rows, 2 * part + at : 2 * part + at + HEAD_DIM] = dv.astype(BF)
            out_ref[0, base:last, at : at + HEAD_DIM] = (dq_ref[...].T * HEAD_DIM**-0.5).astype(BF)
    sums = jnp.sum(out_ref[0].astype(F32), axis=0, keepdims=True)
    grad = dot(low_ref[...], out_ref[0], 0, 0)
    w = jnp.where(step == 0, w_one[...], w_two[...]).astype(F32)
    shift = jnp.sum(w[:, : 3 * part] * sums, axis=-1, keepdims=True)
    gain = jnp.sum(w[:, : 3 * part] * grad, axis=-1, keepdims=True)
    gain = (gain - w[:, 577:578] * shift) / w[:, 576:577]
    row = lax.broadcasted_iota(jnp.int32, (width, part), 0) - order[2 * half + step] * part
    here = row == lax.broadcasted_iota(jnp.int32, (width, part), 1)
    columns = [gain, shift] + [
        jnp.sum(jnp.where(here, sums[:, at : at + part], 0.0), axis=-1, keepdims=True)
        for at in (0, 2 * part)
    ]
    lane = lax.broadcasted_iota(jnp.int32, (width, 64), 1)
    vecs = jnp.zeros((width, 64), F32)
    if not half:
        more = jnp.concatenate([two_ref[...], jnp.zeros((120, width), F32)]).T[:, :64]
        vecs = jnp.where(step == 0, more, vecs)
    for i, column in enumerate(columns):
        vecs = jnp.where(lane == i, column, vecs)
    stage[:, : 3 * part] = grad.astype(BF)
    stage[:, 3 * part : 640] = vecs.astype(BF)
    if half:
        stage[:, 640:] = jnp.concatenate([o_refs[0][0], o_refs[1][0]], axis=1)
    rows = width // 8
    for g in range(2):

        @pl.when(step == g)
        def _(g=g):
            copies = []
            for i in range(8):
                src = stage.at[pl.ds(pl.multiple_of(rows * table[i], 32), rows)]
                dst = slabs[2].at[i] if g else slabs[i // 4].at[i % 4]
                copies.append(pltpu.make_async_copy(src, dst, sems.at[i]))
            for c in copies:
                c.start()
            for c in copies:
                c.wait()


def attend_back(half, order, table, qkv, ctx, dctx, lse, low, o_part, weights, two):
    groups, count, part = qkv.shape
    part //= 3
    width = low.shape[1]
    at = lambda g, *_: (2 * half + g, 0, 0)
    cols = FAR if half else 640
    slabs = [(PLACED, (n, width // 8, cols), BF) for n in (4, 4, 8)]
    o_specs = [
        pl.BlockSpec((1, width, part), lambda g, order, table, b=b: (order[b + g], 0, 0))
        for b in ((2, 0) if half else ())
    ]
    return call(
        partial(attend_back_kernel, half), "attend_back", (2,),
        [
            pl.BlockSpec((1, count, 3 * part), at),
            pl.BlockSpec((1, count, part), at),
            pl.BlockSpec((1, count, part), at),
            pl.BlockSpec((1, 8, count), at),
            full((count, width)),
        ]
        + [pl.BlockSpec((width, 640), lambda *_: (0, 0), pipeline_mode=pl.Buffered(1))] * 2
        + [full((8, width))] + o_specs,
        [(pl.BlockSpec((1, count, 3 * part), lambda g, *_: (g, 0, 0)), (2, count, 3 * part), BF)]
        + slabs,
        [
            pltpu.VMEM((HEAD_DIM, SEQ_LEN), F32),
            pltpu.VMEM((width, cols), BF),
            pltpu.SemaphoreType.DMA((8,)),
        ],
        cost=(24_000_000_000, 14_000_000, 4_000_000), ahead=2,
    )(order, table, qkv, ctx, dctx, lse, low, *weights, two, *[o_part] * len(o_specs))


def dispatch_kernel(first, target_ref, rows_ref, out_ref):
    count = rows_ref.shape[0]
    for at in range(0, out_ref.shape[0], 256):
        slot = lax.broadcasted_iota(jnp.int32, (256, count), 0) + (first + at)
        picks = (target_ref[...] == slot).astype(F32).astype(BF)
        out_ref[at : at + 256] = dot(picks, rows_ref[...], 1, 0).astype(BF)


def dispatch(target, rows, first=0):
    count, width = rows.shape
    slots = count - first
    return call(
        partial(dispatch_kernel, first), "dispatch", (1,),
        [full((1, count)), full((count, width))],
        [(full((slots, width)), (slots, width), BF)],
        cost=(2 * count * count * width, 3_000_000, 0),
    )(target.reshape(1, count), rows)[0]


def column(row_ref):
    row = row_ref[...].astype(F32)
    return jnp.broadcast_to(row, (8, row.shape[1])).T[:, :1].astype(jnp.int32)


def mix_kernel(order, slab, x_ref, ctx_ref, vec_ref, target_ref, *refs):
    wo_refs, (h_ref, whole_ref, low_ref, sent_ref) = refs[:GROUPS], refs[GROUPS:]
    rows, width = x_ref.shape
    count = low_ref.shape[0]
    part = width // GROUPS
    step = pl.program_id(0)

    @pl.when(step == 0)
    def _():
        for q in range(GROUPS):
            first, second = slab[2 * order[q]], slab[2 * order[q] + 1]
            pieces = [jnp.concatenate([wo[first], wo[second]]) for wo in wo_refs]
            for n in range(GROUPS):
                piece = pieces[0]
                for r in range(1, GROUPS):
                    piece = jnp.where(order[r] == n, pieces[r], piece)
                whole_ref[q * part : q * part + part, n * part : n * part + part] = piece

    h = x_ref[...].astype(F32) + vec_ref[4:5]
    for r in range(GROUPS):
        h += dot(ctx_ref[r], whole_ref[r * part : r * part + part], 1, 0)
    h_ref[...] = h
    unit, _ = normalize(h)
    low_ref[pl.ds(pl.multiple_of(step * rows, 256), rows)] = (
        unit * vec_ref[5:6] + vec_ref[6:7]
    ).astype(BF)

    @pl.when(step == pl.num_programs(0) - 1)
    def _():
        for at in range(0, count // 2, 256):
            index = lax.broadcasted_iota(jnp.int32, (256, count), 0) + at
            picks = (target_ref[...] == index).astype(F32).astype(BF)
            sent_ref[at : at + 256] = dot(picks, low_ref[...], 1, 0).astype(BF)


def mix(order, slab, x, ctx, weights, vec, target):
    count, width = x.shape
    part = width // GROUPS
    rows = min(256, count)
    return call(
        mix_kernel, "mix", (count // rows,),
        [SCALARS, SCALARS, chunk((rows, width)), chunk((GROUPS, rows, part), 1), full((8, width)),
         full((1, count))] + [full((8, width // 8, part))] * GROUPS,
        [
            (chunk((rows, width)), (count, width), F32),
            (full((width, width)), (width, width), BF),
            (full((count, width)), (count, width), BF),
            (full((count // 2, width)), (count // 2, width), BF),
        ],
        cost=(2 * count * width * (width + count), 12_000_000, 0),
    )(order, slab, x, ctx, vec, target.reshape(1, count), *weights)


def unmix_kernel(
    order, h_ref, g_ref, dm_one, dm_two, target_ref, ctx_ref, whole_ref, vec_ref,
    dh_ref, dctx_ref, grad_ref, sum_ref, total_ref,
):
    rows, width = h_ref.shape
    part = width // GROUPS
    step = pl.program_id(0)
    dm = None
    target = column(target_ref)
    for half, sent in enumerate((dm_one, dm_two)):
        index = lax.broadcasted_iota(jnp.int32, (rows, sent.shape[0]), 1) + half * sent.shape[0]
        picks = (target == index).astype(F32).astype(BF)
        got = dot(picks, sent[...], 1, 0)
        dm = got if dm is None else dm + got
    unit, inverse = normalize(h_ref[...])
    dh = g_ref[...].astype(F32) + normalize_back(dm, unit, inverse, vec_ref[5:6])
    low = dh.astype(BF)
    dh_ref[...] = low
    sums = [
        jnp.sum(term, axis=0, keepdims=True) for term in (low.astype(F32), dm * unit, dm)
    ]
    zeros = jnp.zeros((1, width), F32)
    sums = jnp.concatenate([zeros] * 4 + sums + [zeros])
    for r in range(GROUPS):
        dctx_ref[r] = dot(low, whole_ref[r * part : r * part + part], 1, 1).astype(BF)
    grads = [dot(ctx_ref[q], low, 0, 0) for q in range(GROUPS)]

    @pl.when(step == 0)
    def _():
        sum_ref[...] = sums
        for q in range(GROUPS):
            total_ref[q] = grads[q]

    @pl.when(step > 0)
    def _():
        sum_ref[...] += sums
        for q in range(GROUPS):
            total_ref[q] += grads[q]

    @pl.when(step == pl.num_programs(0) - 1)
    def _():
        for q in range(GROUPS):
            grad = total_ref[q].astype(BF)
            at = pl.ds(pl.multiple_of(order[q] * part, 64), part)
            for n in range(GROUPS):
                grad_ref[n, at, :] = grad[:, n * part : n * part + part]


def unmix(order, h, g, dm_one, dm_two, target, ctx, whole, vec):
    count, width = h.shape
    part = width // GROUPS
    rows = min(512, count)
    half = full((count // 2, width))
    by_rows, by_ctx = chunk((rows, width)), chunk((GROUPS, rows, part), 1)
    return call(
        unmix_kernel, "unmix", (count // rows,),
        [SCALARS, by_rows, by_rows, half, half, chunk((1, rows), 1), by_ctx, full((width, width)),
         full((8, width))],
        [
            (by_rows, (count, width), BF),
            (by_ctx, (GROUPS, count, part), BF),
            (full((GROUPS, width, part)), (GROUPS, width, part), BF),
            (full((8, width)), (8, width), F32),
        ],
        [pltpu.VMEM((GROUPS, part, width), F32)],
        cost=(2 * count * width * (2 * width + count), 20_000_000, 0),
    )(order, h, g, dm_one, dm_two, target.reshape(1, count), ctx, whole, vec)


def finish_kernel(h_ref, target_ref, gy_ref, out_ref):
    slot = lax.broadcasted_iota(jnp.int32, (h_ref.shape[0], gy_ref.shape[0]), 1)
    picks = (column(target_ref) == slot).astype(F32).astype(BF)
    out_ref[...] = (h_ref[...] + dot(picks, gy_ref[...], 1, 0)).astype(BF)


def finish(h, target, gy):
    count, width = h.shape
    rows = min(256, count)
    return call(
        finish_kernel, "finish", (count // rows,),
        [chunk((rows, width)), chunk((1, rows), 1), full((count, width))],
        [(chunk((rows, width)), (count, width), BF)],
        cost=(2 * count * count * width, 6_000_000, 0),
    )(h, target.reshape(1, count), gy)[0]


def gelu_pair(v):
    cdf = 0.5 + 0.5 * lax.erf(v * 0.5**0.5)
    return v * cdf, cdf + v * jnp.exp(-0.5 * v * v) * (0.5 / jnp.pi) ** 0.5


def expert_kernel(
    x_ref, g_ref, win_ref, bin_ref, wout_ref, bout_ref, center_ref, _,
    gy_ref, dm_ref, dy_ref, hid_ref, du_ref, dbin_ref, small_ref,
    y_acc, dm_acc, gate_ref, gates,
):
    step = pl.program_id(0)
    rows, width = x_ref.shape

    @pl.when(step == 0)
    def _():
        z = jnp.sum(x_ref[...].astype(F32) * center_ref[...].astype(F32), axis=-1, keepdims=True)
        gate = 1.0 / (1.0 + jnp.exp(-z))
        gate_ref[...] = jnp.broadcast_to(gate, gate_ref.shape)
        dy_ref[...] = (gate * g_ref[...].reshape(rows, width).astype(F32)).astype(BF)

    act, slope = gelu_pair(dot(x_ref[...], win_ref[...], 1, 0) + bin_ref[...].astype(F32))
    hid = act.astype(BF)
    hid_ref[...] = hid
    y = dot(hid, wout_ref[...], 1, 0)
    du = (dot(dy_ref[...], wout_ref[...], 1, 1) * slope).astype(BF)
    du_ref[...] = du
    dbin_ref[...] = jnp.broadcast_to(
        jnp.sum(du.astype(F32), axis=0, keepdims=True), dbin_ref.shape
    )
    dm = dot(du, win_ref[...], 1, 1)

    @pl.when(step == 0)
    def _():
        y_acc[...] = y
        dm_acc[...] = dm

    @pl.when(step > 0)
    def _():
        y_acc[...] += y
        dm_acc[...] += dm

    @pl.when(step == pl.num_programs(0) - 1)
    def _():
        gate = gate_ref[:, :1]
        g = g_ref[...].reshape(rows, width).astype(F32)
        y = (y_acc[...] + bout_ref[...].astype(F32)).astype(BF).astype(F32)
        gy_ref[...] = (gate * y).astype(BF).reshape(gy_ref.shape)
        dz = gate * (1.0 - gate) * jnp.sum(g * y, axis=-1, keepdims=True)
        dm_ref[...] = (dm_acc[...] + dz * center_ref[...].astype(F32)).astype(BF)
        small_ref[0:1, :] = jnp.sum(dy_ref[...].astype(F32), axis=0, keepdims=True)
        small_ref[1:2, :] = jnp.sum(dz * x_ref[...].astype(F32), axis=0, keepdims=True)


def expert(half, x, g, win, bias_in, wout, bias_out, center, gy):
    rows, width = x.shape
    ff = win.shape[1]
    step = min(1024, ff)
    along = lambda i: (0, i)
    side = pl.BlockSpec(
        (g.shape[0], 1) + g.shape[2:], lambda i: (0, half, 0, 0), pipeline_mode=pl.Buffered(1)
    )
    return call(
        expert_kernel, "expert", (ff // step,),
        [
            full((rows, width)),
            side,
            pl.BlockSpec((width, step), along),
            pl.BlockSpec((1, step), along),
            pl.BlockSpec((step, width), lambda i: (i, 0)),
            full((1, width)),
            full((1, width)),
            PLACED,
        ],
        [
            (side, g.shape, BF),
            (full((rows, width)), (rows, width), BF),
            (full((rows, width)), (rows, width), BF),
            (pl.BlockSpec((rows, step), along), (rows, ff), BF),
            (pl.BlockSpec((rows, step), along), (rows, ff), BF),
            (pl.BlockSpec((8, step), along), (8, ff), F32),
            (full((8, width)), (8, width), F32),
        ],
        [
            pltpu.VMEM((rows, width), F32),
            pltpu.VMEM((rows, width), F32),
            pltpu.VMEM((rows, 128), F32),
            pltpu.SMEM((1,), jnp.int32),
        ],
        cost=(8 * rows * width * ff, 22_000_000, 2 * rows * ff),
        input_output_aliases={} if gy is None else {7: 0},
    )(x, g, win, bias_in, wout, bias_out, center, x if gy is None else gy)


def weigh_kernel(split, which, *refs):
    hid, du, dy, x, bias, small = (refs[i : i + 2] for i in range(0, 12, 2))
    ff = hid[0].shape[1]
    width = dy[0].shape[1]
    step = pl.program_id(0)
    small = small[0][...] + small[1][...]
    row = lax.broadcasted_iota(jnp.int32, (16, width), 0)
    bias = (bias[0][...] + bias[1][...])[0:1]
    if ff < width:
        bias = jnp.concatenate([bias, jnp.zeros((1, width - ff), F32)], axis=1)
    rest = jnp.where(row == 0, bias, 0.0)
    rest = jnp.where(row == 1, small[0:1], rest)
    rest = jnp.where(row == 2, small[1:2], rest)

    def pair(i):
        rows, cols = (x, du) if split else (du, x)
        return rows[i][...], cols[i][...]

    def put(out):
        out[:ff] = (dot(hid[0][...], dy[0][...], 0, 0) + dot(hid[1][...], dy[1][...], 0, 0)).astype(BF)
        out[ff : 2 * ff] = (
            dot(*pair(0), 0, 0) + dot(*pair(1), 0, 0)
        ).astype(BF)
        out[2 * ff :] = rest.astype(BF)

    if not split:
        put(refs[12].at[0])
        return
    for late, out in enumerate(refs[12:]):

        @pl.when(step // 2 == late)
        def _(out=out):
            put(out.at[0])


def weigh(which, n, split, hid, du, dy, x, bias, small):
    rows, ff = hid[0].shape
    width = dy[0].shape[1]
    part = ff // n
    size = 2 * part + 16
    along = lambda i, which: (0, which[i])
    wide = pl.BlockSpec((rows, part), along)
    if split:
        first = pl.BlockSpec((1, size, width), lambda i, which: (jnp.minimum(i, 1), 0, 0))
        last = pl.BlockSpec((1, size, width), lambda i, which: (jnp.maximum(i - 2, 0), 0, 0))
        outs = [(first, (2, size, width), BF), (last, (2, size, width), BF)]
    else:
        outs = [(pl.BlockSpec((1, size, width), lambda i, which: (i, 0, 0)), (n, size, width), BF)]
    got = call(
        partial(weigh_kernel, split), "weigh", (n,),
        [wide] * 4 + [full((rows, width))] * 4 + [pl.BlockSpec((8, part), along)] * 2
        + [full((8, width))] * 2,
        outs, cost=(8 * rows * width * ff, 26_000_000, 0), ahead=1,
    )(which, *hid, *du, *dy, *x, *bias, *small)
    return got if split else got[0]


def unproject_kernel(*refs):
    one_ref, two_ref, *w_refs = refs[: GROUPS + 2]
    x_ref, dh_ref, vec_ref, out_ref = refs[GROUPS + 2 :]
    part = x_ref.shape[1] // GROUPS
    da = None
    for r, w in enumerate(w_refs):
        got = dot((one_ref, two_ref)[r // 2][r % 2], w[:, : 3 * part], 1, 1)
        da = got if da is None else da + got
    unit, inverse = normalize(x_ref[...].astype(F32))
    out_ref[...] = dh_ref[...].astype(F32) + normalize_back(da, unit, inverse, vec_ref[0:1])


def unproject(grads, weights, x, dh, vec):
    count, width = x.shape
    part = width // GROUPS
    rows = min(256, count)
    w = pl.BlockSpec((width, 640), lambda i: (0, 0), pipeline_mode=pl.Buffered(1))
    return call(
        unproject_kernel, "unproject", (count // rows,),
        [chunk((2, rows, 3 * part), 1)] * 2 + [w] * GROUPS
        + [chunk((rows, width)), chunk((rows, width)), full((8, width))],
        [(chunk((rows, width)), (count, width), F32)],
        cost=(6 * count * width * width, 20_000_000, 0),
    )(*grads, *weights, x, dh, vec)[0]


def add(a, b):
    return (a.astype(F32) + b.astype(F32)).astype(BF)


class Place:
    def __init__(self, mesh):
        self.n_dp = mesh.shape["dp"]
        self.n_e = mesh.shape["expert"]
        self.staged = self.n_dp == 4 and self.n_e == 8
        if not self.staged:
            return
        dev = lambda x, c, z, y: (x * 2 + c) * 8 + z * 2 + y
        every = [
            (x, c, z, y) for x in range(2) for c in range(2) for z in range(4) for y in range(2)
        ]
        to = lambda move: [(dev(*p), dev(*move(*p))) for p in every]
        self.core = to(lambda x, c, z, y: (x, 1 - c, z, y))
        self.x = to(lambda x, c, z, y: (1 - x, c, z, y))
        self.across = to(lambda x, c, z, y: (1 - x, 1 - c, z, y))
        self.y = to(lambda x, c, z, y: (x, c, z, 1 - y))
        self.z = [to(lambda x, c, z, y, k=k: (x, c, z ^ k, y)) for k in range(1, 4)]

    def tables(self):
        r = jnp.arange(4, dtype=jnp.int32)
        i = jnp.arange(8, dtype=jnp.int32)
        if not self.staged:
            return r, i, r, i
        d, e = lax.axis_index("dp"), lax.axis_index("expert")
        z, y = e // 2, e % 2
        weighed = d ^ jnp.where(r < 2, 3 - 2 * r, 6 - 2 * r)
        return d ^ r, (z ^ i % 4) * 2 + (y ^ i // 4), weighed, (y ^ i % 2) * 4 + (z ^ i // 2)

    def move(self, array, way):
        return lax.ppermute(array, BOTH, way)


def whole_of(have):
    n_dp, n_e = lax.axis_size("dp"), lax.axis_size("expert")
    rows, cols = have.shape[1:]
    have = have.reshape(n_dp, n_e, rows, cols).transpose(1, 2, 0, 3)
    return have.reshape(n_e * rows, n_dp * cols)


def gather_all(array):
    return whole_of(lax.all_gather(array, BOTH, axis=0, tiled=False))


def scatter_all(array):
    n_dp, n_e = lax.axis_size("dp"), lax.axis_size("expert")
    rows, cols = array.shape[0] // n_e, array.shape[1] // n_dp
    parts = array.reshape(n_e, rows, n_dp, cols).transpose(2, 0, 1, 3)
    parts = parts.reshape(n_dp * n_e, rows, cols)
    return lax.psum_scatter(parts, BOTH, scatter_dimension=0, tiled=False)


def fetch(place, table, weights, out_weights, vectors, filler):
    barrier = lax.optimization_barrier
    stacked = jnp.stack(vectors)
    pad = 64 - len(vectors)
    if place.staged:
        rows = out_weights.shape[0]
        extra = jnp.concatenate([stacked.T, jnp.zeros((rows, pad), BF)], axis=1)
        shard = jnp.concatenate([*weights, extra], axis=1)
        own = jnp.stack([shard] + [place.move(shard, way) for way in place.z])
        own, out_weights, filler = barrier((own, out_weights, filler))
        got = place.move(own, place.y)
        out_own = jnp.stack([out_weights] + [place.move(out_weights, way) for way in place.z])
        got, out_own = barrier((got, out_own))
        near = assemble(table, own, got)
        across = place.move(near, place.x)
        far = place.move(near, place.core)
        return (near, far, across), (out_own, place.move(out_own, place.y)), filler
    vecs = lax.all_gather(stacked, "expert", axis=1, tiled=True)
    width = vecs.shape[1]
    extra = jnp.concatenate([vecs, jnp.zeros((pad, width), BF)]).T
    extra = jnp.broadcast_to(extra[None], (GROUPS, width, 64))
    by_group = lambda w: gather_all(w).reshape(width, GROUPS, -1).transpose(1, 0, 2)
    grouped = jnp.concatenate([*(by_group(w) for w in weights), extra], axis=2)
    out = by_group(out_weights)
    out = out.reshape(GROUPS, 8, width // 8, -1)
    return [grouped[i] for i in range(GROUPS)], [out[i] for i in range(GROUPS)], filler


def reduce_y(place, keep, send, cols):
    got = place.move(send, place.y)
    total = keep[0, :, :cols].astype(F32) + got[0, :, :cols].astype(F32)
    sends = [add(keep[k, :, :cols], got[k, :, :cols]) for k in range(1, 4)]
    return total, sends, add(keep[:, :, cols:], got[:, :, cols:])


def reduce_z(place, sends):
    return [place.move(part, way) for part, way in zip(sends, place.z)]


def columns_of(place, total, count):
    cols = (FAR - 640) // 2
    parts = [total[:, i * cols : (i + 1) * cols] for i in range(3)]
    vecs = total[:, 576 : 576 + 8].T
    vecs = vecs + sum(place.move(vecs, way) for way in (place.core, place.x, place.across))
    return parts, [vecs[i] for i in range(count)]


def reduce_plain(near, far, count):
    slabs = jnp.stack([a[:, :640] for a in (*near, *far)])
    width = slabs.shape[1]
    part = width // GROUPS
    whole = lambda array: array.transpose(1, 0, 2).reshape(width, width)
    parts = [whole(slabs[:, :, i * part : (i + 1) * part]) for i in range(3)]
    parts.append(whole(jnp.stack([far[0][:, -part:], far[1][:, -part:]] + [a[:, 640:-part] for a in far])))
    parts = [scatter_all(p).astype(F32) for p in parts]
    vecs = jnp.sum(slabs[:, :, 576 : 576 + count].astype(F32), axis=0).T
    vecs = lax.psum_scatter(vecs, "expert", scatter_dimension=1, tiled=True)
    vecs = lax.psum(vecs, "dp")
    return parts, [vecs[i] for i in range(count)]


def shards(
    place,
    block_entries,
    assignments,
    positions_within,
    specialist_quotas,
    standardize_one_scale,
    standardize_one_shift,
    asking_weights,
    asking_shift,
    lookup_weights,
    content_weights,
    content_shift,
    context_mixing_weights,
    context_mixing_shift,
    standardize_two_scale,
    standardize_two_shift,
    gating_prototypes,
    specialist_widen_weights,
    specialist_widen_shift,
    specialist_contract_weights,
    specialist_contract_shift,
    upstream_adjoint,
):
    count, width = block_entries.shape
    experts = specialist_quotas.shape[0]
    cap = count // experts
    n_dp = place.n_dp
    order, table, weighed, place_of = place.tables()
    barrier = lax.optimization_barrier

    chosen = assignments[:, None] == lax.broadcasted_iota(jnp.int32, (count, experts), 1)
    limit = jnp.sum(jnp.where(chosen, specialist_quotas[None, :], 0), axis=1)
    kept = positions_within < limit
    target = jnp.where(kept, assignments * cap + positions_within, count)
    late = positions_within >= cap // 2
    halved = jnp.where(late, positions_within + (count - cap) // 2, positions_within)
    halved = jnp.where(kept, assignments * (cap // 2) + halved, count)

    def exchange(rows):
        sent = rows.reshape(experts, -1, width)
        got = lax.all_to_all(sent, "expert", split_axis=0, concat_axis=0, tiled=True)
        return got.reshape(rows.shape)

    weights, out, sent_g = fetch(
        place,
        table,
        (asking_weights, lookup_weights, content_weights),
        context_mixing_weights,
        (
            standardize_one_scale,
            standardize_one_shift,
            asking_shift,
            content_shift,
            context_mixing_shift,
            standardize_two_scale,
            standardize_two_shift,
        ),
        dispatch(target, upstream_adjoint),
    )

    sent_g, first = barrier((sent_g, weights[1]))
    weights = (weights[0], first, *weights[2:])
    rows_g = exchange(sent_g).reshape(experts, 2, cap // 2, width)

    *before, low_in, vec = attend(0, order, weights[:2], x=block_entries)
    if place.staged:
        before, out = barrier((before, out))
        out_near = jnp.concatenate(out)
        before, across, out_near = barrier((before, weights[2], out_near))
        weights = (*weights[:2], across, place.move(across, place.core))
        out_across = place.move(out_near, place.x)
        out = (out_near, place.move(out_near, place.core))
    qkv, ctx, lse = attend(1, order, weights[2:], low=low_in, vec=vec, before=before)
    ctx, rows_g = barrier((ctx, rows_g))
    if place.staged:
        ctx, out_across = barrier((ctx, out_across))
        out += (out_across, place.move(out_across, place.core))
    h1, whole_o, low_mid, sent_one = mix(order, place_of, block_entries, ctx, out, vec, halved)

    sent_two = dispatch(halved, low_mid, count // 2)
    x_one, sent_two = barrier((exchange(sent_one), sent_two))
    x_two = exchange(sent_two)
    matrices = (
        specialist_widen_weights[0], specialist_widen_shift, specialist_contract_weights[0],
        specialist_contract_shift, gating_prototypes,
    )
    gy, dm_one, dy_one, hid_one, du_one, dbin_one, small_one = expert(
        0, x_one, rows_g, *matrices, None
    )
    x_two, dm_one = barrier((x_two, dm_one))
    dm_one = exchange(dm_one)
    gy, dm_two, dy_two, hid_two, du_two, dbin_two, small_two = expert(
        1, x_two, rows_g, *matrices, gy
    )
    dm_one, dm_two, hid_two = barrier((dm_one, dm_two, hid_two))
    dm_two = exchange(dm_two)
    sides = (
        (hid_one, hid_two), (du_one, du_two), (dy_one, dy_two), (x_one, x_two),
        (dbin_one, dbin_two), (small_one, small_two),
    )
    if place.staged:
        grads_far, grads = weigh(
            weighed, n_dp, True, *sides
        )
        grads_far, gy, dm_two = barrier((grads_far, gy, dm_two))
        came_far = place.move(grads_far, place.core)
        crossing = add(grads[0], came_far[0])
    else:
        grads = weigh(jnp.arange(n_dp, dtype=jnp.int32), n_dp, False, *sides)
        grads = lax.psum_scatter(grads, "dp", scatter_dimension=0, tiled=False)
    gy = exchange(gy.reshape(count, width))

    dh1, dctx, grad_o, two = unmix(
        order, h1, upstream_adjoint, dm_one, dm_two, halved, ctx, whole_o, vec
    )
    back = lambda half, dctx: attend_back(
        half, order, table, qkv, ctx, dctx, lse, low_in, grad_o, weights[2 * half : 2 * half + 2],
        two,
    )
    if place.staged:
        dctx, crossing = barrier((dctx, crossing))
        came = place.move(crossing, place.x)
        far, keep, send, more = back(1, dctx)
        more = place.move(more, place.core)
        far, gy = barrier((far, gy))
        output = finish(h1, target, gy)
        send = add(send, more[4:])
        dctx, output, send = barrier((dctx, output, send))
        cols = width // GROUPS
        across, sends, own_o = reduce_y(place, add(keep, more[:4]), send, FAR - cols)
        near, keep, send, more = back(0, dctx)
        near, keep, send, more, across, sends, own_o = barrier(
            (near, keep, send, more, across, sends, own_o)
        )
        more = place.move(more, place.core)
        got = reduce_z(place, sends)
        send, keep = add(send, more[4:]), add(keep, more[:4])
        near, send, keep = barrier((near, send, keep))
        got_y = place.move(send, place.y)
        input_grad = unproject((near, far), weights, block_entries, dh1, vec)
        got_far = got
        got, input_grad, came = barrier((got_y, input_grad, came))
        wide = lambda k, a: jnp.concatenate([a, own_o[k].astype(a.dtype)], axis=1)
        total = wide(0, keep[0].astype(F32) + got[0].astype(F32))
        got = reduce_z(place, [wide(k, add(keep[k], got[k])) for k in range(1, 4)])
        got_far, came, input_grad = barrier((got_far, came, input_grad))
        across = across + sum(g.astype(F32) for g in got_far)
        across = place.move(across.astype(BF), place.x)
        pick = lambda at: sum(
            a[at : at + width].astype(F32) for a in (grads[1], came_far[1], came)
        )
        got, grads, across = barrier((got, [pick(0), pick(width), pick(2 * width)], across))
        total += across.astype(F32)
        total += sum(g.astype(F32) for g in got)
        (sum_q, sum_k, sum_v), small = columns_of(place, total, 7)
        sum_o = total[:, 640:]
    else:
        parts = [back(half, dctx) for half in range(2)]
        slabs = [
            [jnp.concatenate(p[1:3]).reshape(width, -1), p[3].reshape(width, -1)]
            for p in parts
        ]
        (sum_q, sum_k, sum_v, sum_o), small = reduce_plain(*slabs, 7)
        input_grad = unproject([p[0] for p in parts], weights, block_entries, dh1, vec)
        output = finish(h1, target, gy)

        part = (grads.shape[0] - 16) // 2
        grads = [grads[:part], grads[part : 2 * part].T, grads[2 * part :]]
        grads = [g.astype(F32) for g in grads]

    grad_out, grad_in, rest = grads
    part = grad_out.shape[0]
    own = lax.axis_index("dp") * (width // n_dp)
    grad_bin = rest[0:1, :part]
    grad_bout = lax.dynamic_slice(rest[1:2], (0, own), (1, width // n_dp))
    grad_centers = rest[2:3]
    return (
        output,
        input_grad,
        small[0],
        small[1],
        sum_q,
        small[2],
        sum_k,
        sum_v,
        small[3],
        sum_o,
        small[4],
        small[5],
        small[6],
        grad_centers,
        grad_in[None],
        grad_bin,
        grad_out[None],
        grad_bout,
    )


def solution(mesh):
    placed = (
        P(("dp", "expert"), None),
        P(("dp", "expert")),
        P(("dp", "expert")),
        P(),
        P("expert"),
        P("expert"),
        P("expert", "dp"),
        P("expert"),
        P("expert", "dp"),
        P("expert", "dp"),
        P("expert"),
        P("expert", "dp"),
        P("expert"),
        P("expert"),
        P("expert"),
        P("expert", None),
        P("expert", None, None),
        P("expert", None),
        P("expert", None, None),
        P("expert", None),
        P(("dp", "expert"), None),
    )
    return jax.shard_map(
        partial(shards, Place(mesh)),
        mesh=mesh,
        in_specs=placed,
        out_specs=(
            P(("dp", "expert"), None),
            P(("dp", "expert"), None),
            P("expert"),
            P("expert"),
            P("expert", "dp"),
            P("expert"),
            P("expert", "dp"),
            P("expert", "dp"),
            P("expert"),
            P("expert", "dp"),
            P("expert"),
            P("expert"),
            P("expert"),
            P("expert", None),
            P("expert", None, "dp"),
            P("expert", "dp"),
            P("expert", "dp", None),
            P("expert", "dp"),
        ),
        check_vma=False,
    )
```
